32 devices in a mesh: dp: 8 (over y, x, core), tensor: 4 (over z).
Axes of the slice: x: 2, y: 2, z: 4, core: 2. Of those that a mesh axis runs over, the one named last changes fastest.
Arguments:
- inputs: bfloat16 [16384, 768], P(('dp', 'tensor')), may hold values from -6 to 6
- gate_weight: bfloat16 [768, 1536], P('dp', 'tensor'), may hold values from -0.21875 to 0.21875
- value_weight: bfloat16 [768, 1536], P('dp', 'tensor'), may hold values from -0.21875 to 0.21875
- step_weight: bfloat16 [768, 2, 24], P('dp', None, 'tensor'), may hold values from -0.21875 to 0.21875
- shared_weight: bfloat16 [768, 256], P('dp'), may hold values from -0.21875 to 0.21875
- output_weight: bfloat16 [1536, 768], P('tensor', 'dp'), may hold values from -0.15625 to 0.15625
- value_kernel: float32 [4, 1536], replicated, may hold values from -3 to 3
- shared_kernel: float32 [4, 256], replicated, may hold values from -3 to 3
- step_bias: float32 [2, 24], replicated, may hold values from -5 to -1
- decay_log: float32 [24], replicated, may hold values from 0 to 2.5
- skip_gain: float32 [24], replicated, may hold values from 0.5 to 2
- input_gain: float32 [768], replicated, may hold values from 0.1 to 1.9
- output_gain: float32 [1536], replicated, may hold values from 0.1 to 1.9
- cotangent: bfloat16 [16384, 768], P(('dp', 'tensor')), may hold values from -6 to 6
Outputs:
- mixed: bfloat16 [16384, 768], P(('dp', 'tensor'))
- grad_input: bfloat16 [16384, 768], P(('dp', 'tensor'))
- grad_gate: float32 [768, 1536], P('dp', 'tensor')
- grad_value: float32 [768, 1536], P('dp', 'tensor')
- grad_step: float32 [768, 2, 24], P('dp', None, 'tensor')
- grad_shared: float32 [768, 256], P('dp')
- grad_output: float32 [1536, 768], P('tensor', 'dp')
- grad_vkernel: float32 [4, 1536], replicated
- grad_skernel: float32 [4, 256], replicated
- grad_bias: float32 [2, 24], replicated
- grad_decay: float32 [24], replicated
- grad_skip: float32 [24], replicated
- grad_ingain: float32 [768], replicated
- grad_outgain: float32 [1536], replicated
The draws below stay inside these ranges and needn't reach their ends.
All inputs are finite; a program needn't handle non-finite values.
Results may differ from the reference program's by a relative error of at most 0.0087.
Values may be sent and summed in bfloat16 or wider, within the bound.
No kernel may reach another device: no remote copies, remote signals or barrier semaphores. Data moves between devices by JAX's collectives and lax.ppermute only.
A program may use at most 256 MiB of HBM per device.

```python
import jax
import jax.numpy as jnp
from jax import lax

D = 768
HEADS = 24
NSTATE = 64
KCONV = 4
LEN = 2048
SPAN = 128
INNER = 1536
TOK_DEV = 2048
TOKENS = 16384
N_DP = 8


def raised(drawn, own_key, source, target, blocks, factor):
    def block_of(position):
        return (jnp.arange(drawn.shape[position]) // (drawn.shape[position] // blocks)).reshape((-1,) + (1,) * (drawn.ndim - 1 - position))

    first = jax.random.permutation(own_key, blocks)[block_of(target)]
    second = (block_of(target) + blocks // 2) % blocks
    return jnp.where((block_of(source) == first) | (block_of(source) == second), factor * drawn, drawn)


def levels(own_key, extent, cuts, smallest, top_value):
    def one(dim, parts):
        heights = jax.random.uniform(jax.random.fold_in(jax.random.fold_in(own_key, 6), dim), (parts,), jnp.float32, smallest / len(cuts), top_value / len(cuts))
        return jnp.repeat(jnp.exp(heights), extent[dim] // parts).reshape((-1,) + (1,) * (len(extent) - dim - 1))

    gain = one(*cuts[0])
    for cut in cuts[1:]:
        gain = gain * one(*cut)
    return gain


def normal_values(own_key, dims, deviation, most, pieces=(), dtype=jnp.bfloat16):
    values = jax.random.normal(own_key, dims, jnp.float32) * deviation
    if len(pieces) > 0:
        values = levels(own_key, dims, pieces, -0.22, 0.18) * values
    return jnp.clip(values, min=-most, max=most).astype(dtype)


def heavy_noise(stream_key, shape, width, most, cuts, heavy, held_as=jnp.bfloat16):
    drawn = width * jax.random.normal(stream_key, shape, jnp.float32)
    if cuts:
        drawn = drawn * levels(stream_key, shape, cuts, -0.22, 0.18)
    return jnp.clip(raised(drawn, jax.random.fold_in(stream_key, 3), *heavy), -most, most).astype(held_as)


def setup_inputs(seed: int = 0) -> dict:
    seeds = jax.random.split(jax.random.key(seed), 15)
    return {
        "inputs": heavy_noise(seeds[0], (TOKENS, D), 1.0, 6.0, ((0, 32),), (0, 1, 32, 2.75)),
        "gate_weight": normal_values(seeds[1], (D, INNER), D ** -0.5, 0.21875, ((0, 8), (1, 4))),
        "value_weight": normal_values(seeds[2], (D, INNER), D ** -0.5, 0.21875, ((0, 8), (1, 4))),
        "step_weight": normal_values(seeds[3], (D, 2, HEADS), D ** -0.5, 0.21875, ((0, 8), (2, 4))),
        "shared_weight": normal_values(seeds[4], (D, 4 * NSTATE), D ** -0.5, 0.21875, ((0, 8),)),
        "output_weight": normal_values(seeds[5], (INNER, D), INNER ** -0.5, 0.15625, ((0, 4), (1, 8))),
        "value_kernel": normal_values(seeds[6], (KCONV, INNER), KCONV ** -0.5, 3.0, (), jnp.float32),
        "shared_kernel": normal_values(seeds[7], (KCONV, 4 * NSTATE), KCONV ** -0.5, 3.0, (), jnp.float32),
        "step_bias": jnp.clip(jax.random.uniform(seeds[8], (2, HEADS), jnp.float32, -5.0, -1.0), -5.0, -1.0),
        "decay_log": jnp.clip(jax.random.uniform(seeds[9], (HEADS,), jnp.float32, 0.0, 2.5), 0.0, 2.5),
        "skip_gain": jnp.clip(jax.random.uniform(seeds[10], (HEADS,), jnp.float32, 0.5, 2.0), 0.5, 2.0),
        "input_gain": jnp.clip(1.0 + 0.18 * jax.random.normal(seeds[11], (D,), jnp.float32), 0.1, 1.9),
        "output_gain": jnp.clip(1.0 + 0.18 * jax.random.normal(seeds[12], (INNER,), jnp.float32), 0.1, 1.9),
        "cotangent": heavy_noise(seeds[13], (TOKENS, D), 1.0, 6.0, ((0, 32),), (0, 1, 32, 2.75)),
    }


HIGHEST_PREC = lax.Precision.HIGHEST
EPSILON = 1e-06

@jax.custom_vjp
def low(v):
    return lax.optimization_barrier(v.astype(jnp.bfloat16)).astype(jnp.float32)

@jax.custom_vjp
def low_back(v):
    return v

def low_keep(v):
    return (low(v), None)

def low_pass(kept, grad):
    return (grad,)

def back_keep(v):
    return (v, None)

def back_low(kept, grad):
    return (low(grad),)
low.defvjp(low_keep, low_pass)
low_back.defvjp(back_keep, back_low)

def causal_conv(signal, kernel):
    tap_count = kernel.shape[0]
    length = signal.shape[1]
    padded = jnp.pad(signal, ((0, 0), (tap_count - 1, 0), (0, 0)))
    result = jnp.zeros(signal.shape, jnp.float32)
    for offset in range(tap_count):
        result = result + padded[:, offset:offset + length, :] * kernel[offset]
    return result

def span_scan(values, step_sizes, decay_rates, state_in, state_out):
    groups, length, head_count, head_size = values.shape
    span_count = length // SPAN
    values = values.reshape(groups, span_count, SPAN, head_count, head_size)
    step_sizes = step_sizes.reshape(groups, span_count, SPAN, head_count)
    state_in = state_in.reshape(groups, span_count, SPAN, -1)
    state_out = state_out.reshape(groups, span_count, SPAN, -1)
    cumul = jnp.cumsum(step_sizes * decay_rates, axis=2)
    scaled = step_sizes[..., None] * values
    strict = jnp.arange(SPAN)[:, None] > jnp.arange(SPAN)[None, :]
    strict = strict[None, None, :, :, None]
    spread = cumul[:, :, :, None, :] - cumul[:, :, None, :, :]
    decays = jnp.where(strict, jnp.exp(jnp.where(strict, spread, 0.0)), 0.0)
    inner_prod = jnp.einsum('gctn,gcsn->gcts', state_out, state_in, precision=HIGHEST_PREC)
    within = jnp.einsum('gctsh,gcshp->gcthp', inner_prod[..., None] * decays, scaled, precision=HIGHEST_PREC)
    span_total = cumul[:, :, -1, :]
    weights = jnp.exp(span_total[:, :, None, :] - cumul)
    states = jnp.einsum('gcsn,gcshp->gchnp', state_in, weights[..., None] * scaled, precision=HIGHEST_PREC)

    def advance(running, inputs_now):
        span_state, span_sum = inputs_now
        return (jnp.exp(span_sum)[:, :, None, None] * running + span_state, running)
    initial = jnp.zeros((groups, head_count, state_in.shape[-1], head_size), jnp.float32)
    entering = lax.scan(advance, initial, (jnp.moveaxis(states, 1, 0), jnp.moveaxis(span_total, 1, 0)))[1]
    entering = jnp.moveaxis(entering, 0, 1)
    carried = jnp.einsum('gctn,gchnp->gcthp', state_out, entering, precision=HIGHEST_PREC) * jnp.exp(cumul)[..., None]
    return (within + carried).reshape(groups, length, head_count, head_size)

def mixer(value_pre, shared_pre, step_pre, value_kernel, shared_kernel, step_bias, decay_log, skip_gain):
    groups, length, columns = value_pre.shape
    head_count = step_pre.shape[-1]
    signal = jax.nn.silu(causal_conv(value_pre, value_kernel)).reshape(groups, length, head_count, columns // head_count)
    shared = jax.nn.silu(causal_conv(shared_pre, shared_kernel))
    state_size = shared.shape[-1] // 4
    step_sizes = jax.nn.softplus(step_pre + step_bias)
    decay_rates = -jnp.exp(decay_log)
    forward = span_scan(signal, step_sizes[:, :, 0], decay_rates, shared[..., :state_size], shared[..., state_size:2 * state_size])
    backward = jnp.flip(span_scan(jnp.flip(signal, 1), jnp.flip(step_sizes[:, :, 1], 1), decay_rates, jnp.flip(shared[..., 2 * state_size:3 * state_size], 1), jnp.flip(shared[..., 3 * state_size:], 1)), 1)
    return (forward + backward + skip_gain[:, None] * signal).reshape(groups, length, columns)

def layer(inputs, gate_weight, value_weight, step_weight, shared_weight, output_weight, value_kernel, shared_kernel, step_bias, decay_log, skip_gain, input_gain, output_gain):
    in_scale = lax.rsqrt(lax.optimization_barrier(jnp.mean(inputs * inputs, axis=-1, keepdims=True)) + EPSILON)
    normed = low(inputs * in_scale * input_gain)
    tokens = inputs.shape[0]
    groups = tokens // LEN
    gate_pre = low_back(jnp.dot(normed, gate_weight, precision=HIGHEST_PREC))
    value_pre = low_back(jnp.dot(normed, value_weight, precision=HIGHEST_PREC))
    step_pre = low_back(jnp.dot(normed, step_weight.reshape(D, 2 * HEADS), precision=HIGHEST_PREC))
    shared_pre = low_back(jnp.dot(normed, shared_weight, precision=HIGHEST_PREC))
    scan_out = mixer(value_pre.reshape(groups, LEN, INNER), shared_pre.reshape(groups, LEN, 4 * NSTATE), step_pre.reshape(groups, LEN, 2, HEADS), value_kernel, shared_kernel, step_bias, decay_log, skip_gain).reshape(tokens, INNER)
    gated = scan_out * jax.nn.silu(gate_pre)
    out_scale = lax.rsqrt(lax.optimization_barrier(jnp.mean(gated * gated, axis=-1, keepdims=True)) + EPSILON)
    normalized = low(gated * out_scale * output_gain)
    return inputs + low_back(jnp.dot(normalized, output_weight, precision=HIGHEST_PREC))

def reference(inputs, gate_weight, value_weight, step_weight, shared_weight, output_weight, value_kernel, shared_kernel, step_bias, decay_log, skip_gain, input_gain, output_gain, cotangent):
    params = tuple((weight.astype(jnp.float32) for weight in (gate_weight, value_weight, step_weight, shared_weight, output_weight, value_kernel, shared_kernel, step_bias, decay_log, skip_gain, input_gain, output_gain)))
    wide_in = inputs.astype(jnp.float32).reshape(N_DP, TOK_DEV, D)
    wide_cot = cotangent.astype(jnp.float32).reshape(N_DP, TOK_DEV, D)

    def group_step(totals, pair):
        block_in, block_cot = pair
        result, pull = jax.vjp(layer, block_in, *params)
        grads = pull(block_cot)
        summed = tuple((first + second for first, second in zip(totals, grads[1:])))
        return (summed, (result.astype(jnp.bfloat16), grads[0].astype(jnp.bfloat16)))
    initial = tuple((jnp.zeros(weight.shape, jnp.float32) for weight in params))
    totals, outputs = lax.scan(group_step, initial, (wide_in, wide_cot))
    mixed = outputs[0].reshape(TOKENS, D)
    grad_input = outputs[1].reshape(TOKENS, D)
    return (mixed, grad_input, totals[0], totals[1], totals[2], totals[3], totals[4], totals[5], totals[6], totals[7], totals[8], totals[9], totals[10], totals[11])
```

```python
import functools

import jax
import jax.numpy as jnp
from jax import lax
from jax.experimental import pallas as pl
from jax.experimental.pallas import tpu as pltpu
from jax.sharding import PartitionSpec as P

F32 = jnp.float32
BF16 = jnp.bfloat16
EPSILON = 1e-06
SPAN = 128
HALO = 16
TAPS = 4
LANES = 128
LOG2E = 1.4426950408889634
EXACT = lax.Precision.HIGHEST
LIMIT = 58 * 1024 * 1024

NN = (((1,), (0,)), ((), ()))
NT = (((1,), (1,)), ((), ()))
TN = (((0,), (0,)), ((), ()))


def mm(a, b, dims=NN, precision=None):
    return lax.dot_general(a, b, dims, preferred_element_type=F32, precision=precision)


def iota(shape, dim):
    return lax.broadcasted_iota(jnp.int32, shape, dim)


def sigmoid(v):
    return 1.0 / (1.0 + jnp.exp(-v))


def chunk_rows(c, base=0):
    return pl.ds(base + c * SPAN, SPAN)


def spread_matrix(j, d, own, head, width, dtype):
    col = iota((LANES, width), 1) // head
    return (iota((LANES, width), 0) == own * (2 * j + d) + col).astype(dtype)


def gather_matrix(j, d, own, head, width, dtype):
    row = iota((width, LANES), 0) // head
    return (iota((width, LANES), 1) == own * (2 * j + d) + row).astype(dtype)


def call(kernel, out_shape, scratch=(), smem_first=True, flops=0, count=0):
    def run(*args):
        specs = [
            pl.BlockSpec(memory_space=pltpu.SMEM if (smem_first and i == 0) else pltpu.VMEM)
            for i in range(len(args))
        ]
        moved = sum(a.size * a.dtype.itemsize for a in args)
        outs = jax.tree.leaves(out_shape)
        moved += sum(o.size * o.dtype.itemsize for o in outs)
        return pl.pallas_call(
            kernel,
            out_shape=out_shape,
            in_specs=specs,
            out_specs=jax.tree.map(lambda _: pl.BlockSpec(memory_space=pltpu.VMEM), out_shape),
            scratch_shapes=list(scratch),
            cost_estimate=pl.CostEstimate(flops=flops, bytes_accessed=moved, transcendentals=count),
            compiler_params=pltpu.CompilerParams(vmem_limit_bytes=LIMIT),
        )(*args)

    return run


def sds(shape, dtype=F32):
    return jax.ShapeDtypeStruct(shape, dtype)


def put_weights(ids, pieces, full, shares, per):
    if len(pieces) == 1:
        full[...] = pieces[0][...]
        return
    for rel, piece in enumerate(pieces):
        row = pl.multiple_of((ids[1] ^ rel) * per, per)
        for d in range(shares):
            j = (ids[0] + shares - d) % shares
            full[j, pl.ds(row, per), :] = piece[d]


def take_grads(ids, pieces, held, d, per):
    if len(pieces) == 1:
        pieces[0][(ids[0] + pieces[0].shape[0] - d) % pieces[0].shape[0]] = held[...]
        return
    for rel, piece in enumerate(pieces):
        row = pl.multiple_of((ids[1] ^ rel) * per, per)
        piece[d] = held[pl.ds(row, per), :]


def cyclic(size, d):
    return [(i, (i + d) % size) for i in range(size)]


def xor(size, bit):
    return [(i, i ^ bit) for i in range(size)]


def gather_weights(pack, shares, groups, fast):
    if not fast:
        rows = lax.all_gather(pack, "dp", axis=0, tiled=True)
        return [lax.all_gather(rows, "tensor", axis=0, tiled=False)]
    held = jnp.stack(
        [pack] + [lax.ppermute(pack, "tensor", cyclic(shares, d)) for d in range(1, shares)]
    )
    near = [held] + [
        lax.ppermute(held, "dp", xor(groups, 2 * k)) for k in range(1, groups // 2)
    ]
    pieces = []
    for block in near:
        pieces += [block, lax.ppermute(block, "dp", xor(groups, 1))]
    return pieces


def scatter_grads(pieces, shares, groups, fast):
    if not fast:
        part = lax.psum_scatter(pieces[0].astype(F32), "dp", scatter_dimension=1, tiled=True)
        return lax.psum_scatter(part, "tensor", scatter_dimension=0, tiled=False)
    pairs = []
    for k in range(groups // 2):
        other = lax.ppermute(pieces[2 * k + 1], "dp", xor(groups, 1))
        pairs.append((pieces[2 * k].astype(F32) + other.astype(F32)).astype(BF16))
    total = pairs[0].astype(F32)
    for k in range(1, groups // 2):
        total = total + lax.ppermute(pairs[k], "dp", xor(groups, 2 * k)).astype(F32)
    total = total.astype(BF16)
    out = total[0].astype(F32)
    for d in range(1, shares):
        out = out + lax.ppermute(total[d], "tensor", cyclic(shares, shares - d)).astype(F32)
    return out


def ordered_sum(parts, places):
    held = jnp.stack(parts)
    total = None
    for place in places:
        part = lax.dynamic_index_in_dim(held, place, 0, keepdims=False).astype(F32)
        total = part if total is None else total + part
    return total


def sum_all(v, shares, groups, fast):
    if not fast:
        return lax.psum(v, ("dp", "tensor"))
    z, g = lax.axis_index("tensor"), lax.axis_index("dp")
    v = v + lax.ppermute(v, "dp", xor(groups, 1))
    near = [v] + [lax.ppermute(v, "dp", xor(groups, 2 * k)) for k in range(1, groups // 2)]
    v = ordered_sum(near, [m ^ (g // 2) for m in range(groups // 2)])
    line = [v] + [lax.ppermute(v, "tensor", cyclic(shares, d)) for d in range(1, shares)]
    return ordered_sum(line, [(z + shares - m) % shares for m in range(shares)])


def front_kernel(cfg, *refs):
    n = cfg["pieces"]
    ids, halo, inputs, gain, vk, sk, bias, rate = refs[:8]
    pieces = refs[8 : 8 + n]
    (
        w1, normed, vext, u_out, x_out, side, su_out, bc_out, c2, rho2, c2t, rho2t, dec, states, tots,
        pay1, pay2, pay3, acc,
    ) = refs[8 + n :]
    shares, own, head, cols, rows = (cfg[k] for k in ("shares", "own", "head", "cols", "rows"))
    blocks = rows // SPAN
    put_weights(ids, pieces, w1, shares, cfg["per"])

    def norm(block):
        wide = block.astype(F32)
        scale = lax.rsqrt(jnp.mean(wide * wide, axis=1, keepdims=True) + EPSILON)
        return (wide * scale * gain[...]).astype(BF16)

    normed[0:HALO, :] = norm(halo[...])
    for c in range(blocks):
        normed[chunk_rows(c, HALO), :] = norm(inputs[chunk_rows(c), :])

    def project(j, _):
        acc[...] = mm(normed[...], w1[j])
        vext[j] = acc[:, :cols].astype(BF16)
        side[j] = acc[:, cols : cols + LANES]
        for c in range(blocks):
            for p in range(cols // LANES):
                lanes = pl.ds(p * LANES, LANES)
                u = jnp.zeros((SPAN, LANES), F32)
                for m in range(TAPS):
                    u = u + vk[j, m : m + 1, lanes] * acc[chunk_rows(c, HALO - TAPS + 1 + m), lanes]
                u_out[j, chunk_rows(c), lanes] = u.astype(BF16)
                x_out[j, chunk_rows(c), lanes] = (u * sigmoid(u)).astype(BF16)
            u = jnp.zeros((SPAN, LANES), F32)
            for m in range(TAPS):
                u = u + sk[j, m : m + 1, :] * acc[
                    chunk_rows(c, HALO - TAPS + 1 + m), pl.ds(cols, LANES)
                ]
            su_out[j, chunk_rows(c), :] = u
            bc_out[j, chunk_rows(c), :] = (u * sigmoid(u)).astype(BF16)
        return 0

    lax.fori_loop(0, shares, project, 0)

    lane = iota((SPAN, LANES), 1)
    is_fwd = lane % (2 * own) < own
    low = iota((SPAN, SPAN), 0) >= iota((SPAN, SPAN), 1)
    prefix = low.astype(F32)
    suffix = (iota((SPAN, SPAN), 0) <= iota((SPAN, SPAN), 1)).astype(F32)
    for c in range(blocks):
        raw = jnp.zeros((SPAN, LANES), F32)
        for j in range(shares):
            moved = pltpu.roll(
                side[j, chunk_rows(c, HALO), :], (2 * own * j - cfg["state"]) % LANES, 1
            )
            raw = jnp.where((lane >= 2 * own * j) & (lane < 2 * own * (j + 1)), moved, raw)
        v = raw + bias[...]
        tail = jnp.exp(-jnp.abs(v))
        dt = jnp.where(v < -15.0, jnp.exp(jnp.minimum(v, 0.0)), jnp.maximum(v, 0.0) + jnp.log1p(tail))
        sig = sigmoid(v)
        log_dt = jnp.where(v < -15.0, v, jnp.log(jnp.maximum(dt, 1e-30)))
        ratio = jnp.where(v < -15.0, 1.0, sig / jnp.maximum(dt, 1e-30))
        a = dt * rate[...]
        cum = jnp.where(is_fwd, mm(prefix, a, precision=EXACT), mm(suffix, a, precision=EXACT))
        tot = jnp.sum(a, axis=0, keepdims=True)
        rho = cum - log_dt
        cc = cum * LOG2E
        rr = rho * LOG2E
        c2[chunk_rows(c), :] = cc
        rho2[chunk_rows(c), :] = rr
        c2t[c] = cc.T
        rho2t[c] = rr.T
        dec[0, chunk_rows(c), :] = a
        dec[1, chunk_rows(c), :] = ratio
        dec[2, chunk_rows(c), :] = jnp.exp(tot - rho)
        dec[3, chunk_rows(c), :] = jnp.exp(cum)
        tots[c : c + 1, :] = tot
    lane1 = iota((1, LANES), 1)
    fwd1 = lane1 % (2 * own) < own
    lead = []
    for c in range(blocks):
        after = jnp.zeros((1, LANES), F32)
        before = jnp.zeros((1, LANES), F32)
        for k in range(blocks):
            if k > c:
                after = after + tots[k : k + 1, :]
            if k < c:
                before = before + tots[k : k + 1, :]
        lead.append(jnp.exp(jnp.where(fwd1, after, before)))
        tots[blocks + c : blocks + c + 1, :] = jnp.where(fwd1, before, after)
    lead = jnp.concatenate(lead + [jnp.zeros((8 - blocks, LANES), F32)], axis=0)
    whole = tots[0:1, :]
    for c in range(1, blocks):
        whole = whole + tots[c : c + 1, :]
    tots[2 * blocks : 2 * blocks + 8, :] = jnp.broadcast_to(whole, (8, LANES))

    def sums(j, _):
        dev = []
        for d in range(2):
            grow = spread_matrix(j, d, own, head, cols, BF16)
            wide = mm(lead, grow.astype(F32), precision=EXACT)
            total = jnp.zeros((cfg["state"], cols), F32)
            for c in range(blocks):
                weight = mm(dec[2, chunk_rows(c), :].astype(BF16), grow)
                xw = (weight * x_out[j, chunk_rows(c), :].astype(F32)).astype(BF16)
                s = mm(bc_out[2 * d, chunk_rows(c), :], xw, TN)[: cfg["state"]]
                states[j, d, c] = s
                total = total + wide[c : c + 1, :] * s
            dev.append(total)
        for dist, pay in ((1, pay1), (2, pay2), (3, pay3)):
            pay[j] = jnp.where(ids[0] + dist < shares, dev[0], dev[1]).astype(BF16)
        return 0

    lax.fori_loop(0, shares, sums, 0)


def within_kernel(cfg, bc, c2, rho2t, x, y):
    shares, own, cols, rows = (cfg[k] for k in ("shares", "own", "cols", "rows"))
    t = iota((SPAN, SPAN), 0)
    s = iota((SPAN, SPAN), 1)
    low = t > s
    first = iota((SPAN, LANES), 1) < cfg["head"]

    def block(c, _):
        at = pl.ds(pl.multiple_of(c * SPAN, SPAN), SPAN)
        g = jnp.where(low, mm(bc[1, at, :], bc[0, at, :], NT), mm(bc[3, at, :], bc[2, at, :], NT))
        g = jnp.where(t == s, 0.0, g)
        cc = c2[at, :]
        for j in range(shares):
            for p in range(own // 2):
                mats = []
                for i in (2 * p, 2 * p + 1):
                    f, b = 2 * own * j + i, 2 * own * j + own + i
                    col = jnp.where(low, cc[:, f : f + 1], cc[:, b : b + 1])
                    row = jnp.where(low, rho2t[c, f : f + 1, :], rho2t[c, b : b + 1, :])
                    mats.append((jnp.exp2(col - row) * g).astype(BF16))
                xp = x[j, at, p * LANES : (p + 1) * LANES]
                zero = jnp.zeros_like(xp)
                pair = jnp.concatenate([jnp.where(first, xp, zero), jnp.where(first, zero, xp)], axis=0)
                y[j, at, p * LANES : (p + 1) * LANES] = mm(jnp.concatenate(mats, axis=1), pair)
        return 0

    lax.fori_loop(0, rows // SPAN, block, 0)


def gate_kernel(cfg, *refs):
    n = cfg["pieces"]
    ids, normed, cot = refs[:3]
    pieces = refs[3 : 3 + n]
    w2, gate, gn = refs[3 + n :]
    shares, cols, rows = (cfg[k] for k in ("shares", "cols", "rows"))
    put_weights(ids, pieces, w2, shares, cfg["per"])

    def project(j, _):
        gate[j] = mm(normed[HALO : HALO + rows, :], w2[j, :, :cols])
        gn[j] = mm(cot[...], w2[j, :, cols:])
        return 0

    lax.fori_loop(0, shares, project, 0)


def incoming(ids, shares, r1, r2, r3, j, near, far):
    z = ids[0]

    def keep(test, v):
        return jnp.where(test, v.astype(F32), 0.0)

    before = (
        keep(z >= 1, r1[j])
        + near[0] * keep(z >= 2, r2[j])
        + near[1] * keep(z >= 3, r3[j])
    )
    after = (
        keep(z <= shares - 2, r3[j])
        + far[0] * keep(z <= shares - 3, r2[j])
        + far[1] * keep(z <= shares - 4, r1[j])
    )
    return before, after


def middle_kernel(cfg, *refs):
    (
        ids, yin, x, gate, gn, states, bc, dec, tots, l1, l2, l3, r1, r2, r3, skip, ogain,
        enter, dy, normal, dgate, edy, rr, dlocal, p1, p2, p3, dskip, dgain,
        ys, ef, eb,
    ) = refs
    shares, own, head, cols, rows = (cfg[k] for k in ("shares", "own", "head", "cols", "rows"))
    blocks, inner = rows // SPAN, cols * shares

    def spread_row(row, grow):
        return mm(jnp.broadcast_to(row, (8, LANES)), grow, precision=EXACT)[0:1, :]

    def enter_states(j, _):
        gf = spread_matrix(j, 0, own, head, cols, F32)
        gb = spread_matrix(j, 1, own, head, cols, F32)
        near = (spread_row(jnp.exp(l1[0:1, :]), gf), spread_row(jnp.exp(l1[0:1, :] + l2[0:1, :]), gf))
        far = (spread_row(jnp.exp(l3[0:1, :]), gb), spread_row(jnp.exp(l3[0:1, :] + l2[0:1, :]), gb))
        e, e_b = incoming(ids, shares, r1, r2, r3, j, near, far)
        for c in range(blocks):
            enter[j, 0, c] = e.astype(BF16)
            e = spread_row(jnp.exp(tots[c : c + 1, :]), gf) * e + states[j, 0, c]
        for c in reversed(range(blocks)):
            enter[j, 1, c] = e_b.astype(BF16)
            e_b = spread_row(jnp.exp(tots[c : c + 1, :]), gb) * e_b + states[j, 1, c]
        return 0

    lax.fori_loop(0, shares, enter_states, 0)
    dskip[...] = jnp.zeros_like(dskip)
    dgain[...] = jnp.zeros_like(dgain)

    def block(c, _):
        at = pl.ds(pl.multiple_of(c * SPAN, SPAN), SPAN)
        ec = dec[3, at, :].astype(BF16)

        def first(j, sums):
            square, dot = sums
            ecf = mm(ec, spread_matrix(j, 0, own, head, cols, BF16))
            ecb = mm(ec, spread_matrix(j, 1, own, head, cols, BF16))
            cf = mm(bc[1, at, : cfg["state"]], enter[j, 0, c]) * ecf
            cb = mm(bc[3, at, : cfg["state"]], enter[j, 1, c]) * ecb
            ef[j] = cf
            eb[j] = cb
            v = yin[j, at, :] + skip[j] * x[j, at, :].astype(F32) + cf + cb
            ys[j] = v
            g = gate[j, at, :]
            gated = v * g * sigmoid(g)
            square = square + jnp.sum(gated * gated, axis=1, keepdims=True)
            dot = dot + jnp.sum(gn[j, at, :] * ogain[j] * gated, axis=1, keepdims=True)
            return square, dot

        zero = jnp.zeros((SPAN, 1), F32)
        square, dot = lax.fori_loop(0, shares, first, (zero, zero))
        inv = lax.rsqrt(square / inner + EPSILON)
        back = inv * inv * inv * dot / inner

        def second(j, acc):
            v = ys[j]
            g = gate[j, at, :]
            sig = sigmoid(g)
            act = g * sig
            gated = v * act
            scaled = gated * inv
            normal[j, at, :] = (scaled * ogain[j]).astype(BF16)
            dgain[j] += jnp.sum(gn[j, at, :] * scaled, axis=0, keepdims=True)
            dgated = inv * (gn[j, at, :] * ogain[j]) - gated * back
            d_scan = dgated * act
            dy[j, at, :] = d_scan.astype(BF16)
            dgate[j, at, :] = (dgated * v * sig * (1.0 + g * (1.0 - sig))).astype(BF16)
            dskip[j] += jnp.sum(d_scan * x[j, at, :].astype(F32), axis=0, keepdims=True)
            for d, kept in ((0, ef), (1, eb)):
                acc = acc + mm((d_scan * kept[j]).astype(BF16), gather_matrix(j, d, own, head, cols, BF16))
                wide = mm(ec, spread_matrix(j, d, own, head, cols, BF16))
                edy[j, d, at, :] = (wide * d_scan).astype(BF16)
                dlocal[j, d, c] = mm(bc[1 + 2 * d, at, :], edy[j, d, at, :], TN)[: cfg["state"]]
            return acc

        rr[at, :] = lax.fori_loop(0, shares, second, jnp.zeros((SPAN, LANES), F32))
        return 0

    lax.fori_loop(0, blocks, block, 0)
    trail = jnp.exp(tots[blocks : 2 * blocks, :])
    trail = jnp.concatenate([trail, jnp.zeros((8 - blocks, LANES), F32)], axis=0)

    def leave(j, _):
        dev = []
        for d in range(2):
            wide = mm(trail, spread_matrix(j, d, own, head, cols, F32), precision=EXACT)
            total = jnp.zeros((cfg["state"], cols), F32)
            for c in range(blocks):
                total = total + wide[c : c + 1, :] * dlocal[j, d, c]
            dev.append(total)
        for dist, pay in ((1, p1), (2, p2), (3, p3)):
            pay[j] = jnp.where(ids[0] + dist < shares, dev[1], dev[0]).astype(BF16)
        return 0

    lax.fori_loop(0, shares, leave, 0)


def output_kernel(cfg, *refs):
    n = cfg["pieces"]
    ids, inputs, cot, normed, normal, dgate, w2 = refs[:7]
    mixed, gx = refs[7:9]
    pieces = refs[9 : 9 + n]
    (held,) = refs[9 + n :]
    shares, cols, rows = (cfg[k] for k in ("shares", "cols", "rows"))

    def project(d, _):
        j = (ids[0] + shares - d) % shares
        part = mm(normal[j], w2[j, :, cols:], NT)
        back = mm(dgate[j], w2[j, :, :cols], NT)

        @pl.when(d == 0)
        def _():
            mixed[...] = part
            gx[...] = back

        @pl.when(d > 0)
        def _():
            mixed[...] += part
            gx[...] += back

        held[:, :cols] = mm(normed[HALO : HALO + rows, :], dgate[j], TN).astype(BF16)
        held[:, cols:] = mm(cot[...], normal[j], TN).astype(BF16)
        take_grads(ids, pieces, held, d, cfg["per"])
        return 0

    lax.fori_loop(0, shares, project, 0)
    mixed[...] += inputs[...].astype(F32)


def back_within_kernel(cfg, bc, rho2, c2t, x, dy, dx, dbc, da, dk, das, ras):
    shares, own, cols, rows = (cfg[k] for k in ("shares", "own", "cols", "rows"))
    s = iota((SPAN, SPAN), 0)
    t = iota((SPAN, SPAN), 1)
    up = t > s
    first = iota((SPAN, LANES), 1) < cfg["head"]
    tri = jnp.concatenate([(s >= t).astype(BF16), (s <= t).astype(BF16)], axis=1)
    lane = iota((SPAN, LANES), 1)
    row0 = iota((LANES, SPAN), 0)
    is_fwd = row0 % (2 * own) < own

    def block(c, _):
        at = pl.ds(pl.multiple_of(c * SPAN, SPAN), SPAN)
        g = jnp.where(up, mm(bc[0, at, :], bc[1, at, :], NT), mm(bc[2, at, :], bc[3, at, :], NT))
        g = jnp.where(t == s, 0.0, g)
        rho = rho2[at, :]
        dg = jnp.zeros((SPAN, SPAN), F32)
        das[...] = jnp.zeros_like(das)
        ras[...] = jnp.zeros_like(ras)
        for j in range(shares):
            for p in range(own // 2):
                lanes = slice(p * LANES, (p + 1) * LANES)
                xp, dyp = x[j, at, lanes], dy[j, at, lanes]
                zero = jnp.zeros_like(xp)
                xs = jnp.concatenate([jnp.where(first, xp, zero), jnp.where(first, zero, xp)], axis=0)
                ds_ = jnp.concatenate([jnp.where(first, dyp, zero), jnp.where(first, zero, dyp)], axis=0)
                dm = mm(xs, dyp, NT)
                ws, zs = [], []
                for q in range(2):
                    i = 2 * p + q
                    f, b = 2 * own * j + i, 2 * own * j + own + i
                    row = jnp.where(up, c2t[c, f : f + 1, :], c2t[c, b : b + 1, :])
                    col = jnp.where(up, rho[:, f : f + 1], rho[:, b : b + 1])
                    pw = jnp.exp2(row - col)
                    ud = dm[q * SPAN : (q + 1) * SPAN] * pw
                    dg = dg + ud
                    ws.append((pw * g).astype(BF16))
                    zd = ud * g
                    zs.append(zd.astype(BF16))
                    rf = jnp.sum(jnp.where(up, zd, 0.0), axis=0, keepdims=True)
                    ras[f : f + 1, :] = rf
                    ras[b : b + 1, :] = jnp.sum(zd, axis=0, keepdims=True) - rf
                dx[j, at, lanes] = mm(jnp.concatenate(ws, axis=1), ds_)
                cross = mm(jnp.concatenate(zs, axis=0), tri)
                for q in range(2):
                    i = 2 * p + q
                    f, b = 2 * own * j + i, 2 * own * j + own + i
                    part = cross[q * SPAN : (q + 1) * SPAN]
                    das[f : f + 1, :] = jnp.sum(jnp.where(up, part[:, :SPAN], 0.0), axis=0, keepdims=True)
                    das[b : b + 1, :] = jnp.sum(
                        jnp.where(t < s, part[:, SPAN:], 0.0), axis=0, keepdims=True
                    )
        df = jnp.where(up, dg, 0.0).astype(BF16)
        db = jnp.where(t < s, dg, 0.0).astype(BF16)
        dbc[0, at, :] = mm(df, bc[1, at, :])
        dbc[1, at, :] = mm(df, bc[0, at, :], TN)
        dbc[2, at, :] = mm(db, bc[3, at, :])
        dbc[3, at, :] = mm(db, bc[2, at, :], TN)
        a = das[...]
        later = jnp.where(lane < SPAN - 1, pltpu.roll(a, SPAN - 1, 1), 0.0)
        sooner = jnp.where(lane > 0, pltpu.roll(a, 1, 1), 0.0)
        kd = ras[...] - a + jnp.where(is_fwd, later, sooner)
        da[at, :] = a.T
        dk[at, :] = kd.T
        return 0

    lax.fori_loop(0, rows // SPAN, block, 0)


def tail_kernel(cfg, *refs):
    (
        ids, x, u, dy, dxi, vext, side, su, bc, dbc, dec, tots, enter, edy, rr, da, dk, dlocal,
        l1, l2, l3, r1, r2, r3, skip, vk, sk,
        dp, dvk, dsk, dstep,
        du, dsu, dst, dstate, xs, qs,
    ) = refs
    shares, own, head, cols, rows = (cfg[k] for k in ("shares", "own", "head", "cols", "rows"))
    blocks, ns = rows // SPAN, cfg["state"]

    def spread_row(row, grow):
        return mm(jnp.broadcast_to(row, (8, LANES)), grow, precision=EXACT)[0:1, :]

    xs[...] = jnp.zeros_like(xs)
    qs[...] = jnp.zeros_like(qs)
    du[...] = jnp.zeros_like(du)
    dsu[...] = jnp.zeros_like(dsu)
    dst[...] = dbc[...]

    def values(j, _):
        gf = spread_matrix(j, 0, own, head, cols, F32)
        gb = spread_matrix(j, 1, own, head, cols, F32)
        near = (spread_row(jnp.exp(l1[0:1, :]), gb), spread_row(jnp.exp(l1[0:1, :] + l2[0:1, :]), gb))
        far = (spread_row(jnp.exp(l3[0:1, :]), gf), spread_row(jnp.exp(l3[0:1, :] + l2[0:1, :]), gf))
        e_b, e = incoming(ids, shares, r1, r2, r3, j, near, far)
        for d, order, now in ((0, list(reversed(range(blocks))), e), (1, list(range(blocks)), e_b)):
            for c in order:
                low = now.astype(BF16)
                dstate[d, c] = low
                kept = spread_row(jnp.exp(tots[c : c + 1, :]), gf if d == 0 else gb)
                through = kept * jnp.sum(enter[j, d, c].astype(F32) * now, axis=0, keepdims=True)
                xs[c : c + 1, :] += mm(
                    jnp.broadcast_to(through, (8, cols)),
                    gather_matrix(j, d, own, head, cols, F32),
                    precision=EXACT,
                )[0:1, :]
                now = kept * now + dlocal[j, d, c]
        for c in range(blocks):
            at = chunk_rows(c)
            weights = dec[2, at, :].astype(BF16)
            xv = x[j, at, :].astype(F32)
            dx = dxi[j, at, :] + skip[j] * dy[j, at, :].astype(F32)
            for d in range(2):
                wide = mm(weights, spread_matrix(j, d, own, head, cols, BF16))
                inner = mm(bc[2 * d, at, :ns], dstate[d, c]) * wide
                dx = dx + inner
                qs[at, :] += mm((inner * xv).astype(BF16), gather_matrix(j, d, own, head, cols, BF16))
                dst[2 * d, at, :ns] += mm((wide * xv).astype(BF16), dstate[d, c], NT)
                dst[2 * d + 1, at, :ns] += mm(edy[j, d, at, :], enter[j, d, c], NT)
            uv = u[j, at, :].astype(F32)
            sig = sigmoid(uv)
            du[chunk_rows(c, HALO), :] = dx * sig * (1.0 + uv * (1.0 - sig))
        for m in range(TAPS):
            dvk[j, m : m + 1, :] = jnp.zeros((1, cols), F32)
        for start, size in [(0, HALO)] + [(HALO + c * SPAN, SPAN) for c in range(blocks)]:
            for p in range(cols // LANES):
                lanes = pl.ds(p * LANES, LANES)
                old = vext[j, pl.ds(start, size), lanes].astype(F32)
                dv = jnp.zeros((size, LANES), F32)
                for m in range(TAPS):
                    shifted = du[pl.ds(start + TAPS - 1 - m, size), lanes]
                    dv = dv + vk[j, m : m + 1, lanes] * shifted
                    dvk[j, m : m + 1, lanes] += jnp.sum(old * shifted, axis=0, keepdims=True)
                dp[j, pl.ds(start, size), lanes] = dv.astype(BF16)
        return 0

    lax.fori_loop(0, shares, values, 0)

    lane = iota((SPAN, LANES), 1)
    is_fwd = lane % (2 * own) < own
    at0 = iota((SPAN, SPAN), 0)
    at1 = iota((SPAN, SPAN), 1)
    prefix, suffix = (at0 >= at1).astype(F32), (at0 <= at1).astype(F32)
    before, after = (at0 > at1).astype(F32), (at0 < at1).astype(F32)
    dbias = jnp.zeros((1, LANES), F32)
    ddecay = jnp.zeros((1, LANES), F32)
    steps = []
    for c in range(blocks):
        at = chunk_rows(c)
        rv, qv = rr[at, :], qs[at, :]
        total = da[at, :] + xs[c : c + 1, :]
        total = total + jnp.where(
            is_fwd,
            mm(suffix, rv, precision=EXACT) + mm(before, qv, precision=EXACT),
            mm(prefix, rv, precision=EXACT) + mm(after, qv, precision=EXACT),
        )
        through = total * dec[0, at, :]
        step = (dk[at, :] + qv + through) * dec[1, at, :]
        step = jnp.where(lane < 2 * own * shares, step, 0.0)
        steps.append(step)
        dbias = dbias + jnp.sum(step, axis=0, keepdims=True)
        ddecay = ddecay + jnp.sum(through, axis=0, keepdims=True)
    dstep[0:1, :] = dbias
    dstep[1:2, :] = ddecay

    for k in range(4):
        for c in range(blocks):
            at = chunk_rows(c)
            uv = su[k, at, :]
            sig = sigmoid(uv)
            dsu[chunk_rows(c, HALO), :] = dst[k, at, :] * sig * (1.0 + uv * (1.0 - sig))
        for m in range(TAPS):
            dsk[k, m : m + 1, :] = jnp.zeros((1, LANES), F32)
        for start, size in [(0, HALO)] + [(HALO + c * SPAN, SPAN) for c in range(blocks)]:
            old = side[k, pl.ds(start, size), :]
            dv = jnp.zeros((size, LANES), F32)
            for m in range(TAPS):
                shifted = dsu[pl.ds(start + TAPS - 1 - m, size), :]
                dv = dv + sk[k, m : m + 1, :] * shifted
                dsk[k, m : m + 1, :] += jnp.sum(old * shifted, axis=0, keepdims=True)
            if start >= HALO:
                moved = pltpu.roll(steps[(start - HALO) // SPAN], (ns - 2 * own * k) % LANES, 1)
                here = (lane >= ns) & (lane < ns + 2 * own)
                dv = dv + jnp.where(here, moved, 0.0)
            dp[k, pl.ds(start, size), pl.ds(cols, LANES)] = dv.astype(BF16)


def last_kernel(cfg, *refs):
    n = cfg["pieces"]
    ids, halo, inputs, normed, dp, w1, gx = refs[:7]
    gn, dgain = refs[7:9]
    pieces = refs[9 : 9 + n]
    (held,) = refs[9 + n :]
    shares, rows = cfg["shares"], cfg["rows"]

    def project(d, _):
        j = (ids[0] + shares - d) % shares
        held[...] = mm(normed[...], dp[j], TN).astype(BF16)
        take_grads(ids, pieces, held, d, cfg["per"])
        back = mm(dp[j], w1[j], NT)

        @pl.when(d == 0)
        def _():
            gn[...] = back

        @pl.when(d > 0)
        def _():
            gn[...] += back

        return 0

    lax.fori_loop(0, shares, project, 0)
    gn[HALO:, :] += gx[...]

    def plain(block):
        wide = block.astype(F32)
        return wide * lax.rsqrt(jnp.mean(wide * wide, axis=1, keepdims=True) + EPSILON)

    total = jnp.sum(gn[0:HALO, :] * plain(halo[...]), axis=0, keepdims=True)
    for c in range(rows // SPAN):
        total = total + jnp.sum(
            gn[chunk_rows(c, HALO), :] * plain(inputs[chunk_rows(c), :]), axis=0, keepdims=True
        )
    dgain[...] = jnp.broadcast_to(total, dgain.shape)


def finish_kernel(cfg, inputs, cot, gain, gn, edge, out):
    rows = cfg["rows"]
    for c in range(rows // SPAN):
        at = chunk_rows(c)
        wide = inputs[at, :].astype(F32)
        g = gn[chunk_rows(c, HALO), :]
        if c == rows // SPAN - 1:
            g = jnp.concatenate([g[: SPAN - HALO], g[SPAN - HALO :] + edge[...]], axis=0)
        scale = lax.rsqrt(jnp.mean(wide * wide, axis=1, keepdims=True) + EPSILON)
        f = g * gain[...]
        mean = jnp.mean(f * wide, axis=1, keepdims=True)
        grad = cot[at, :].astype(F32) + scale * f - wide * (scale * scale * scale) * mean
        out[at, :] = grad.astype(BF16)


def shards(
    inputs, gate_weight, value_weight, step_weight, shared_weight, output_weight, value_kernel,
    shared_kernel, step_bias, decay_log, skip_gain, input_gain, output_gain, cotangent,
):
    shares, groups = lax.axis_size("tensor"), lax.axis_size("dp")
    z, g = lax.axis_index("tensor"), lax.axis_index("dp")
    rows, width = inputs.shape
    per, cols = gate_weight.shape
    own = step_weight.shape[2]
    heads = own * shares
    head = cols // own
    ns = shared_weight.shape[1] // 4
    inner = cols * shares
    blocks = rows // SPAN
    fast = groups == 8 and per % 32 == 0
    n = groups if fast else 1
    cfg = dict(
        shares=shares, own=own, head=head, cols=cols, rows=rows, state=ns, per=per, pieces=n
    )
    ids = jnp.stack([z, g]).astype(jnp.int32)
    ext = HALO + rows
    side_w = LANES
    pk = cols + side_w

    shared_own = lax.dynamic_slice_in_dim(shared_weight, z * ns, ns, 1)
    flat_step = step_weight.reshape(per, 2 * own)
    pack1 = jnp.concatenate(
        [value_weight, shared_own, flat_step, jnp.zeros((per, side_w - ns - 2 * own), BF16)], axis=1
    )
    pack2 = jnp.concatenate([gate_weight, output_weight.T], axis=1)
    halo = lax.ppermute(inputs[rows - HALO :], "tensor", [(i, i + 1) for i in range(shares - 1)])
    parts1 = gather_weights(pack1, shares, groups, fast)
    parts2 = gather_weights(pack2, shares, groups, fast)

    def by_share(v):
        v = v.reshape(v.shape[0], shares, cols).transpose(1, 0, 2)
        return jnp.pad(v, ((0, 0), (0, 8 - v.shape[1]), (0, 0)))

    vk = by_share(value_kernel)
    sk = jnp.pad(
        shared_kernel.reshape(TAPS, 4, ns).transpose(1, 0, 2), ((0, 0), (0, 8 - TAPS), (0, side_w - ns))
    )

    def by_lane(v):
        v = v.reshape(2, shares, own).transpose(1, 0, 2).reshape(1, 2 * heads)
        return jnp.pad(v, ((0, 0), (0, LANES - 2 * heads)))

    bias = by_lane(step_bias)
    rate = by_lane(jnp.broadcast_to(-jnp.exp(decay_log), (2, heads)))
    skip = jnp.repeat(skip_gain, head).reshape(shares, 1, cols)
    ogain = output_gain.reshape(shares, 1, cols)
    gain = input_gain.reshape(1, width)

    pay_shape = sds((shares, ns, cols), BF16)
    front = call(
        functools.partial(front_kernel, cfg),
        (
            sds((shares, width, pk), BF16),
            sds((ext, width), BF16),
            sds((shares, ext, cols), BF16),
            sds((shares, rows, cols), BF16),
            sds((shares, rows, cols), BF16),
            sds((shares, ext, side_w)),
            sds((4, rows, side_w)),
            sds((4, rows, side_w), BF16),
            sds((rows, LANES)),
            sds((rows, LANES)),
            sds((blocks, LANES, SPAN)),
            sds((blocks, LANES, SPAN)),
            sds((4, rows, LANES)),
            sds((shares, 2, blocks, ns, cols)),
            sds((2 * blocks + 8, LANES)),
            pay_shape, pay_shape, pay_shape,
        ),
        scratch=[pltpu.VMEM((ext, pk), F32)],
        flops=2 * ext * width * pk * shares,
    )
    (
        w1, normed, vext, u, x, side, su, bc, c2, rho2, c2t, rho2t, dec, states, tots, pay1, pay2, pay3,
    ) = front(ids, halo, inputs, gain, vk, sk, bias, rate, *parts1)
    send = tots[2 * blocks :]

    def shift(v, d):
        return lax.ppermute(v, "tensor", cyclic(shares, d))

    l1, l2, l3 = (shift(send, d) for d in (1, 2, 3))
    r1, r2, r3 = shift(pay1, 1), shift(pay2, 2), shift(pay3, 3)

    yin = call(
        functools.partial(within_kernel, cfg),
        sds((shares, rows, cols)),
        smem_first=False,
        flops=2 * rows * SPAN * inner * 2,
    )(bc, c2, rho2t, x)
    w2, gate, gn_out = call(
        functools.partial(gate_kernel, cfg),
        (sds((shares, width, 2 * cols), BF16), sds((shares, rows, cols)), sds((shares, rows, cols))),
        flops=4 * rows * width * inner,
    )(ids, normed, cotangent, *parts2)

    middle = call(
        functools.partial(middle_kernel, cfg),
        (
            sds((shares, 2, blocks, ns, cols), BF16),
            sds((shares, rows, cols), BF16),
            sds((shares, rows, cols), BF16),
            sds((shares, rows, cols), BF16),
            sds((shares, 2, rows, cols), BF16),
            sds((rows, LANES)),
            sds((shares, 2, blocks, ns, cols)),
            pay_shape, pay_shape, pay_shape,
            sds((shares, 1, cols)),
            sds((shares, 1, cols)),
        ),
        scratch=[pltpu.VMEM((shares, SPAN, cols), F32)] * 3,
        flops=rows * inner * 512,
    )
    enter, dy, normal, dgate, edy, rr, dlocal, q1, q2, q3, dskip, dogain = middle(
        ids, yin, x, gate, gn_out, states, bc, dec, tots, l1, l2, l3, r1, r2, r3, skip, ogain
    )
    s1, s2, s3 = shift(q1, 1), shift(q2, 2), shift(q3, 3)

    def piece_shapes(c):
        if fast:
            return tuple(sds((shares, per, c), BF16) for _ in range(n))
        return (sds((shares, width, c), BF16),)

    mixed, gx, *grads2 = call(
        functools.partial(output_kernel, cfg),
        (sds((rows, width)), sds((rows, width))) + piece_shapes(2 * cols),
        scratch=[pltpu.VMEM((width, 2 * cols), BF16)],
        flops=8 * rows * width * inner,
    )(ids, inputs, cotangent, normed, normal, dgate, w2)
    mixed = mixed.astype(BF16)
    out2 = scatter_grads(grads2, shares, groups, fast)

    dxi, dbc, da, dk = call(
        functools.partial(back_within_kernel, cfg),
        (sds((shares, rows, cols)), sds((4, rows, side_w)), sds((rows, LANES)), sds((rows, LANES))),
        scratch=[pltpu.VMEM((LANES, SPAN), F32), pltpu.VMEM((LANES, SPAN), F32)],
        smem_first=False,
        flops=2 * rows * SPAN * inner * 8,
    )(bc, rho2, c2t, x, dy)

    dp, dvk, dsk, dstep = call(
        functools.partial(tail_kernel, cfg),
        (
            sds((shares, ext, pk), BF16), sds((shares, 8, cols)), sds((4, 8, side_w)), sds((8, LANES)),
        ),
        scratch=[
            pltpu.VMEM((ext + HALO, cols), F32),
            pltpu.VMEM((ext + HALO, side_w), F32),
            pltpu.VMEM((4, rows, side_w), F32),
            pltpu.VMEM((2, blocks, ns, cols), BF16),
            pltpu.VMEM((8, LANES), F32),
            pltpu.VMEM((rows, LANES), F32),
        ],
        flops=rows * inner * 1024,
    )(
        ids, x, u, dy, dxi, vext, side, su, bc, dbc, dec, tots, enter, edy, rr, da, dk, dlocal,
        l1, l2, l3, s1, s2, s3, skip, vk, sk,
    )

    gn, dgain, *grads1 = call(
        functools.partial(last_kernel, cfg),
        (sds((ext, width)), sds((8, width))) + piece_shapes(pk),
        scratch=[pltpu.VMEM((width, pk), BF16)],
        flops=4 * ext * width * pk * shares,
    )(ids, halo, inputs, normed, dp, w1, gx)
    edge = lax.ppermute(gn[:HALO], "tensor", [(i + 1, i) for i in range(shares - 1)])
    out1 = scatter_grads(grads1, shares, groups, fast)
    grad_input = call(
        functools.partial(finish_kernel, cfg), sds((rows, width), BF16), smem_first=False
    )(inputs, cotangent, gain, gn, edge)

    parts = [
        dvk[:, :TAPS, :].transpose(1, 0, 2).reshape(-1),
        dsk[:, :TAPS, :ns].transpose(1, 0, 2).reshape(-1),
        dstep[0],
        dstep[1],
        dskip.reshape(heads, head).sum(axis=1),
        dgain[0],
        dogain.reshape(-1),
    ]
    sizes = [p.shape[0] for p in parts]
    flat = jnp.concatenate(parts)
    pad = -flat.shape[0] % 1024
    flat = jnp.pad(flat, (0, pad)).reshape(-1, LANES)
    flat = sum_all(flat, shares, groups, fast).reshape(-1)
    outs, start = [], 0
    for size in sizes:
        outs.append(flat[start : start + size])
        start += size

    def from_lane(v):
        return v[: 2 * heads].reshape(shares, 2, own).transpose(1, 0, 2).reshape(2, heads)

    grad_step = out1[:, cols + ns : cols + ns + 2 * own].reshape(per, 2, own)
    shared_all = lax.all_gather(out1[:, cols : cols + ns], "tensor", axis=1, tiled=True)
    return (
        mixed,
        grad_input,
        out2[:, :cols],
        out1[:, :cols],
        grad_step,
        shared_all,
        out2[:, cols:].T,
        outs[0].reshape(TAPS, inner),
        outs[1].reshape(TAPS, 4 * ns),
        from_lane(outs[2]),
        from_lane(outs[3]).sum(axis=0),
        outs[4],
        outs[5],
        outs[6],
    )


def solution(mesh):
    both = P(("dp", "tensor"), None)
    placed = (
        both, P("dp", "tensor"), P("dp", "tensor"), P("dp", None, "tensor"), P("dp", None),
        P("tensor", "dp"), P(), P(), P(), P(), P(), P(), P(), both,
    )
    return jax.shard_map(
        shards,
        mesh=mesh,
        in_specs=placed,
        out_specs=(
            both, both, P("dp", "tensor"), P("dp", "tensor"), P("dp", None, "tensor"), P("dp", None),
            P("tensor", "dp"), P(), P(), P(), P(), P(), P(), P(),
        ),
        check_vma=False,
    )
```

```python
import functools

import jax
import jax.numpy as jnp
from jax import lax
from jax.experimental import pallas as pl
from jax.experimental.pallas import tpu as pltpu
from jax.sharding import PartitionSpec as P

F32 = jnp.float32
BF16 = jnp.bfloat16
EPSILON = 1e-06
SPAN = 128
HALO = 16
TAPS = 4
LANES = 128
LOG2E = 1.4426950408889634
EXACT = lax.Precision.HIGHEST
LIMIT = 24 * 1024 * 1024

NN = (((1,), (0,)), ((), ()))
NT = (((1,), (1,)), ((), ()))
TN = (((0,), (0,)), ((), ()))


def mm(a, b, dims=NN, precision=None):
    return lax.dot_general(a, b, dims, preferred_element_type=F32, precision=precision)


def iota(shape, dim):
    return lax.broadcasted_iota(jnp.int32, shape, dim)


def sigmoid(v):
    return 0.5 * jnp.tanh(0.5 * v) + 0.5


def split(v, n):
    parts = []
    for _ in range(n):
        part = v.astype(BF16)
        parts.append(part)
        v = v - part.astype(F32)
    return parts


def mm_right(ones, v, n):
    total = None
    for part in split(v, n):
        term = mm(ones, part)
        total = term if total is None else total + term
    return total


def mm_left(v, ones, n, dims=(((1,), (0,)), ((), ()))):
    total = None
    for part in split(v, n):
        term = mm(part, ones, dims)
        total = term if total is None else total + term
    return total


def fold(v):
    return v.reshape(v.shape[0] // 8, 8, v.shape[1]).sum(axis=0)


def chunk_rows(c, base=0):
    return pl.ds(base + c * SPAN, SPAN)


def call(kernel, out_shape, scratch=(), us=1.0, limit=LIMIT):
    def run(*args):
        specs = [
            pl.BlockSpec(memory_space=pltpu.SMEM if i == 0 else pltpu.VMEM)
            for i in range(len(args))
        ]
        return pl.pallas_call(
            kernel,
            out_shape=out_shape,
            in_specs=specs,
            out_specs=jax.tree.map(lambda _: pl.BlockSpec(memory_space=pltpu.VMEM), out_shape),
            scratch_shapes=list(scratch),
            cost_estimate=pl.CostEstimate(
                flops=int(us * 1.1e9), bytes_accessed=int(us * 3.0e6), transcendentals=0
            ),
            compiler_params=pltpu.CompilerParams(vmem_limit_bytes=limit),
        )(*args)

    return run


def sds(shape, dtype=F32):
    return jax.ShapeDtypeStruct(shape, dtype)


def put_weights(ids, pieces, full, shares, per):
    if len(pieces) == 1:
        full[...] = pieces[0][...]
        return
    for rel, piece in enumerate(pieces):
        row = pl.multiple_of((ids[1] ^ rel) * per, per)
        for d in range(shares):
            j = (ids[0] + shares - d) % shares
            full[j, pl.ds(row, per), :] = piece[d]


def take_grads(ids, pieces, held, d, per):
    if len(pieces) == 1:
        shares = pieces[0].shape[0]
        pieces[0][(ids[0] + shares - d) % shares] = held[...]
        return
    for rel in range(2 * pieces[0].shape[0]):
        row = pl.multiple_of((ids[1] ^ rel) * per, per)
        pieces[rel % 2][rel // 2, d] = held[pl.ds(row, per), :]


def cyclic(size, d):
    return [(i, (i + d) % size) for i in range(size)]


def xor(size, bit):
    return [(i, i ^ bit) for i in range(size)]


def along(v, d, shares):
    return lax.ppermute(v, "tensor", cyclic(shares, d))


def after(values, *others):
    out = lax.optimization_barrier((values,) + others)
    return out[0]


def sum_kernel(ids, *refs):
    parts, out, held = refs[:-2], refs[-2], refs[-1]
    for k, part in enumerate(parts):
        held[k] = part[...]
    total = held[ids[0]]
    for m in range(1, len(parts)):
        total = total + held[ids[m]]
    out[...] = total


def pair_kernel(ids, keep, other, *outs):
    for k, out in enumerate(outs):
        out[...] = (keep[k].astype(F32) + other[k].astype(F32)).astype(BF16)


def quad_kernel(cfg, first, ids, *refs):
    n, shares, cols = cfg["groups"] // 2, cfg["shares"], cfg["cols"]
    parts, outs = refs[:n], refs[n:]
    sides = []
    for d in range(shares):
        total = parts[0][d].astype(F32)
        for part in parts[1:]:
            total = total + part[d].astype(F32)
        if first:
            outs[d][:, :cols] = total[:, :cols].astype(BF16)
            sides.append(total[:, cols:])
        else:
            outs[d][...] = total.astype(BF16)
    if first:
        low = iota(sides[0].shape, 1) < cfg["state"]
        half = LANES // 2
        for d in range(shares):
            out = outs[d]
            for k in range(shares // 2):
                both = jnp.where(low, sides[2 * k], pltpu.roll(sides[2 * k + 1], half, 1))
                out[:, cols + k * LANES : cols + (k + 1) * LANES] = both.astype(BF16)
            step = jnp.where(low, pltpu.roll(sides[d], half, 1), 0.0)
            out[:, cols + shares * half :] = step.astype(BF16)


def line_kernel(cfg, ids, *refs):
    shares, cols, ns = cfg["shares"], cfg["cols"], cfg["state"]
    parts = refs[:shares]
    value, step, shared, held = refs[shares:]
    own = parts[0][:, :cols].astype(F32)
    side = parts[0][:, cols + shares * ns :].astype(F32)
    for part in parts[1:]:
        own = own + part[:, :cols].astype(F32)
        side = side + part[:, cols + shares * ns :].astype(F32)
    value[...] = own
    step[...] = side[:, : step.shape[1]]
    wide = shares * ns
    for e in range(shares):
        kinds = parts[e][:, cols : cols + wide].astype(F32)
        held[e] = pltpu.roll(kinds, (wide - ns * e) % wide, 1) if e else kinds
    total = held[(shares - ids[0]) % shares]
    for q in range(1, shares):
        total = total + held[(q + shares - ids[0]) % shares]
    turned = jnp.concatenate(
        [total[:, ((shares - m) % shares) * ns :][:, :ns] for m in range(shares)], axis=1
    )
    shared[...] = pltpu.roll(turned, ids[0] * ns, 1)


def line2_kernel(cfg, ids, *refs):
    shares, cols = cfg["shares"], cfg["cols"]
    parts = refs[:shares]
    gate, out = refs[shares:]
    total = parts[0][...].astype(F32)
    for part in parts[1:]:
        total = total + part[...].astype(F32)
    gate[...] = total[:, :cols]
    out[...] = total[:, cols:]


def fill_spread(cfg, spread):
    own, head, cols = cfg["own"], cfg["head"], cfg["cols"]
    lane = iota((LANES, cols), 0)
    place = iota((LANES, cols), 1) // head
    for k in range(2 * cfg["shares"]):
        spread[k] = (lane == own * k + place).astype(F32).astype(BF16)


def front_kernel(cfg, *refs):
    n = cfg["pieces"]
    ids, halo, inputs, gain, vk, sk, params = refs[:7]
    pieces = refs[7 : 7 + n]
    (
        w1, normed, vext, u_out, x_out, side, su_out, bc_out, bct, c2, rho2, c2t, rho2t, dec, states, tots,
        spread, pay1, pay2, pay3, acc,
    ) = refs[7 + n :]
    shares, own, cols, rows, ns = (cfg[k] for k in ("shares", "own", "cols", "rows", "state"))
    blocks = rows // SPAN
    put_weights(ids, pieces, w1, shares, cfg["per"])
    fill_spread(cfg, spread)

    def norm(block):
        wide = block.astype(F32)
        scale = lax.rsqrt(jnp.mean(wide * wide, axis=1, keepdims=True) + EPSILON)
        return (wide * scale * gain[...]).astype(BF16)

    normed[0:HALO, :] = norm(halo[...])
    for c in range(2 * blocks):
        size = SPAN // 2
        normed[pl.ds(HALO + c * size, size), :] = norm(inputs[pl.ds(c * size, size), :])

    def project(j, _):
        acc[...] = mm(normed[...], w1[j])
        side[j] = acc[:, cols : cols + LANES]
        for c in range(blocks):
            vext[j, chunk_rows(c), :] = acc[chunk_rows(c), :cols].astype(BF16)
        vext[j, blocks * SPAN :, :] = acc[blocks * SPAN :, :cols].astype(BF16)
        for c in range(blocks):
            for p in range(cols // LANES + 1):
                lanes = pl.ds(p * LANES, LANES)
                u = None
                for m in range(TAPS):
                    if p < cols // LANES:
                        tap = vk[m : m + 1, pl.ds(pl.multiple_of(j * cols + p * LANES, LANES), LANES)]
                    else:
                        tap = sk[j, m : m + 1, :]
                    term = tap * acc[chunk_rows(c, HALO - TAPS + 1 + m), lanes]
                    u = term if u is None else u + term
                v = u * sigmoid(u)
                if p < cols // LANES:
                    u_out[j, chunk_rows(c), lanes] = u.astype(BF16)
                    x_out[j, chunk_rows(c), lanes] = v.astype(BF16)
                else:
                    su_out[j, chunk_rows(c), :] = u
                    bc_out[j, chunk_rows(c), :] = v.astype(BF16)
                    bct[j, c] = v.T.astype(BF16)
        return 0

    lax.fori_loop(0, shares, project, 0)

    lane = iota((SPAN, LANES), 1)
    is_fwd = lane % (2 * own) < own
    at0, at1 = iota((SPAN, SPAN), 0), iota((SPAN, SPAN), 1)
    both = jnp.concatenate([(at0 >= at1).astype(F32), (at0 <= at1).astype(F32)], axis=0).astype(BF16)
    rate = jnp.where(iota((1, LANES), 1) < 2 * own * shares, -jnp.exp(params[1:2, :]), 0.0)
    for c in range(blocks):
        raw = jnp.zeros((SPAN, LANES), F32)
        for j in range(shares):
            moved = pltpu.roll(side[j, chunk_rows(c, HALO), :], (2 * own * j - ns) % LANES, 1)
            raw = jnp.where((lane >= 2 * own * j) & (lane < 2 * own * (j + 1)), moved, raw)
        v = raw + params[0:1, :]
        small = jnp.exp(jnp.minimum(v, 0.0))
        dt = jnp.where(v < -15.0, small, jnp.maximum(v, 0.0) + jnp.log1p(jnp.exp(-jnp.abs(v))))
        log_dt = jnp.where(v < -15.0, v, jnp.log(jnp.maximum(dt, 1e-30)))
        ratio = jnp.where(v < -15.0, 1.0, sigmoid(v) / jnp.maximum(dt, 1e-30))
        a = dt * rate
        sums = mm_right(both, a, 3)
        cum = jnp.where(is_fwd, sums[:SPAN], sums[SPAN:])
        tot = jnp.sum(a, axis=0, keepdims=True)
        rho = cum - log_dt
        cc = cum * LOG2E
        rr = rho * LOG2E
        c2[chunk_rows(c), :] = cc
        rho2[chunk_rows(c), :] = rr
        c2t[c] = cc.T
        rho2t[c] = rr.T
        dec[0, chunk_rows(c), :] = a
        dec[1, chunk_rows(c), :] = ratio
        dec[2, chunk_rows(c), :] = jnp.exp(tot - rho)
        dec[3, chunk_rows(c), :] = jnp.exp(cum)
        tots[c : c + 1, :] = tot
    fwd1 = iota((1, LANES), 1) % (2 * own) < own
    zero = jnp.zeros((1, LANES), F32)
    lead = []
    for c in range(blocks):
        later, sooner = zero, zero
        for k in range(blocks):
            if k > c:
                later = later + tots[k : k + 1, :]
            if k < c:
                sooner = sooner + tots[k : k + 1, :]
        lead.append(jnp.exp(jnp.where(fwd1, later, sooner)))
        tots[blocks + c : blocks + c + 1, :] = jnp.where(fwd1, sooner, later)
    lead = jnp.concatenate(lead + [zero] * (8 - blocks), axis=0)
    whole = tots[0:1, :]
    for c in range(1, blocks):
        whole = whole + tots[c : c + 1, :]
    extra = jnp.concatenate([p.astype(F32) for p in split(whole, 3)] + [zero] * (HALO - 3), axis=0)
    extra = jnp.concatenate([extra, jnp.zeros((HALO, cols - LANES), F32)], axis=1).astype(BF16)
    for pay in (pay1, pay2, pay3):
        pay[shares * ns :, :] = extra

    def sums(j, _):
        dev = []
        for d in range(2):
            grow = spread[2 * j + d]
            wide = mm_left(lead, grow, 2)
            total = jnp.zeros((ns, cols), F32)
            for c in range(blocks):
                weight = mm(dec[2, chunk_rows(c), :].astype(BF16), grow)
                xw = (weight * x_out[j, chunk_rows(c), :].astype(F32)).astype(BF16)
                s = mm(bct[2 * d, c, :ns, :], xw)
                states[j, d, c] = s
                total = total + wide[c : c + 1, :] * s
            dev.append(total)
        at = pl.ds(pl.multiple_of(j * ns, ns), ns)
        for dist, pay in ((1, pay1), (2, pay2), (3, pay3)):
            pay[at, :] = jnp.where(ids[0] + dist < shares, dev[0], dev[1]).astype(BF16)
        return 0

    lax.fori_loop(0, shares, sums, 0)


def stack_pair(first, v):
    zero = jnp.zeros_like(v)
    return jnp.concatenate([jnp.where(first, v, zero), jnp.where(first, zero, v)], axis=0)


def within_kernel(cfg, ids, bc, c2, rho2t, x, y):
    shares, own, rows = (cfg[k] for k in ("shares", "own", "rows"))
    t, s = iota((SPAN, SPAN), 0), iota((SPAN, SPAN), 1)
    low = t > s
    first = iota((SPAN, LANES), 1) < cfg["head"]

    def block(c, _):
        at = pl.ds(pl.multiple_of(c * SPAN, SPAN), SPAN)
        g = jnp.where(low, mm(bc[1, at, :], bc[0, at, :], NT), mm(bc[3, at, :], bc[2, at, :], NT))
        g = jnp.where(t == s, 0.0, g)
        cc = c2[at, :]
        for j in range(shares):
            for p in range(own // 2):
                mats = []
                for i in (2 * p, 2 * p + 1):
                    f, b = 2 * own * j + i, 2 * own * j + own + i
                    col = jnp.where(low, cc[:, f : f + 1], cc[:, b : b + 1])
                    row = jnp.where(low, rho2t[c, f : f + 1, :], rho2t[c, b : b + 1, :])
                    mats.append((jnp.exp2(col - row) * g).astype(BF16))
                lanes = slice(p * LANES, (p + 1) * LANES)
                y[j, at, lanes] = mm(jnp.concatenate(mats, axis=1), stack_pair(first, x[j, at, lanes]))
        return 0

    lax.fori_loop(0, rows // SPAN, block, 0)


def gate_kernel(cfg, *refs):
    n = cfg["pieces"]
    ids, normed, cot = refs[:3]
    pieces = refs[3 : 3 + n]
    w2, gate, gn = refs[3 + n :]
    shares, cols, rows = (cfg[k] for k in ("shares", "cols", "rows"))
    put_weights(ids, pieces, w2, shares, cfg["per"])

    def project(j, _):
        gate[j] = mm(normed[HALO : HALO + rows, :], w2[j, :, :cols])
        gn[j] = mm(cot[...], w2[j, :, cols:])
        return 0

    lax.fori_loop(0, shares, project, 0)


def incoming(ids, cfg, r1, r2, r3, j, near, far):
    z, shares, ns = ids[0], cfg["shares"], cfg["state"]
    at = pl.ds(pl.multiple_of(j * ns, ns), ns)

    def keep(test, ref):
        return jnp.where(test, ref[at, :].astype(F32), 0.0)

    before = keep(z >= 1, r1) + near[0] * keep(z >= 2, r2) + near[1] * keep(z >= 3, r3)
    behind = (
        keep(z <= shares - 2, r3)
        + far[0] * keep(z <= shares - 3, r2)
        + far[1] * keep(z <= shares - 4, r1)
    )
    return before, behind


def middle_kernel(cfg, *refs):
    (
        ids, yin, x, gate, gn, states, bc, bct, dec, tots, spread, params, ogain, r1, r2, r3,
        enter, dy, normal, dgate, edy, rr, dlocal, rowsum, keeps, p1, p2, p3,
        ys, acts, ef, eb,
    ) = refs
    shares, own, cols, rows, ns = (cfg[k] for k in ("shares", "own", "cols", "rows", "state"))
    blocks, inner = rows // SPAN, cols * shares
    zero = jnp.zeros((1, LANES), F32)

    def whole(r):
        at = pl.ds(shares * ns, HALO)
        v = r[at, :LANES].astype(F32)
        return v[0:1, :] + v[1:2, :] + v[2:3, :]

    l1, l2, l3 = whole(r1), whole(r2), whole(r3)
    lines = [tots[c : c + 1, :] for c in range(2 * blocks)] + [l1, l1 + l2, l3, l3 + l2]
    lines = jnp.exp(jnp.concatenate(lines + [zero] * (HALO - len(lines)), axis=0))
    skip_rows = jnp.concatenate([params[2:3, :]] + [zero] * 7, axis=0)

    def grow_lines(j, _):
        for d in range(2):
            keeps[j, d] = mm_left(lines, spread[2 * j + d], 2)
        keeps[j, 2, 0:8] = mm_left(skip_rows, spread[2 * j], 2)
        return 0

    lax.fori_loop(0, shares, grow_lines, 0)

    def enter_states(j, _):
        kf, kb = keeps[j, 0], keeps[j, 1]
        b = 2 * blocks
        e, e_b = incoming(
            ids, cfg, r1, r2, r3, j,
            (kf[b : b + 1, :], kf[b + 1 : b + 2, :]), (kb[b + 2 : b + 3, :], kb[b + 3 : b + 4, :]),
        )
        for c in range(blocks):
            enter[j, 0, c] = e.astype(BF16)
            e = kf[c : c + 1, :] * e + states[j, 0, c]
        for c in reversed(range(blocks)):
            enter[j, 1, c] = e_b.astype(BF16)
            e_b = kb[c : c + 1, :] * e_b + states[j, 1, c]
        return 0

    lax.fori_loop(0, shares, enter_states, 0)
    rowsum[...] = jnp.zeros_like(rowsum)
    pages = cols // LANES

    def block(c, _):
        at = pl.ds(pl.multiple_of(c * SPAN, SPAN), SPAN)
        ec = dec[3, at, :].astype(BF16)

        def first(j, sums):
            square, dot = sums
            for p in range(pages):
                lanes = slice(p * LANES, (p + 1) * LANES)
                cf = mm(bc[1, at, :ns], enter[j, 0, c, :, lanes]) * mm(ec, spread[2 * j, :, lanes])
                cb = mm(bc[3, at, :ns], enter[j, 1, c, :, lanes]) * mm(ec, spread[2 * j + 1, :, lanes])
                ef[j, :, lanes] = cf.astype(BF16)
                eb[j, :, lanes] = cb.astype(BF16)
                v = yin[j, at, lanes] + keeps[j, 2, 0:1, lanes] * x[j, at, lanes].astype(F32) + cf + cb
                ys[j, :, lanes] = v
                g = gate[j, at, lanes]
                act = g * sigmoid(g)
                acts[j, :, lanes] = act
                gated = v * act
                square = square + gated * gated
                dot = dot + gn[j, at, lanes] * ogain[j, :, lanes] * gated
            return square, dot

        blank = jnp.zeros((SPAN, LANES), F32)
        square, dot = lax.fori_loop(0, shares, first, (blank, blank))
        square = jnp.sum(square, axis=1, keepdims=True)
        dot = jnp.sum(dot, axis=1, keepdims=True)
        inv = lax.rsqrt(square / inner + EPSILON)
        back = inv * inv * inv * dot / inner

        def second(j, total):
            for p in range(pages):
                lanes = slice(p * LANES, (p + 1) * LANES)
                v, act, g = ys[j, :, lanes], acts[j, :, lanes], gate[j, at, lanes]
                gnv, og = gn[j, at, lanes], ogain[j, :, lanes]
                sig = sigmoid(g)
                gated = v * act
                scaled = gated * inv
                normal[j, at, lanes] = (scaled * og).astype(BF16)
                rowsum[j, 0, :, lanes] += fold(gnv * scaled)
                dgated = inv * (gnv * og) - gated * back
                d_scan = dgated * act
                low = d_scan.astype(BF16)
                dy[j, at, lanes] = low
                dgate[j, at, lanes] = (dgated * v * (sig + act * (1.0 - sig))).astype(BF16)
                rowsum[j, 1, :, lanes] += fold(d_scan * x[j, at, lanes].astype(F32))
                for d, kept in ((0, ef), (1, eb)):
                    product = (d_scan * kept[j, :, lanes].astype(F32)).astype(BF16)
                    total = total + mm(product, spread[2 * j + d, :, lanes], NT)
                    wide = (mm(ec, spread[2 * j + d, :, lanes]) * d_scan).astype(BF16)
                    edy[j, d, at, lanes] = wide
                    dlocal[j, d, c, :, lanes] = mm(bct[1 + 2 * d, c, :ns, :], wide)
            return total

        rr[at, :] = lax.fori_loop(0, shares, second, blank)
        return 0

    lax.fori_loop(0, blocks, block, 0)
    for pay in (p1, p2, p3):
        pay[shares * ns :, :] = jnp.zeros((HALO, cols), BF16)

    def leave(j, _):
        dev = []
        for d in range(2):
            total = jnp.zeros((ns, cols), F32)
            for c in range(blocks):
                total = total + keeps[j, d, blocks + c : blocks + c + 1, :] * dlocal[j, d, c]
            dev.append(total)
        at = pl.ds(pl.multiple_of(j * ns, ns), ns)
        for dist, pay in ((1, p1), (2, p2), (3, p3)):
            pay[at, :] = jnp.where(ids[0] + dist < shares, dev[1], dev[0]).astype(BF16)
        return 0

    lax.fori_loop(0, shares, leave, 0)


def output_kernel(cfg, *refs):
    ids, inputs, cot, normed, normal, dgate, w2 = refs[:7]
    mixed, gx = refs[7:9]
    pieces, (total, held) = refs[9:-2], refs[-2:]
    shares, cols, rows = (cfg[k] for k in ("shares", "cols", "rows"))

    def project(d, _):
        j = (ids[0] + shares - d) % shares
        held[:, :cols] = mm(normed[HALO : HALO + rows, :], dgate[j], TN).astype(BF16)
        held[:, cols:] = mm(cot[...], normal[j], TN).astype(BF16)
        take_grads(ids, pieces, held, d, cfg["per"])
        part = mm(normal[j], w2[j, :, cols:], NT)
        back = mm(dgate[j], w2[j, :, :cols], NT)

        @pl.when(d == 0)
        def _():
            total[...] = part
            gx[...] = back

        @pl.when(d > 0)
        def _():
            total[...] += part
            gx[...] += back

        return 0

    lax.fori_loop(0, shares, project, 0)
    mixed[...] = (total[...] + inputs[...].astype(F32)).astype(BF16)


def back_within_kernel(cfg, ids, bc, bct, rho2, c2t, x, dy, edy, enter, rr, keeps, dx, dbc, da, dk, das, ras):
    shares, own, rows, ns = (cfg[k] for k in ("shares", "own", "rows", "state"))
    s, t = iota((SPAN, SPAN), 0), iota((SPAN, SPAN), 1)
    up = t > s
    first = iota((SPAN, LANES), 1) < cfg["head"]
    after_t = (s >= t).astype(F32).astype(BF16)
    until_t = (s <= t).astype(F32).astype(BF16)
    tri = jnp.concatenate([after_t, until_t], axis=1)
    sums = jnp.concatenate([until_t, after_t], axis=0)
    lane = iota((SPAN, LANES), 1)
    is_fwd = iota((LANES, SPAN), 0) % (2 * own) < own

    def block(c, _):
        at = pl.ds(pl.multiple_of(c * SPAN, SPAN), SPAN)
        g = jnp.where(up, mm(bc[0, at, :], bc[1, at, :], NT), mm(bc[2, at, :], bc[3, at, :], NT))
        g = jnp.where(t == s, 0.0, g)
        rho = rho2[at, :]
        dg = jnp.zeros((SPAN, SPAN), F32)
        das[...] = jnp.zeros_like(das)
        ras[...] = jnp.zeros_like(ras)
        for j in range(shares):
            for p in range(own // 2):
                lanes = slice(p * LANES, (p + 1) * LANES)
                dyp = dy[j, at, lanes]
                dm = mm(stack_pair(first, x[j, at, lanes]), dyp, NT)
                ws, zs = [], []
                for q in range(2):
                    i = 2 * p + q
                    f, b = 2 * own * j + i, 2 * own * j + own + i
                    row = jnp.where(up, c2t[c, f : f + 1, :], c2t[c, b : b + 1, :])
                    col = jnp.where(up, rho[:, f : f + 1], rho[:, b : b + 1])
                    pw = jnp.exp2(row - col)
                    ud = dm[q * SPAN : (q + 1) * SPAN] * pw
                    dg = dg + ud
                    ws.append((pw * g).astype(BF16))
                    zd = ud * g
                    zs.append(zd.astype(BF16))
                    rf = jnp.sum(jnp.where(up, zd, 0.0), axis=0, keepdims=True)
                    ras[f : f + 1, :] = rf
                    ras[b : b + 1, :] = jnp.sum(zd, axis=0, keepdims=True) - rf
                back = mm(jnp.concatenate(ws, axis=1), stack_pair(first, dyp))
                dx[j, at, lanes] = back + keeps[j, 2, 0:1, lanes] * dyp.astype(F32)
                cross = mm(jnp.concatenate(zs, axis=0), tri)
                for q in range(2):
                    i = 2 * p + q
                    f, b = 2 * own * j + i, 2 * own * j + own + i
                    part = cross[q * SPAN : (q + 1) * SPAN]
                    das[f : f + 1, :] = jnp.sum(jnp.where(up, part[:, :SPAN], 0.0), axis=0, keepdims=True)
                    das[b : b + 1, :] = jnp.sum(
                        jnp.where(t < s, part[:, SPAN:], 0.0), axis=0, keepdims=True
                    )
        df = jnp.where(up, dg, 0.0)
        db = jnp.where(t < s, dg, 0.0)
        dcf = mm(df.T.astype(BF16), bc[0, at, :])
        dcb = mm(db.T.astype(BF16), bc[2, at, :])
        cf, cb = jnp.zeros((SPAN, ns), F32), jnp.zeros((SPAN, ns), F32)
        for j in range(shares):
            cf = cf + mm(edy[j, 0, at, :], enter[j, 0, c], NT)
            cb = cb + mm(edy[j, 1, at, :], enter[j, 1, c], NT)
        dbc[0, at, :] = mm(df.astype(BF16), bc[1, at, :])
        dbc[1, at, :] = dcf
        dbc[1, at, :ns] += cf
        dbc[2, at, :] = mm(db.astype(BF16), bc[3, at, :])
        dbc[3, at, :] = dcb
        dbc[3, at, :ns] += cb
        a = das[...]
        later = jnp.where(lane < SPAN - 1, pltpu.roll(a, SPAN - 1, 1), 0.0)
        sooner = jnp.where(lane > 0, pltpu.roll(a, 1, 1), 0.0)
        kd = ras[...] - a + jnp.where(is_fwd, later, sooner)
        through = mm_right(sums, rr[at, :], 2)
        da[at, :] = a.T + jnp.where(lane % (2 * own) < own, through[:SPAN], through[SPAN:])
        dk[at, :] = kd.T
        return 0

    lax.fori_loop(0, rows // SPAN, block, 0)


def tail_kernel(cfg, *refs):
    (
        ids, x, u, dxi, vext, side, su, bc, dbc, dec, enter, da, dk, dlocal, rowsum, keeps, spread,
        r1, r2, r3, vk, sk,
        dp, small,
        du, dsu, dst, dstate, xs, qs, taps,
    ) = refs
    shares, own, cols, rows, ns = (cfg[k] for k in ("shares", "own", "cols", "rows", "state"))
    blocks, pages = rows // SPAN, cols // LANES

    xs[...] = jnp.zeros_like(xs)
    du[...] = jnp.zeros_like(du)
    dsu[...] = jnp.zeros_like(dsu)
    dst[...] = dbc[...]

    def chain(j, _):
        kf, kb = keeps[j, 0], keeps[j, 1]
        b = 2 * blocks
        now_b, now_f = incoming(
            ids, cfg, r1, r2, r3, j,
            (kb[b : b + 1, :], kb[b + 1 : b + 2, :]), (kf[b + 2 : b + 3, :], kf[b + 3 : b + 4, :]),
        )
        for d, order, now, kept in (
            (0, list(reversed(range(blocks))), now_f, kf),
            (1, list(range(blocks)), now_b, kb),
        ):
            rows_x = [None] * blocks
            for c in order:
                dstate[j, d, c] = now.astype(BF16)
                rows_x[c] = kept[c : c + 1, :] * jnp.sum(
                    enter[j, d, c].astype(F32) * now, axis=0, keepdims=True
                )
                now = kept[c : c + 1, :] * now + dlocal[j, d, c]
            rows_x = jnp.concatenate(rows_x + [jnp.zeros((8 - blocks, cols), F32)], axis=0)
            xs[...] += mm_left(rows_x, spread[2 * j + d], 2, NT)
        return 0

    lax.fori_loop(0, shares, chain, 0)

    def states_part(c, _):
        at = pl.ds(pl.multiple_of(c * SPAN, SPAN), SPAN)
        weights = dec[2, at, :].astype(BF16)

        def share(j, total):
            for p in range(pages):
                lanes = slice(p * LANES, (p + 1) * LANES)
                xv = x[j, at, lanes].astype(F32)
                dx = dxi[j, at, lanes]
                for d in range(2):
                    grow = spread[2 * j + d, :, lanes]
                    wide = mm(weights, grow)
                    through = mm(bc[2 * d, at, :ns], dstate[j, d, c, :, lanes]) * wide
                    dx = dx + through
                    total = total + mm((through * xv).astype(BF16), grow, NT)
                    dst[2 * d, at, :ns] += mm((wide * xv).astype(BF16), dstate[j, d, c, :, lanes], NT)
                uv = u[j, at, lanes].astype(F32)
                sig = sigmoid(uv)
                du[j, pl.ds(pl.multiple_of(c * SPAN + HALO, HALO), SPAN), lanes] = dx * sig * (
                    1.0 + uv * (1.0 - sig)
                )
            return total

        qs[at, :] = lax.fori_loop(0, shares, share, jnp.zeros((SPAN, LANES), F32))
        return 0

    lax.fori_loop(0, blocks, states_part, 0)
    parts = [(0, HALO)] + [(HALO + c * SPAN, SPAN) for c in range(blocks)]

    def values(j, _):
        for p in range(pages):
            lanes = slice(p * LANES, (p + 1) * LANES)
            near = pl.ds(pl.multiple_of(j * cols + p * LANES, LANES), LANES)
            sums = [jnp.zeros((8, LANES), F32) for _ in range(TAPS)]
            for start, size in parts:
                old = vext[j, pl.ds(start, size), lanes].astype(F32)
                dv = None
                for m in range(TAPS):
                    shifted = du[j, pl.ds(start + TAPS - 1 - m, size), lanes]
                    term = vk[m : m + 1, near] * shifted
                    dv = term if dv is None else dv + term
                    sums[m] = sums[m] + fold(old * shifted)
                dp[j, pl.ds(start, size), lanes] = dv.astype(BF16)
            for m in range(TAPS):
                row = jnp.sum(sums[m], axis=0, keepdims=True)
                small[pl.ds(m * shares * pages + j * pages + p, 1), :] = row
            row = jnp.sum(rowsum[j, 0, :, lanes], axis=0, keepdims=True)
            small[pl.ds(cfg["gain_row"] + j * pages + p, 1), :] = row
        return 0

    lax.fori_loop(0, shares, values, 0)

    lane = iota((SPAN, LANES), 1)
    is_fwd = lane % (2 * own) < own
    at0, at1 = iota((SPAN, SPAN), 0), iota((SPAN, SPAN), 1)
    both = jnp.concatenate([(at0 > at1).astype(F32), (at0 < at1).astype(F32)], axis=0).astype(BF16)
    dbias = jnp.zeros((1, LANES), F32)
    ddecay = jnp.zeros((1, LANES), F32)
    steps = []
    for c in range(blocks):
        at = chunk_rows(c)
        qv = qs[at, :]
        sums = mm_right(both, qv, 2)
        total = da[at, :] + xs[c : c + 1, :] + jnp.where(is_fwd, sums[:SPAN], sums[SPAN:])
        through = total * dec[0, at, :]
        step = (dk[at, :] + qv + through) * dec[1, at, :]
        step = jnp.where(lane < 2 * own * shares, step, 0.0)
        steps.append(step)
        dbias = dbias + jnp.sum(step, axis=0, keepdims=True)
        ddecay = ddecay + jnp.sum(through, axis=0, keepdims=True)
    base = cfg["rest_row"]
    small[base : base + 1, :] = dbias
    small[base + 1 : base + 2, :] = ddecay
    skips = jnp.zeros((8, LANES), F32)
    for j in range(shares):
        skips = skips + mm_left(rowsum[j, 1], spread[2 * j], 2, NT)
    small[base + 2 : base + 3, :] = jnp.sum(skips, axis=0, keepdims=True)
    small[base + 3 : base + 8, :] = jnp.zeros((5, LANES), F32)

    for k in range(4):
        for c in range(blocks):
            at = chunk_rows(c)
            uv = su[k, at, :]
            sig = sigmoid(uv)
            dsu[k, chunk_rows(c, HALO), :] = dst[k, at, :] * sig * (1.0 + uv * (1.0 - sig))
        sums = [jnp.zeros((8, LANES), F32) for _ in range(TAPS)]
        for start, size in parts:
            old = side[k, pl.ds(start, size), :]
            dv = None
            for m in range(TAPS):
                shifted = dsu[k, pl.ds(start + TAPS - 1 - m, size), :]
                term = sk[k, m : m + 1, :] * shifted
                dv = term if dv is None else dv + term
                sums[m] = sums[m] + fold(old * shifted)
            if start >= HALO:
                moved = pltpu.roll(steps[(start - HALO) // SPAN], (ns - 2 * own * k) % LANES, 1)
                dv = dv + jnp.where((lane >= ns) & (lane < ns + 2 * own), moved, 0.0)
            dp[k, pl.ds(start, size), pl.ds(cols, LANES)] = dv.astype(BF16)
        for m in range(TAPS):
            row = cfg["state_row"] + m * 4 + k
            small[row : row + 1, :] = jnp.sum(sums[m], axis=0, keepdims=True)
    small[cfg["input_row"] :, :] = jnp.zeros_like(small[cfg["input_row"] :, :])


def last_kernel(cfg, *refs):
    ids, halo, inputs, normed, dp, w1, gx, small_in = refs[:8]
    gn, small = refs[8:10]
    pieces, held = refs[10:-1], refs[-1]
    shares, rows, width = cfg["shares"], cfg["rows"], inputs.shape[1]

    def project(d, _):
        j = (ids[0] + shares - d) % shares
        held[...] = mm(normed[...], dp[j], TN).astype(BF16)
        take_grads(ids, pieces, held, d, cfg["per"])
        back = mm(dp[j], w1[j], NT)

        @pl.when(d == 0)
        def _():
            gn[...] = back
            gn[HALO:, :] += gx[...]

        @pl.when(d > 0)
        def _():
            gn[...] += back

        return 0

    lax.fori_loop(0, shares, project, 0)

    def plain(block):
        wide = block.astype(F32)
        return wide * lax.rsqrt(jnp.mean(wide * wide, axis=1, keepdims=True) + EPSILON)

    total = gn[0:8, :] * plain(halo[...])[0:8, :] + gn[8:16, :] * plain(halo[...])[8:16, :]
    for c in range(rows // SPAN):
        total = total + fold(gn[chunk_rows(c, HALO), :] * plain(inputs[chunk_rows(c), :]))
    total = jnp.sum(total, axis=0, keepdims=True)
    small[...] = small_in[...]
    for b in range(width // LANES):
        row = cfg["input_row"] + b
        small[row : row + 1, :] = total[:, b * LANES : (b + 1) * LANES]


def finish_kernel(cfg, ids, inputs, cot, gain, gn, edge, out):
    rows = cfg["rows"]
    size = SPAN // 2
    for c in range(rows // size):
        at = pl.ds(c * size, size)
        wide = inputs[at, :].astype(F32)
        g = gn[pl.ds(HALO + c * size, size), :]
        if c == rows // size - 1:
            g = jnp.concatenate([g[: size - HALO], g[size - HALO :] + edge[...]], axis=0)
        scale = lax.rsqrt(jnp.mean(wide * wide, axis=1, keepdims=True) + EPSILON)
        f = g * gain[...]
        mean = jnp.mean(f * wide, axis=1, keepdims=True)
        grad = cot[at, :].astype(F32) + scale * f - wide * (scale * scale * scale) * mean
        out[at, :] = grad.astype(BF16)


def gather_line(pack, shares):
    return jnp.stack([pack] + [along(pack, d, shares) for d in range(1, shares)])


def gather_layer(held, groups):
    return [held] + [lax.ppermute(held, "dp", xor(groups, 2 * k)) for k in range(1, groups // 2)]


def gather_pair(near, groups):
    pieces = []
    for block in near:
        pieces += [block, lax.ppermute(block, "dp", xor(groups, 1))]
    return pieces


def gather_any(pack):
    rows = lax.all_gather(pack, "dp", axis=0, tiled=True)
    return [lax.all_gather(rows, "tensor", axis=0, tiled=False)]


def scatter_any(pieces):
    part = lax.psum_scatter(pieces[0].astype(F32), "dp", scatter_dimension=1, tiled=True)
    return lax.psum_scatter(part, "tensor", scatter_dimension=0, tiled=False)


def scatter_pair(cfg, ids, keep, send):
    groups, shares, per, c = cfg["groups"], cfg["shares"], cfg["per"], keep.shape[-1]
    other = lax.ppermute(send, "dp", xor(groups, 1))
    shapes = tuple(sds((shares, per, c), BF16) for _ in range(groups // 2))
    return call(pair_kernel, shapes, us=1.5)(ids, keep, other)


def scatter_layer(cfg, ids, pairs, first):
    groups, shares, per, cols = (cfg[k] for k in ("groups", "shares", "per", "cols"))
    parts = [pairs[0]] + [lax.ppermute(pairs[k], "dp", xor(groups, 2 * k)) for k in range(1, groups // 2)]
    shapes = tuple(sds((per, 2 * cols), BF16) for _ in range(shares))
    return call(functools.partial(quad_kernel, cfg, first), shapes, us=1.5)(ids, *parts)


def scatter_line(cfg, blocks):
    shares = cfg["shares"]
    return [blocks[0]] + [along(blocks[d], shares - d, shares) for d in range(1, shares)]


def shards(
    inputs, gate_weight, value_weight, step_weight, shared_weight, output_weight, value_kernel,
    shared_kernel, step_bias, decay_log, skip_gain, input_gain, output_gain, cotangent,
):
    shares, groups = lax.axis_size("tensor"), lax.axis_size("dp")
    z, g = lax.axis_index("tensor"), lax.axis_index("dp")
    rows, width = inputs.shape
    per, cols = gate_weight.shape
    own = step_weight.shape[2]
    heads = own * shares
    ns = shared_weight.shape[1] // 4
    inner = cols * shares
    blocks, pages = rows // SPAN, cols // LANES
    fast = groups == 8 and per % 32 == 0
    cfg = dict(
        shares=shares, groups=groups, own=own, head=cols // own, cols=cols, rows=rows, state=ns, per=per,
        pieces=groups if fast else 1,
    )
    cfg["gain_row"] = TAPS * shares * pages
    cfg["state_row"] = cfg["gain_row"] + shares * pages
    cfg["rest_row"] = cfg["state_row"] + 4 * TAPS
    cfg["input_row"] = cfg["rest_row"] + 8
    small_rows = -(-(cfg["input_row"] + width // LANES) // 8) * 8
    ids = jnp.stack([z, g]).astype(jnp.int32)
    ext = HALO + rows
    pk = cols + LANES

    halo = lax.ppermute(inputs[rows - HALO :], "tensor", [(i, i + 1) for i in range(shares - 1)])
    shared_own = lax.dynamic_slice_in_dim(shared_weight, z * ns, ns, 1)
    flat_step = step_weight.reshape(per, 2 * own)
    blank = jnp.zeros((per, LANES - ns - 2 * own), BF16)
    pack1 = jnp.concatenate([value_weight, shared_own, flat_step, blank], axis=1)
    pack2 = jnp.concatenate([gate_weight, output_weight.T], axis=1)

    def by_lane(v):
        v = v.reshape(-1, 2, shares, own).transpose(0, 2, 1, 3).reshape(-1, 2 * heads)
        return jnp.pad(v, ((0, 8 - v.shape[0]), (0, LANES - 2 * heads)))

    params = by_lane(
        jnp.stack([step_bias, jnp.broadcast_to(decay_log, (2, heads)), jnp.broadcast_to(skip_gain, (2, heads))])
    )
    sk = jnp.pad(
        shared_kernel.reshape(TAPS, 4, ns).transpose(1, 0, 2), ((0, 0), (0, 8 - TAPS), (0, LANES - ns))
    )
    ogain = output_gain.reshape(shares, 1, cols)
    gain = input_gain.reshape(1, width)

    if fast:
        line1 = gather_line(pack1, shares)
        line2 = gather_line(after(pack2, line1), shares)
        near1 = gather_layer(line1, groups)
        near1, params, sk, ogain, gain, ids = lax.optimization_barrier((near1, params, sk, ogain, gain, ids))
        parts1 = gather_pair(near1, groups)
        near2 = gather_layer(after(line2, *near1), groups)
        parts2 = gather_pair(near2, groups)
    else:
        parts1, parts2 = gather_any(pack1), gather_any(pack2)

    pay_shape = sds((shares * ns + HALO, cols), BF16)
    (
        w1, normed, vext, u, x, side, su, bc, bct, c2, rho2, c2t, rho2t, dec, states, tots, spread,
        pay1, pay2, pay3,
    ) = call(
        functools.partial(front_kernel, cfg),
        (
            sds((shares, width, pk), BF16),
            sds((ext, width), BF16),
            sds((shares, ext, cols), BF16),
            sds((shares, rows, cols), BF16),
            sds((shares, rows, cols), BF16),
            sds((shares, ext, LANES)),
            sds((4, rows, LANES)),
            sds((4, rows, LANES), BF16),
            sds((4, blocks, LANES, SPAN), BF16),
            sds((rows, LANES)),
            sds((rows, LANES)),
            sds((blocks, LANES, SPAN)),
            sds((blocks, LANES, SPAN)),
            sds((4, rows, LANES)),
            sds((shares, 2, blocks, ns, cols)),
            sds((2 * blocks, LANES)),
            sds((2 * shares, LANES, cols), BF16),
            pay_shape, pay_shape, pay_shape,
        ),
        scratch=[pltpu.VMEM((ext, pk), F32)],
        us=14.0,
    )(ids, halo, inputs, gain, value_kernel, sk, params, *parts1)
    r1, r2, r3 = along(pay1, 1, shares), along(pay2, 2, shares), along(pay3, 3, shares)

    yin = call(functools.partial(within_kernel, cfg), sds((shares, rows, cols)), us=5.0)(
        ids, bc, c2, rho2t, x
    )
    w2, gate, gn_out = call(
        functools.partial(gate_kernel, cfg),
        (sds((shares, width, 2 * cols), BF16), sds((shares, rows, cols)), sds((shares, rows, cols))),
        us=6.0,
    )(ids, normed, cotangent, *parts2)

    enter, dy, normal, dgate, edy, rr, dlocal, rowsum, keeps, q1, q2, q3 = call(
        functools.partial(middle_kernel, cfg),
        (
            sds((shares, 2, blocks, ns, cols), BF16),
            sds((shares, rows, cols), BF16),
            sds((shares, rows, cols), BF16),
            sds((shares, rows, cols), BF16),
            sds((shares, 2, rows, cols), BF16),
            sds((rows, LANES)),
            sds((shares, 2, blocks, ns, cols)),
            sds((shares, 2, 8, cols)),
            sds((shares, 3, HALO, cols)),
            pay_shape, pay_shape, pay_shape,
        ),
        scratch=[pltpu.VMEM((shares, SPAN, cols), F32)] * 2 + [pltpu.VMEM((shares, SPAN, cols), BF16)] * 2,
        us=16.0,
    )(ids, yin, x, gate, gn_out, states, bc, bct, dec, tots, spread, params, ogain, r1, r2, r3)
    s1, s2, s3 = along(q1, 1, shares), along(q2, 2, shares), along(q3, 3, shares)

    def piece_shapes(c):
        if fast:
            return (sds((groups // 2, shares, per, c), BF16),) * 2
        return (sds((shares, width, c), BF16),)

    mixed, gx, *grads2 = call(
        functools.partial(output_kernel, cfg),
        (sds((rows, width), BF16), sds((rows, width))) + piece_shapes(2 * cols),
        scratch=[pltpu.VMEM((rows, width), F32), pltpu.VMEM((width, 2 * cols), BF16)],
        us=10.0,
    )(ids, inputs, cotangent, normed, normal, dgate, w2)
    dy_late = dy
    if fast:
        pairs2 = scatter_pair(cfg, ids, *grads2)
        dy_late = after(dy, pairs2)

    dxi, dbc, da, dk = call(
        functools.partial(back_within_kernel, cfg),
        (sds((shares, rows, cols)), sds((4, rows, LANES)), sds((rows, LANES)), sds((rows, LANES))),
        scratch=[pltpu.VMEM((LANES, SPAN), F32), pltpu.VMEM((LANES, SPAN), F32)],
        us=9.0,
    )(ids, bc, bct, rho2, c2t, x, dy_late, edy, enter, rr, keeps)
    if fast:
        blocks2 = scatter_layer(cfg, ids, pairs2, False)

    dp, small = call(
        functools.partial(tail_kernel, cfg),
        (sds((shares, ext, pk), BF16), sds((small_rows, LANES))),
        scratch=[
            pltpu.VMEM((shares, ext + HALO, cols), F32),
            pltpu.VMEM((4, ext + HALO, LANES), F32),
            pltpu.VMEM((4, rows, LANES), F32),
            pltpu.VMEM((shares, 2, blocks, ns, cols), BF16),
            pltpu.VMEM((8, LANES), F32),
            pltpu.VMEM((rows, LANES), F32),
            pltpu.VMEM((8, LANES), F32),
        ],
        us=16.0,
    )(
        ids, x, u, dxi, vext, side, su, bc, dbc, dec, enter, da, dk, dlocal, rowsum, keeps, spread,
        s1, s2, s3, value_kernel, sk,
    )
    gn, small, *grads1 = call(
        functools.partial(last_kernel, cfg),
        (sds((ext, width)), sds((small_rows, LANES))) + piece_shapes(pk),
        scratch=[pltpu.VMEM((width, pk), BF16)],
        us=7.0,
    )(ids, halo, inputs, normed, dp, w1, gx, small)
    edge = lax.ppermute(gn[:HALO], "tensor", [(i + 1, i) for i in range(shares - 1)])

    if fast:
        pairs1 = scatter_pair(cfg, ids, *grads1)
        blocks1 = scatter_layer(cfg, ids, pairs1, True)
        line2 = scatter_line(cfg, blocks2)
        grad_gate, grad_output = call(
            functools.partial(line2_kernel, cfg), (sds((per, cols)), sds((per, cols))), us=1.0
        )(ids, *line2)
        line1 = scatter_line(cfg, blocks1)
        grad_value, grad_step, grad_shared = call(
            functools.partial(line_kernel, cfg),
            (sds((per, cols)), sds((per, 2 * own)), sds((per, shares * ns))),
            scratch=[pltpu.VMEM((shares, per, shares * ns), F32)],
            us=1.0,
        )(ids, *line1)

        small = small + lax.ppermute(small, "dp", xor(groups, 1))
        four = [small] + [lax.ppermute(small, "dp", xor(groups, 2 * k)) for k in range(1, groups // 2)]

        def add(parts, places):
            return call(
                sum_kernel,
                sds((small_rows, LANES)),
                scratch=[pltpu.VMEM((len(parts), small_rows, LANES), F32)],
                us=1.0,
            )(jnp.stack(places).astype(jnp.int32), *parts)

        small = add(four, [m ^ (g // 2) for m in range(groups // 2)])
        line = [small] + [along(small, d, shares) for d in range(1, shares)]
        small = add(line, [(z + shares - m) % shares for m in range(shares)])
    else:
        out1, out2 = scatter_any(grads1), scatter_any(grads2)
        grad_gate, grad_output = out2[:, :cols], out2[:, cols:]
        grad_value, grad_step = out1[:, :cols], out1[:, cols + ns : cols + ns + 2 * own]
        grad_shared = lax.all_gather(out1[:, cols : cols + ns], "tensor", axis=1, tiled=True)
        small = lax.psum(small, ("dp", "tensor"))

    grad_input = call(functools.partial(finish_kernel, cfg), sds((rows, width), BF16), us=2.0)(
        ids, inputs, cotangent, gain, gn, edge
    )

    def from_lane(v):
        return v[: 2 * heads].reshape(shares, 2, own).transpose(1, 0, 2).reshape(2, heads)

    rest = cfg["rest_row"]
    return (
        mixed,
        grad_input,
        grad_gate,
        grad_value,
        grad_step.reshape(per, 2, own),
        grad_shared,
        grad_output.T,
        small[: cfg["gain_row"]].reshape(TAPS, inner),
        small[cfg["state_row"] : rest].reshape(TAPS, 4, LANES)[:, :, :ns].reshape(TAPS, 4 * ns),
        from_lane(small[rest]),
        from_lane(small[rest + 1]).sum(axis=0),
        from_lane(small[rest + 2])[0],
        small[cfg["input_row"] : cfg["input_row"] + width // LANES].reshape(width),
        small[cfg["gain_row"] : cfg["state_row"]].reshape(inner),
    )


def solution(mesh):
    both = P(("dp", "tensor"), None)
    placed = (
        both, P("dp", "tensor"), P("dp", "tensor"), P("dp", None, "tensor"), P("dp", None),
        P("tensor", "dp"), P(), P(), P(), P(), P(), P(), P(), both,
    )
    return jax.shard_map(
        shards,
        mesh=mesh,
        in_specs=placed,
        out_specs=(
            both, both, P("dp", "tensor"), P("dp", "tensor"), P("dp", None, "tensor"), P("dp", None),
            P("tensor", "dp"), P(), P(), P(), P(), P(), P(), P(),
        ),
        check_vma=False,
    )
```

```python
import functools

import jax
import jax.numpy as jnp
from jax import lax
from jax.experimental import pallas as pl
from jax.experimental.pallas import tpu as pltpu
from jax.sharding import PartitionSpec as P

F32 = jnp.float32
BF16 = jnp.bfloat16
EPSILON = 1e-06
SPAN = 128
HALO = 16
TAPS = 4
LANES = 128
LOG2E = 1.4426950408889634
EXACT = lax.Precision.HIGHEST
LIMIT = 14 * 1024 * 1024

NN = (((1,), (0,)), ((), ()))
NT = (((1,), (1,)), ((), ()))
TN = (((0,), (0,)), ((), ()))


def mm(a, b, dims=NN, precision=None):
    return lax.dot_general(a, b, dims, preferred_element_type=F32, precision=precision)


def iota(shape, dim):
    return lax.broadcasted_iota(jnp.int32, shape, dim)


def sigmoid(v):
    return 0.5 * jnp.tanh(0.5 * v) + 0.5


def split(v, n):
    parts = []
    for _ in range(n):
        part = v.astype(BF16)
        parts.append(part)
        v = v - part.astype(F32)
    return parts


def mm_right(ones, v, n):
    total = None
    for part in split(v, n):
        term = mm(ones, part)
        total = term if total is None else total + term
    return total


def mm_left(v, ones, n, dims=(((1,), (0,)), ((), ()))):
    total = None
    for part in split(v, n):
        term = mm(part, ones, dims)
        total = term if total is None else total + term
    return total


def fold(v):
    return v.reshape(v.shape[0] // 8, 8, v.shape[1]).sum(axis=0)


def chunk_rows(c, base=0):
    return pl.ds(base + c * SPAN, SPAN)


def call(kernel, out_shape, scratch=(), us=1.0, limit=LIMIT):
    def run(*args):
        specs = [
            pl.BlockSpec(memory_space=pltpu.SMEM if i == 0 else pltpu.VMEM)
            for i in range(len(args))
        ]
        return pl.pallas_call(
            kernel,
            out_shape=out_shape,
            in_specs=specs,
            out_specs=jax.tree.map(lambda _: pl.BlockSpec(memory_space=pltpu.VMEM), out_shape),
            scratch_shapes=list(scratch),
            cost_estimate=pl.CostEstimate(
                flops=int(us * 1.1e9), bytes_accessed=int(us * 3.0e6), transcendentals=0
            ),
            compiler_params=pltpu.CompilerParams(vmem_limit_bytes=limit),
        )(*args)

    return run


def sds(shape, dtype=F32):
    return jax.ShapeDtypeStruct(shape, dtype)


def put_weights(ids, pieces, full, shares, per):
    if len(pieces) == 1:
        full[...] = pieces[0][...]
        return
    for rel, piece in enumerate(pieces):
        row = pl.multiple_of((ids[1] ^ rel) * per, per)
        for d in range(shares):
            j = (ids[0] + shares - d) % shares
            full[j, pl.ds(row, per), :] = piece[d]


def take_grads(ids, pieces, held, d, per):
    if len(pieces) == 1:
        shares = pieces[0].shape[0]
        pieces[0][(ids[0] + shares - d) % shares] = held[...]
        return
    for rel in range(2 * pieces[0].shape[0]):
        row = pl.multiple_of((ids[1] ^ rel) * per, per)
        pieces[rel % 2][rel // 2, d] = held[pl.ds(row, per), :]


def cyclic(size, d):
    return [(i, (i + d) % size) for i in range(size)]


def xor(size, bit):
    return [(i, i ^ bit) for i in range(size)]


def along(v, d, shares):
    return lax.ppermute(v, "tensor", cyclic(shares, d))


def spread_out(parts, shares):
    return [along(part, d + 1, shares) for d, part in enumerate(parts)]


def after(values, *others):
    out = lax.optimization_barrier((values,) + others)
    return out[0]


def sum_kernel(ids, *refs):
    parts, out, held = refs[:-2], refs[-2], refs[-1]
    for k, part in enumerate(parts):
        held[k] = part[...]
    total = held[ids[0]]
    for m in range(1, len(parts)):
        total = total + held[ids[m]]
    out[...] = total


def pair_kernel(ids, keep, other, *outs):
    for k, out in enumerate(outs):
        out[...] = (keep[k].astype(F32) + other[k].astype(F32)).astype(BF16)


def quad_kernel(cfg, first, ids, *refs):
    n, shares, cols, ns = cfg["groups"] // 2, cfg["shares"], cfg["cols"], cfg["state"]
    parts, outs, held = refs[:n], refs[n:-1], refs[-1]
    for d in range(shares):
        q = (ids[0] + shares - d) % shares
        total = parts[0][d].astype(F32)
        for part in parts[1:]:
            total = total + part[d].astype(F32)
        if first:
            outs[d][:, :cols] = total[:, :cols].astype(BF16)
            held[q] = total[:, cols:]
        else:
            outs[d][...] = total.astype(BF16)
    if first:
        low = iota((outs[0].shape[0], LANES), 1) < ns
        for k in range(shares // 2):
            both = jnp.where(low, held[2 * k], pltpu.roll(held[2 * k + 1], ns, 1)).astype(BF16)
            for out in outs:
                out[:, cols + k * LANES : cols + (k + 1) * LANES] = both
        for d, out in enumerate(outs):
            step = held[(ids[0] + shares - d) % shares]
            out[:, cols + shares * ns :] = jnp.where(low, pltpu.roll(step, LANES - ns, 1), 0.0).astype(BF16)


def line_kernel(cfg, ids, *refs):
    shares, cols, ns = cfg["shares"], cfg["cols"], cfg["state"]
    parts, (value, step, shared, held) = refs[:shares], refs[shares:]
    for e, part in enumerate(parts):
        held[e] = part[...].astype(F32)
    total = held[(shares - ids[0]) % shares]
    for q in range(1, shares):
        total = total + held[(q + shares - ids[0]) % shares]
    value[...] = total[:, :cols]
    shared[...] = total[:, cols : cols + shares * ns]
    step[...] = total[:, cols + shares * ns :][:, : step.shape[1]]


def line2_kernel(cfg, ids, *refs):
    shares, cols = cfg["shares"], cfg["cols"]
    parts, (gate, out) = refs[:shares], refs[shares:]
    total = parts[0][...].astype(F32)
    for part in parts[1:]:
        total = total + part[...].astype(F32)
    gate[...] = total[:, :cols]
    out[...] = total[:, cols:]


def fill_spread(cfg, spread):
    own, head, cols = cfg["own"], cfg["head"], cfg["cols"]
    lane = iota((LANES, cols), 0)
    place = iota((LANES, cols), 1) // head
    for k in range(2 * cfg["shares"]):
        spread[k] = (lane == own * k + place).astype(F32).astype(BF16)


def front_kernel(cfg, *refs):
    n = cfg["pieces"]
    ids, halo, inputs, gain, vk, sk, params = refs[:7]
    pieces = refs[7 : 7 + n]
    (
        w1, normed, vext, u_out, x_out, side, su_out, bc_out, bct, c2, rho2, c2t, rho2t, dec, states, tots,
        spread, pay1, pay2, pay3, acc,
    ) = refs[7 + n :]
    shares, own, cols, rows, ns = (cfg[k] for k in ("shares", "own", "cols", "rows", "state"))
    blocks = rows // SPAN
    put_weights(ids, pieces, w1, shares, cfg["per"])
    fill_spread(cfg, spread)

    def norm(block):
        wide = block.astype(F32)
        scale = lax.rsqrt(jnp.mean(wide * wide, axis=1, keepdims=True) + EPSILON)
        return (wide * scale * gain[...]).astype(BF16)

    normed[0:HALO, :] = jnp.where(ids[0] > 0, norm(halo[...]).astype(F32), 0.0).astype(BF16)
    for c in range(2 * blocks):
        size = SPAN // 2
        normed[pl.ds(HALO + c * size, size), :] = norm(inputs[pl.ds(c * size, size), :])

    def project(j, _):
        acc[...] = mm(normed[...], w1[j])
        side[j] = acc[:, cols : cols + LANES]
        for c in range(blocks):
            vext[j, chunk_rows(c), :] = acc[chunk_rows(c), :cols].astype(BF16)
        vext[j, blocks * SPAN :, :] = acc[blocks * SPAN :, :cols].astype(BF16)
        for c in range(blocks):
            for p in range(cols // LANES + 1):
                lanes = pl.ds(p * LANES, LANES)
                u = None
                for m in range(TAPS):
                    if p < cols // LANES:
                        tap = vk[m : m + 1, pl.ds(pl.multiple_of(j * cols + p * LANES, LANES), LANES)]
                    else:
                        tap = sk[j, m : m + 1, :]
                    term = tap * acc[chunk_rows(c, HALO - TAPS + 1 + m), lanes]
                    u = term if u is None else u + term
                v = u * sigmoid(u)
                if p < cols // LANES:
                    u_out[j, chunk_rows(c), lanes] = u.astype(BF16)
                    x_out[j, chunk_rows(c), lanes] = v.astype(BF16)
                else:
                    su_out[j, chunk_rows(c), :] = u
                    bc_out[j, chunk_rows(c), :] = v.astype(BF16)
                    bct[j, c] = v.T.astype(BF16)
        return 0

    lax.fori_loop(0, shares, project, 0)

    lane = iota((SPAN, LANES), 1)
    is_fwd = lane % (2 * own) < own
    at0, at1 = iota((SPAN, SPAN), 0), iota((SPAN, SPAN), 1)
    both = jnp.concatenate([(at0 >= at1).astype(F32), (at0 <= at1).astype(F32)], axis=0).astype(BF16)
    rate = jnp.where(iota((1, LANES), 1) < 2 * own * shares, -jnp.exp(params[1:2, :]), 0.0)
    for c in range(blocks):
        raw = jnp.zeros((SPAN, LANES), F32)
        for j in range(shares):
            moved = pltpu.roll(side[j, chunk_rows(c, HALO), :], (2 * own * j - ns) % LANES, 1)
            raw = jnp.where((lane >= 2 * own * j) & (lane < 2 * own * (j + 1)), moved, raw)
        v = raw + params[0:1, :]
        small = jnp.exp(jnp.minimum(v, 0.0))
        dt = jnp.where(v < -15.0, small, jnp.maximum(v, 0.0) + jnp.log1p(jnp.exp(-jnp.abs(v))))
        log_dt = jnp.where(v < -15.0, v, jnp.log(jnp.maximum(dt, 1e-30)))
        ratio = jnp.where(v < -15.0, 1.0, sigmoid(v) / jnp.maximum(dt, 1e-30))
        a = dt * rate
        sums = mm_right(both, a, 3)
        cum = jnp.where(is_fwd, sums[:SPAN], sums[SPAN:])
        tot = jnp.sum(a, axis=0, keepdims=True)
        rho = cum - log_dt
        cc = cum * LOG2E
        rr = rho * LOG2E
        c2[chunk_rows(c), :] = cc
        rho2[chunk_rows(c), :] = rr
        c2t[c] = cc.T
        rho2t[c] = rr.T
        dec[0, chunk_rows(c), :] = a
        dec[1, chunk_rows(c), :] = ratio
        dec[2, chunk_rows(c), :] = jnp.exp(tot - rho)
        dec[3, chunk_rows(c), :] = jnp.exp(cum)
        tots[c : c + 1, :] = tot
    fwd1 = iota((1, LANES), 1) % (2 * own) < own
    zero = jnp.zeros((1, LANES), F32)
    lead = []
    for c in range(blocks):
        later, sooner = zero, zero
        for k in range(blocks):
            if k > c:
                later = later + tots[k : k + 1, :]
            if k < c:
                sooner = sooner + tots[k : k + 1, :]
        lead.append(jnp.exp(jnp.where(fwd1, later, sooner)))
        tots[blocks + c : blocks + c + 1, :] = jnp.where(fwd1, sooner, later)
    lead = jnp.concatenate(lead + [zero] * (8 - blocks), axis=0)
    whole = tots[0:1, :]
    for c in range(1, blocks):
        whole = whole + tots[c : c + 1, :]
    extra = jnp.concatenate([p.astype(F32) for p in split(whole, 3)] + [zero] * (HALO - 3), axis=0)
    extra = jnp.concatenate([extra, jnp.zeros((HALO, cols - LANES), F32)], axis=1).astype(BF16)
    for pay in (pay1, pay2, pay3):
        pay[shares * ns :, :] = extra

    def sums(j, _):
        dev = []
        for d in range(2):
            grow = spread[2 * j + d]
            wide = mm_left(lead, grow, 2)
            total = jnp.zeros((ns, cols), F32)
            for c in range(blocks):
                weight = mm(dec[2, chunk_rows(c), :].astype(BF16), grow)
                xw = (weight * x_out[j, chunk_rows(c), :].astype(F32)).astype(BF16)
                s = mm(bct[2 * d, c, :ns, :], xw)
                states[j, d, c] = s.astype(BF16)
                total = total + wide[c : c + 1, :] * s
            dev.append(total)
        at = pl.ds(pl.multiple_of(j * ns, ns), ns)
        for dist, pay in ((1, pay1), (2, pay2), (3, pay3)):
            pay[at, :] = jnp.where(ids[0] + dist < shares, dev[0], dev[1]).astype(BF16)
        return 0

    lax.fori_loop(0, shares, sums, 0, unroll=True)


def stack_pair(first, v):
    zero = jnp.zeros_like(v)
    return jnp.concatenate([jnp.where(first, v, zero), jnp.where(first, zero, v)], axis=0)


def within_kernel(cfg, ids, bc, c2, rho2t, x, y):
    shares, own, rows = (cfg[k] for k in ("shares", "own", "rows"))
    t, s = iota((SPAN, SPAN), 0), iota((SPAN, SPAN), 1)
    low = t > s
    first = iota((SPAN, LANES), 1) < cfg["head"]

    def block(c, _):
        at = pl.ds(pl.multiple_of(c * SPAN, SPAN), SPAN)
        g = jnp.where(low, mm(bc[1, at, :], bc[0, at, :], NT), mm(bc[3, at, :], bc[2, at, :], NT))
        g = jnp.where(t == s, 0.0, g)
        cc = c2[at, :]
        for j in range(shares):
            for p in range(own // 2):
                mats = []
                for i in (2 * p, 2 * p + 1):
                    f, b = 2 * own * j + i, 2 * own * j + own + i
                    col = jnp.where(low, cc[:, f : f + 1], cc[:, b : b + 1])
                    row = jnp.where(low, rho2t[c, f : f + 1, :], rho2t[c, b : b + 1, :])
                    mats.append((jnp.exp2(col - row) * g).astype(BF16))
                lanes = slice(p * LANES, (p + 1) * LANES)
                y[j, at, lanes] = mm(jnp.concatenate(mats, axis=1), stack_pair(first, x[j, at, lanes])).astype(BF16)
        return 0

    lax.fori_loop(0, rows // SPAN, block, 0)


def gate_kernel(cfg, *refs):
    n = cfg["pieces"]
    ids, normed, cot = refs[:3]
    pieces = refs[3 : 3 + n]
    w2, gate, gn = refs[3 + n :]
    shares, cols, rows = (cfg[k] for k in ("shares", "cols", "rows"))
    put_weights(ids, pieces, w2, shares, cfg["per"])

    def project(j, _):
        gate[j] = mm(normed[HALO : HALO + rows, :], w2[j, :, :cols]).astype(BF16)
        gn[j] = mm(cot[...], w2[j, :, cols:]).astype(BF16)
        return 0

    lax.fori_loop(0, shares, project, 0, unroll=True)


def incoming(ids, cfg, got, j, near, far):
    z, shares, ns = ids[0], cfg["shares"], cfg["state"]
    at = pl.ds(pl.multiple_of(j * ns, ns), ns)
    r1, r2, r3 = (part[at, :].astype(F32) for part in got)

    def keep(test, v):
        return jnp.where(test, v, 0.0)

    before = keep(z >= 1, r1) + near[0] * keep(z >= 2, r2) + near[1] * keep(z >= 3, r3)
    behind = (
        keep(z <= shares - 2, r3)
        + far[0] * keep(z <= shares - 3, r2)
        + far[1] * keep(z <= shares - 4, r1)
    )
    return before, behind


def middle_kernel(cfg, *refs):
    (
        ids, yin, x, gate, gn, states, bc, bct, dec, tots, spread, params, ogain, r1, r2, r3,
        enter, dy, normal, dgate, rr, dlocal, rowsum, keeps, p1, p2, p3,
        ys, acts, ef, eb,
    ) = refs
    shares, own, cols, rows, ns = (cfg[k] for k in ("shares", "own", "cols", "rows", "state"))
    blocks, inner = rows // SPAN, cols * shares
    zero = jnp.zeros((1, LANES), F32)

    def whole(d):
        v = (r1, r2, r3)[d - 1][pl.ds(shares * ns, HALO), :LANES].astype(F32)
        return v[0:1, :] + v[1:2, :] + v[2:3, :]

    l1, l2, l3 = whole(1), whole(2), whole(3)
    lines = [tots[c : c + 1, :] for c in range(2 * blocks)] + [l1, l1 + l2, l3, l3 + l2]
    lines = jnp.exp(jnp.concatenate(lines + [zero] * (HALO - len(lines)), axis=0))
    skip_rows = jnp.concatenate([params[2:3, :]] + [zero] * 7, axis=0)

    def grow_lines(j, _):
        for d in range(2):
            keeps[j, d] = mm_left(lines, spread[2 * j + d], 2)
        keeps[j, 2, 0:8] = mm_left(skip_rows, spread[2 * j], 2)
        return 0

    lax.fori_loop(0, shares, grow_lines, 0, unroll=True)

    def enter_states(j, _):
        kf, kb = keeps[j, 0], keeps[j, 1]
        b = 2 * blocks
        e, e_b = incoming(
            ids, cfg, (r1, r2, r3), j,
            (kf[b : b + 1, :], kf[b + 1 : b + 2, :]), (kb[b + 2 : b + 3, :], kb[b + 3 : b + 4, :]),
        )
        for c in range(blocks):
            enter[j, 0, c] = e.astype(BF16)
            e = kf[c : c + 1, :] * e + states[j, 0, c].astype(F32)
        for c in reversed(range(blocks)):
            enter[j, 1, c] = e_b.astype(BF16)
            e_b = kb[c : c + 1, :] * e_b + states[j, 1, c].astype(F32)
        return 0

    lax.fori_loop(0, shares, enter_states, 0, unroll=True)
    rowsum[...] = jnp.zeros_like(rowsum)
    pages = cols // LANES

    def block(c, _):
        at = pl.ds(pl.multiple_of(c * SPAN, SPAN), SPAN)
        ec = dec[3, at, :].astype(BF16)

        def first(j, sums):
            square, dot = sums
            for p in range(pages):
                lanes = slice(p * LANES, (p + 1) * LANES)
                cf = mm(bc[1, at, :ns], enter[j, 0, c, :, lanes]) * mm(ec, spread[2 * j, :, lanes])
                cb = mm(bc[3, at, :ns], enter[j, 1, c, :, lanes]) * mm(ec, spread[2 * j + 1, :, lanes])
                ef[j, :, lanes] = cf.astype(BF16)
                eb[j, :, lanes] = cb.astype(BF16)
                v = yin[j, at, lanes].astype(F32) + keeps[j, 2, 0:1, lanes] * x[j, at, lanes].astype(F32) + cf + cb
                ys[j, :, lanes] = v
                g = gate[j, at, lanes].astype(F32)
                act = g * sigmoid(g)
                acts[j, :, lanes] = act
                gated = v * act
                square = square + gated * gated
                dot = dot + gn[j, at, lanes].astype(F32) * ogain[j, :, lanes] * gated
            return square, dot

        blank = jnp.zeros((SPAN, LANES), F32)
        square, dot = lax.fori_loop(0, shares, first, (blank, blank), unroll=True)
        square = jnp.sum(square, axis=1, keepdims=True)
        dot = jnp.sum(dot, axis=1, keepdims=True)
        inv = lax.rsqrt(square / inner + EPSILON)
        back = inv * inv * inv * dot / inner

        def second(j, total):
            for p in range(pages):
                lanes = slice(p * LANES, (p + 1) * LANES)
                v, act, g = ys[j, :, lanes], acts[j, :, lanes], gate[j, at, lanes].astype(F32)
                gnv, og = gn[j, at, lanes].astype(F32), ogain[j, :, lanes]
                sig = sigmoid(g)
                gated = v * act
                scaled = gated * inv
                normal[j, at, lanes] = (scaled * og).astype(BF16)
                rowsum[j, 0, :, lanes] += fold(gnv * scaled)
                dgated = inv * (gnv * og) - gated * back
                d_scan = dgated * act
                low = d_scan.astype(BF16)
                dy[j, at, lanes] = low
                dgate[j, at, lanes] = (dgated * v * (sig + act * (1.0 - sig))).astype(BF16)
                rowsum[j, 1, :, lanes] += fold(d_scan * x[j, at, lanes].astype(F32))
                for d, kept in ((0, ef), (1, eb)):
                    product = (d_scan * kept[j, :, lanes].astype(F32)).astype(BF16)
                    total = total + mm(product, spread[2 * j + d, :, lanes], NT)
                    wide = (mm(ec, spread[2 * j + d, :, lanes]) * d_scan).astype(BF16)
                    dlocal[j, d, c, :, lanes] = mm(bct[1 + 2 * d, c, :ns, :], wide).astype(BF16)
            return total

        rr[at, :] = lax.fori_loop(0, shares, second, blank, unroll=True)
        return 0

    lax.fori_loop(0, blocks, block, 0)
    def leave(j, _):
        dev = []
        for d in range(2):
            total = jnp.zeros((ns, cols), F32)
            for c in range(blocks):
                total = total + keeps[j, d, blocks + c : blocks + c + 1, :] * dlocal[j, d, c].astype(F32)
            dev.append(total)
        at = pl.ds(pl.multiple_of(j * ns, ns), ns)
        for dist, pay in ((1, p1), (2, p2), (3, p3)):
            pay[at, :] = jnp.where(ids[0] + dist < shares, dev[1], dev[0]).astype(BF16)
        return 0

    lax.fori_loop(0, shares, leave, 0, unroll=True)


def output_kernel(cfg, *refs):
    ids, inputs, cot, normed, normal, dgate, w2 = refs[:7]
    mixed, gx = refs[7:9]
    pieces, (total, held) = refs[9:-2], refs[-2:]
    shares, cols, rows = (cfg[k] for k in ("shares", "cols", "rows"))

    def project(d, _):
        j = (ids[0] + shares - d) % shares
        held[:, :cols] = mm(normed[HALO : HALO + rows, :], dgate[j], TN).astype(BF16)
        held[:, cols:] = mm(cot[...], normal[j], TN).astype(BF16)
        take_grads(ids, pieces, held, d, cfg["per"])
        part = mm(normal[j], w2[j, :, cols:], NT)
        back = mm(dgate[j], w2[j, :, :cols], NT)

        @pl.when(d == 0)
        def _():
            total[...] = part
            gx[...] = back

        @pl.when(d > 0)
        def _():
            total[...] += part
            gx[...] += back

        return 0

    lax.fori_loop(0, shares, project, 0, unroll=True)
    mixed[...] = (total[...] + inputs[...].astype(F32)).astype(BF16)


def back_within_kernel(cfg, ids, bc, bct, rho2, c2t, x, dy, dec, spread, enter, rr, keeps, dx, dbc, da, dk, das, ras):
    shares, own, rows, ns = (cfg[k] for k in ("shares", "own", "rows", "state"))
    s, t = iota((SPAN, SPAN), 0), iota((SPAN, SPAN), 1)
    up = t > s
    first = iota((SPAN, LANES), 1) < cfg["head"]
    after_t = (s >= t).astype(F32).astype(BF16)
    until_t = (s <= t).astype(F32).astype(BF16)
    tri = jnp.concatenate([after_t, until_t], axis=1)
    sums = jnp.concatenate([until_t, after_t], axis=0)
    lane = iota((SPAN, LANES), 1)
    is_fwd = iota((LANES, SPAN), 0) % (2 * own) < own

    def block(c, _):
        at = pl.ds(pl.multiple_of(c * SPAN, SPAN), SPAN)
        g = jnp.where(up, mm(bc[0, at, :], bc[1, at, :], NT), mm(bc[2, at, :], bc[3, at, :], NT))
        g = jnp.where(t == s, 0.0, g)
        rho = rho2[at, :]
        dg = jnp.zeros((SPAN, SPAN), F32)
        das[...] = jnp.zeros_like(das)
        ras[...] = jnp.zeros_like(ras)
        for j in range(shares):
            for p in range(own // 2):
                lanes = slice(p * LANES, (p + 1) * LANES)
                dyp = dy[j, at, lanes]
                dm = mm(stack_pair(first, x[j, at, lanes]), dyp, NT)
                ws, zs = [], []
                for q in range(2):
                    i = 2 * p + q
                    f, b = 2 * own * j + i, 2 * own * j + own + i
                    row = jnp.where(up, c2t[c, f : f + 1, :], c2t[c, b : b + 1, :])
                    col = jnp.where(up, rho[:, f : f + 1], rho[:, b : b + 1])
                    pw = jnp.exp2(row - col)
                    ud = dm[q * SPAN : (q + 1) * SPAN] * pw
                    dg = dg + ud
                    ws.append((pw * g).astype(BF16))
                    zd = ud * g
                    zs.append(zd.astype(BF16))
                    rf = jnp.sum(jnp.where(up, zd, 0.0), axis=0, keepdims=True)
                    ras[f : f + 1, :] = rf
                    ras[b : b + 1, :] = jnp.sum(zd, axis=0, keepdims=True) - rf
                back = mm(jnp.concatenate(ws, axis=1), stack_pair(first, dyp))
                dx[j, at, lanes] = (back + keeps[j, 2, 0:1, lanes] * dyp.astype(F32)).astype(BF16)
                cross = mm(jnp.concatenate(zs, axis=0), tri)
                for q in range(2):
                    i = 2 * p + q
                    f, b = 2 * own * j + i, 2 * own * j + own + i
                    part = cross[q * SPAN : (q + 1) * SPAN]
                    das[f : f + 1, :] = jnp.sum(jnp.where(up, part[:, :SPAN], 0.0), axis=0, keepdims=True)
                    das[b : b + 1, :] = jnp.sum(
                        jnp.where(t < s, part[:, SPAN:], 0.0), axis=0, keepdims=True
                    )
        df = jnp.where(up, dg, 0.0)
        db = jnp.where(t < s, dg, 0.0)
        dcf = mm(df.T.astype(BF16), bc[0, at, :])
        dcb = mm(db.T.astype(BF16), bc[2, at, :])
        cf, cb = jnp.zeros((SPAN, ns), F32), jnp.zeros((SPAN, ns), F32)
        ec = dec[3, at, :].astype(BF16)
        for j in range(shares):
            dyj = dy[j, at, :].astype(F32)
            cf = cf + mm((mm(ec, spread[2 * j]) * dyj).astype(BF16), enter[j, 0, c], NT)
            cb = cb + mm((mm(ec, spread[2 * j + 1]) * dyj).astype(BF16), enter[j, 1, c], NT)
        dbc[0, at, :] = mm(df.astype(BF16), bc[1, at, :])
        dbc[1, at, :] = dcf
        dbc[1, at, :ns] += cf
        dbc[2, at, :] = mm(db.astype(BF16), bc[3, at, :])
        dbc[3, at, :] = dcb
        dbc[3, at, :ns] += cb
        a = das[...]
        later = jnp.where(lane < SPAN - 1, pltpu.roll(a, SPAN - 1, 1), 0.0)
        sooner = jnp.where(lane > 0, pltpu.roll(a, 1, 1), 0.0)
        kd = ras[...] - a + jnp.where(is_fwd, later, sooner)
        through = mm_right(sums, rr[at, :], 2)
        da[at, :] = a.T + jnp.where(lane % (2 * own) < own, through[:SPAN], through[SPAN:])
        dk[at, :] = kd.T
        return 0

    lax.fori_loop(0, rows // SPAN, block, 0)


def tail_kernel(cfg, *refs):
    (
        ids, x, u, dxi, vext, side, su, bc, dbc, dec, enter, da, dk, dlocal, rowsum, keeps, spread,
        r1, r2, r3, vk, sk,
        dp, small,
        du, dsu, dst, dstate, xs, qs, taps,
    ) = refs
    shares, own, cols, rows, ns = (cfg[k] for k in ("shares", "own", "cols", "rows", "state"))
    blocks, pages = rows // SPAN, cols // LANES

    xs[...] = jnp.zeros_like(xs)
    du[...] = jnp.zeros_like(du)
    dsu[...] = jnp.zeros_like(dsu)
    dst[...] = dbc[...]

    def chain(j, _):
        kf, kb = keeps[j, 0], keeps[j, 1]
        b = 2 * blocks
        now_b, now_f = incoming(
            ids, cfg, (r1, r2, r3), j,
            (kb[b : b + 1, :], kb[b + 1 : b + 2, :]), (kf[b + 2 : b + 3, :], kf[b + 3 : b + 4, :]),
        )
        for d, order, now, kept in (
            (0, list(reversed(range(blocks))), now_f, kf),
            (1, list(range(blocks)), now_b, kb),
        ):
            rows_x = [None] * blocks
            for c in order:
                dstate[j, d, c] = now.astype(BF16)
                rows_x[c] = kept[c : c + 1, :] * jnp.sum(
                    enter[j, d, c].astype(F32) * now, axis=0, keepdims=True
                )
                now = kept[c : c + 1, :] * now + dlocal[j, d, c].astype(F32)
            rows_x = jnp.concatenate(rows_x + [jnp.zeros((8 - blocks, cols), F32)], axis=0)
            xs[...] += mm_left(rows_x, spread[2 * j + d], 2, NT)
        return 0

    lax.fori_loop(0, shares, chain, 0, unroll=True)

    def states_part(c, _):
        at = pl.ds(pl.multiple_of(c * SPAN, SPAN), SPAN)
        weights = dec[2, at, :].astype(BF16)

        def share(j, total):
            for p in range(pages):
                lanes = slice(p * LANES, (p + 1) * LANES)
                xv = x[j, at, lanes].astype(F32)
                dx = dxi[j, at, lanes].astype(F32)
                for d in range(2):
                    grow = spread[2 * j + d, :, lanes]
                    wide = mm(weights, grow)
                    through = mm(bc[2 * d, at, :ns], dstate[j, d, c, :, lanes]) * wide
                    dx = dx + through
                    total = total + mm((through * xv).astype(BF16), grow, NT)
                    dst[2 * d, at, :ns] += mm((wide * xv).astype(BF16), dstate[j, d, c, :, lanes], NT)
                uv = u[j, at, lanes].astype(F32)
                sig = sigmoid(uv)
                du[j, pl.ds(pl.multiple_of(c * SPAN + HALO, HALO), SPAN), lanes] = dx * sig * (
                    1.0 + uv * (1.0 - sig)
                )
            return total

        qs[at, :] = lax.fori_loop(0, shares, share, jnp.zeros((SPAN, LANES), F32), unroll=True)
        return 0

    lax.fori_loop(0, blocks, states_part, 0)
    parts = [(0, HALO)] + [(HALO + c * SPAN, SPAN) for c in range(blocks)]

    def values(j, _):
        for p in range(pages):
            lanes = slice(p * LANES, (p + 1) * LANES)
            near = pl.ds(pl.multiple_of(j * cols + p * LANES, LANES), LANES)
            sums = [jnp.zeros((8, LANES), F32) for _ in range(TAPS)]
            for start, size in parts:
                old = vext[j, pl.ds(start, size), lanes].astype(F32)
                dv = None
                for m in range(TAPS):
                    shifted = du[j, pl.ds(start + TAPS - 1 - m, size), lanes]
                    term = vk[m : m + 1, near] * shifted
                    dv = term if dv is None else dv + term
                    sums[m] = sums[m] + fold(old * shifted)
                dp[j, pl.ds(start, size), lanes] = dv.astype(BF16)
            for m in range(TAPS):
                row = jnp.sum(sums[m], axis=0, keepdims=True)
                small[pl.ds(m * shares * pages + j * pages + p, 1), :] = row
            row = jnp.sum(rowsum[j, 0, :, lanes], axis=0, keepdims=True)
            small[pl.ds(cfg["gain_row"] + j * pages + p, 1), :] = row
        return 0

    lax.fori_loop(0, shares, values, 0, unroll=True)

    lane = iota((SPAN, LANES), 1)
    is_fwd = lane % (2 * own) < own
    at0, at1 = iota((SPAN, SPAN), 0), iota((SPAN, SPAN), 1)
    both = jnp.concatenate([(at0 > at1).astype(F32), (at0 < at1).astype(F32)], axis=0).astype(BF16)
    dbias = jnp.zeros((1, LANES), F32)
    ddecay = jnp.zeros((1, LANES), F32)
    steps = []
    for c in range(blocks):
        at = chunk_rows(c)
        qv = qs[at, :]
        sums = mm_right(both, qv, 2)
        total = da[at, :] + xs[c : c + 1, :] + jnp.where(is_fwd, sums[:SPAN], sums[SPAN:])
        through = total * dec[0, at, :]
        step = (dk[at, :] + qv + through) * dec[1, at, :]
        step = jnp.where(lane < 2 * own * shares, step, 0.0)
        steps.append(step)
        dbias = dbias + jnp.sum(step, axis=0, keepdims=True)
        ddecay = ddecay + jnp.sum(through, axis=0, keepdims=True)
    base = cfg["rest_row"]
    small[base : base + 1, :] = dbias
    small[base + 1 : base + 2, :] = ddecay
    skips = jnp.zeros((8, LANES), F32)
    for j in range(shares):
        skips = skips + mm_left(rowsum[j, 1], spread[2 * j], 2, NT)
    small[base + 2 : base + 3, :] = jnp.sum(skips, axis=0, keepdims=True)
    small[base + 3 : base + 8, :] = jnp.zeros((5, LANES), F32)

    for k in range(4):
        for c in range(blocks):
            at = chunk_rows(c)
            uv = su[k, at, :]
            sig = sigmoid(uv)
            dsu[k, chunk_rows(c, HALO), :] = dst[k, at, :] * sig * (1.0 + uv * (1.0 - sig))
        sums = [jnp.zeros((8, LANES), F32) for _ in range(TAPS)]
        for start, size in parts:
            old = side[k, pl.ds(start, size), :]
            dv = None
            for m in range(TAPS):
                shifted = dsu[k, pl.ds(start + TAPS - 1 - m, size), :]
                term = sk[k, m : m + 1, :] * shifted
                dv = term if dv is None else dv + term
                sums[m] = sums[m] + fold(old * shifted)
            if start >= HALO:
                moved = pltpu.roll(steps[(start - HALO) // SPAN], (ns - 2 * own * k) % LANES, 1)
                dv = dv + jnp.where((lane >= ns) & (lane < ns + 2 * own), moved, 0.0)
            dp[k, pl.ds(start, size), pl.ds(cols, LANES)] = dv.astype(BF16)
        for m in range(TAPS):
            row = cfg["state_row"] + m * 4 + k
            small[row : row + 1, :] = jnp.sum(sums[m], axis=0, keepdims=True)
    small[cfg["input_row"] :, :] = jnp.zeros_like(small[cfg["input_row"] :, :])


def last_kernel(cfg, *refs):
    ids, halo, inputs, normed, dp, w1, gx, small_in = refs[:8]
    gn, small = refs[8:10]
    pieces, held = refs[10:-1], refs[-1]
    shares, rows, width = cfg["shares"], cfg["rows"], inputs.shape[1]

    def project(d, _):
        j = (ids[0] + shares - d) % shares
        held[...] = mm(normed[...], dp[j], TN).astype(BF16)
        take_grads(ids, pieces, held, d, cfg["per"])
        back = mm(dp[j], w1[j], NT)

        @pl.when(d == 0)
        def _():
            gn[...] = back
            gn[HALO:, :] += gx[...]

        @pl.when(d > 0)
        def _():
            gn[...] += back

        return 0

    lax.fori_loop(0, shares, project, 0, unroll=True)

    def plain(block):
        wide = block.astype(F32)
        return wide * lax.rsqrt(jnp.mean(wide * wide, axis=1, keepdims=True) + EPSILON)

    ahead = jnp.where(ids[0] > 0, gn[0:HALO, :] * plain(halo[...]), 0.0)
    total = fold(ahead)
    for c in range(rows // SPAN):
        total = total + fold(gn[chunk_rows(c, HALO), :] * plain(inputs[chunk_rows(c), :]))
    total = jnp.sum(total, axis=0, keepdims=True)
    small[...] = small_in[...]
    for b in range(width // LANES):
        row = cfg["input_row"] + b
        small[row : row + 1, :] = total[:, b * LANES : (b + 1) * LANES]


def finish_kernel(cfg, ids, inputs, cot, gain, gn, edge, out):
    rows = cfg["rows"]
    size = SPAN // 2
    for c in range(rows // size):
        at = pl.ds(c * size, size)
        wide = inputs[at, :].astype(F32)
        g = gn[pl.ds(HALO + c * size, size), :]
        if c == rows // size - 1:
            g = jnp.concatenate([g[: size - HALO], g[size - HALO :] + edge[...]], axis=0)
        scale = lax.rsqrt(jnp.mean(wide * wide, axis=1, keepdims=True) + EPSILON)
        f = g * gain[...]
        mean = jnp.mean(f * wide, axis=1, keepdims=True)
        grad = cot[at, :].astype(F32) + scale * f - wide * (scale * scale * scale) * mean
        out[at, :] = grad.astype(BF16)


def gather_line(pack, shares):
    return jnp.stack([pack] + [along(pack, d, shares) for d in range(1, shares)])


def gather_layer(held, groups):
    return [held] + [lax.ppermute(held, "dp", xor(groups, 2 * k)) for k in range(1, groups // 2)]


def gather_pair(near, groups):
    pieces = []
    for block in near:
        pieces += [block, lax.ppermute(block, "dp", xor(groups, 1))]
    return pieces


def gather_any(pack):
    rows = lax.all_gather(pack, "dp", axis=0, tiled=True)
    return [lax.all_gather(rows, "tensor", axis=0, tiled=False)]


def scatter_any(pieces):
    part = lax.psum_scatter(pieces[0].astype(F32), "dp", scatter_dimension=1, tiled=True)
    return lax.psum_scatter(part, "tensor", scatter_dimension=0, tiled=False)


def scatter_pair(cfg, ids, keep, send):
    groups, shares, per, c = cfg["groups"], cfg["shares"], cfg["per"], keep.shape[-1]
    other = lax.ppermute(send, "dp", xor(groups, 1))
    shapes = tuple(sds((shares, per, c), BF16) for _ in range(groups // 2))
    return call(pair_kernel, shapes, us=1.5)(ids, keep, other)


def scatter_layer(groups, pairs):
    return [pairs[0]] + [lax.ppermute(pairs[k], "dp", xor(groups, 2 * k)) for k in range(1, groups // 2)]


def layer_sum(cfg, ids, parts, first):
    shares, per, cols = (cfg[k] for k in ("shares", "per", "cols"))
    return call(
        functools.partial(quad_kernel, cfg, first),
        (sds((per, 2 * cols), BF16),) * shares,
        scratch=[pltpu.VMEM((shares, per, LANES), F32)],
        us=1.5,
    )(ids, *parts)


def scatter_line(shares, blocks):
    return [blocks[0]] + [along(blocks[d], shares - d, shares) for d in range(1, shares)]


def shards(
    inputs, gate_weight, value_weight, step_weight, shared_weight, output_weight, value_kernel,
    shared_kernel, step_bias, decay_log, skip_gain, input_gain, output_gain, cotangent,
):
    shares, groups = lax.axis_size("tensor"), lax.axis_size("dp")
    z, g = lax.axis_index("tensor"), lax.axis_index("dp")
    rows, width = inputs.shape
    per, cols = gate_weight.shape
    own = step_weight.shape[2]
    heads = own * shares
    ns = shared_weight.shape[1] // 4
    inner = cols * shares
    blocks, pages = rows // SPAN, cols // LANES
    fast = groups == 8 and per % 32 == 0
    cfg = dict(
        shares=shares, groups=groups, own=own, head=cols // own, cols=cols, rows=rows, state=ns, per=per,
        pieces=groups if fast else 1,
    )
    cfg["gain_row"] = TAPS * shares * pages
    cfg["state_row"] = cfg["gain_row"] + shares * pages
    cfg["rest_row"] = cfg["state_row"] + 4 * TAPS
    cfg["input_row"] = cfg["rest_row"] + 8
    small_rows = -(-(cfg["input_row"] + width // LANES) // 8) * 8
    ids = jnp.stack([z, g]).astype(jnp.int32)
    ext = HALO + rows
    pk = cols + LANES

    edge_rows = inputs[rows - HALO :]
    shared_own = lax.dynamic_slice_in_dim(shared_weight, z * ns, ns, 1)
    flat_step = step_weight.reshape(per, 2 * own)
    blank = jnp.zeros((per, LANES - ns - 2 * own), BF16)
    pack1 = jnp.concatenate([value_weight, shared_own, flat_step, blank], axis=1)
    pack2 = jnp.concatenate([gate_weight, output_weight.T], axis=1)

    def by_lane(v):
        v = v.reshape(-1, 2, shares, own).transpose(0, 2, 1, 3).reshape(-1, 2 * heads)
        return jnp.pad(v, ((0, 8 - v.shape[0]), (0, LANES - 2 * heads)))

    params = by_lane(
        jnp.stack([step_bias, jnp.broadcast_to(decay_log, (2, heads)), jnp.broadcast_to(skip_gain, (2, heads))])
    )
    sk = jnp.pad(
        shared_kernel.reshape(TAPS, 4, ns).transpose(1, 0, 2), ((0, 0), (0, 8 - TAPS), (0, LANES - ns))
    )
    ogain = output_gain.reshape(shares, 1, cols)
    gain = input_gain.reshape(1, width)

    if fast:
        line1 = gather_line(pack1, shares)
        pack2 = jnp.concatenate([pack2, edge_rows], axis=0)
        line2 = [pack2] + [along(after(pack2, line1), d, shares) for d in range(1, shares)]
        halo = line2[1][per:]
        line2 = jnp.stack([block[:per] for block in line2])
        near1 = gather_layer(line1, groups)
        near1, params, sk, ogain, gain, ids = lax.optimization_barrier((near1, params, sk, ogain, gain, ids))
        parts1 = gather_pair(near1, groups)
        near2 = gather_layer(after(line2, *near1), groups)
    else:
        parts1, parts2 = gather_any(pack1), gather_any(pack2)
        halo = along(edge_rows, 1, shares)

    (
        w1, normed, vext, u, x, side, su, bc, bct, c2, rho2, c2t, rho2t, dec, states, tots, spread,
        *pays,
    ) = call(
        functools.partial(front_kernel, cfg),
        (
            sds((shares, width, pk), BF16),
            sds((ext, width), BF16),
            sds((shares, ext, cols), BF16),
            sds((shares, rows, cols), BF16),
            sds((shares, rows, cols), BF16),
            sds((shares, ext, LANES)),
            sds((4, rows, LANES)),
            sds((4, rows, LANES), BF16),
            sds((4, blocks, LANES, SPAN), BF16),
            sds((rows, LANES)),
            sds((rows, LANES)),
            sds((blocks, LANES, SPAN)),
            sds((blocks, LANES, SPAN)),
            sds((4, rows, LANES)),
            sds((shares, 2, blocks, ns, cols), BF16),
            sds((2 * blocks, LANES)),
            sds((2 * shares, LANES, cols), BF16),
            *[sds((shares * ns + HALO, cols), BF16)] * 3,
        ),
        scratch=[pltpu.VMEM((ext, pk), F32)],
        us=14.0,
    )(ids, halo, inputs, gain, value_kernel, sk, params, *parts1)
    got = spread_out(pays, shares)

    yin = call(functools.partial(within_kernel, cfg), sds((shares, rows, cols), BF16), us=5.0)(
        ids, bc, c2, rho2t, x
    )
    if fast:
        parts2 = gather_pair(after(near2, yin), groups)
    w2, gate, gn_out = call(
        functools.partial(gate_kernel, cfg),
        (sds((shares, width, 2 * cols), BF16),) + (sds((shares, rows, cols), BF16),) * 2,
        us=6.0,
    )(ids, normed, cotangent, *parts2)

    enter, dy, normal, dgate, rr, dlocal, rowsum, keeps, *pays = call(
        functools.partial(middle_kernel, cfg),
        (
            sds((shares, 2, blocks, ns, cols), BF16),
            sds((shares, rows, cols), BF16),
            sds((shares, rows, cols), BF16),
            sds((shares, rows, cols), BF16),
            sds((rows, LANES)),
            sds((shares, 2, blocks, ns, cols), BF16),
            sds((shares, 2, 8, cols)),
            sds((shares, 3, HALO, cols)),
            *[sds((shares * ns, cols), BF16)] * 3,
        ),
        scratch=[pltpu.VMEM((shares, SPAN, cols), F32)] * 2 + [pltpu.VMEM((shares, SPAN, cols), BF16)] * 2,
        us=16.0,
    )(ids, yin, x, gate, gn_out, states, bc, bct, dec, tots, spread, params, ogain, *got)
    got = spread_out(pays, shares)

    def piece_shapes(c):
        if fast:
            return (sds((groups // 2, shares, per, c), BF16),) * 2
        return (sds((shares, width, c), BF16),)

    mixed, gx, *grads2 = call(
        functools.partial(output_kernel, cfg),
        (sds((rows, width), BF16), sds((rows, width))) + piece_shapes(2 * cols),
        scratch=[pltpu.VMEM((rows, width), F32), pltpu.VMEM((width, 2 * cols), BF16)],
        us=10.0,
    )(ids, inputs, cotangent, normed, normal, dgate, w2)
    dy_late = dy
    if fast:
        pairs2 = scatter_pair(cfg, ids, *grads2)
        dy_late = after(dy, pairs2)

    dxi, dbc, da, dk = call(
        functools.partial(back_within_kernel, cfg),
        (sds((shares, rows, cols), BF16), sds((4, rows, LANES)), sds((rows, LANES)), sds((rows, LANES))),
        scratch=[pltpu.VMEM((LANES, SPAN), F32), pltpu.VMEM((LANES, SPAN), F32)],
        us=9.0,
    )(ids, bc, bct, rho2, c2t, x, dy_late, dec, spread, enter, rr, keeps)
    if fast:
        layer2 = scatter_layer(groups, pairs2)

    dp, small = call(
        functools.partial(tail_kernel, cfg),
        (sds((shares, ext, pk), BF16), sds((small_rows, LANES))),
        scratch=[
            pltpu.VMEM((shares, ext + HALO, cols), F32),
            pltpu.VMEM((4, ext + HALO, LANES), F32),
            pltpu.VMEM((4, rows, LANES), F32),
            pltpu.VMEM((shares, 2, blocks, ns, cols), BF16),
            pltpu.VMEM((8, LANES), F32),
            pltpu.VMEM((rows, LANES), F32),
            pltpu.VMEM((8, LANES), F32),
        ],
        us=16.0,
    )(
        ids, x, u, dxi, vext, side, su, bc, dbc, dec, enter, da, dk, dlocal, rowsum, keeps, spread,
        *got, value_kernel, sk,
    )
    if fast:
        blocks2 = layer_sum(cfg, ids, layer2, False)
        dp = after(dp, blocks2)
    gn, small, *grads1 = call(
        functools.partial(last_kernel, cfg),
        (sds((ext, width)), sds((small_rows, LANES))) + piece_shapes(pk),
        scratch=[pltpu.VMEM((width, pk), BF16)],
        us=7.0,
    )(ids, halo, inputs, normed, dp, w1, gx, small)
    first_rows = gn[:HALO]
    if fast:
        pairs1 = scatter_pair(cfg, ids, *grads1)
        small, first_rows = after((small, first_rows), pairs1)
        layer1 = scatter_layer(groups, pairs1)
        line2 = scatter_line(shares, blocks2)
        grad_gate, grad_output = call(
            functools.partial(line2_kernel, cfg), (sds((per, cols)), sds((per, cols))), us=1.0
        )(ids, *line2)
        grad_value, grad_step, grad_shared = call(
            functools.partial(line_kernel, cfg),
            (sds((per, cols)), sds((per, 2 * own)), sds((per, shares * ns))),
            scratch=[pltpu.VMEM((shares, per, 2 * cols), F32)],
            us=1.0,
        )(ids, *scatter_line(shares, layer_sum(cfg, ids, layer1, True)))

        small = small + lax.ppermute(small, "dp", xor(groups, 1))
        four = [small] + [lax.ppermute(small, "dp", xor(groups, 2 * k)) for k in range(1, groups // 2)]

        def add(parts, places):
            return call(
                sum_kernel,
                sds((small_rows, LANES)),
                scratch=[pltpu.VMEM((len(parts), small_rows, LANES), F32)],
                us=1.0,
            )(jnp.stack(places).astype(jnp.int32), *parts)

        small = add(four, [m ^ (g // 2) for m in range(groups // 2)])
        line = [small] + [along(small, d, shares) for d in range(1, shares)]
        small = add(line, [(z + shares - m) % shares for m in range(shares)])
    else:
        out1, out2 = scatter_any(grads1), scatter_any(grads2)
        grad_gate, grad_output = out2[:, :cols], out2[:, cols:]
        grad_value, grad_step = out1[:, :cols], out1[:, cols + ns : cols + ns + 2 * own]
        grad_shared = lax.all_gather(out1[:, cols : cols + ns], "tensor", axis=1, tiled=True)
        small = lax.psum(small, ("dp", "tensor"))

    edge = lax.ppermute(first_rows, "tensor", [(i + 1, i) for i in range(shares - 1)])
    grad_input = call(functools.partial(finish_kernel, cfg), sds((rows, width), BF16), us=2.0)(
        ids, inputs, cotangent, gain, gn, edge
    )

    def from_lane(v):
        return v[: 2 * heads].reshape(shares, 2, own).transpose(1, 0, 2).reshape(2, heads)

    rest = cfg["rest_row"]
    return (
        mixed,
        grad_input,
        grad_gate,
        grad_value,
        grad_step.reshape(per, 2, own),
        grad_shared,
        grad_output.T,
        small[: cfg["gain_row"]].reshape(TAPS, inner),
        small[cfg["state_row"] : rest].reshape(TAPS, 4, LANES)[:, :, :ns].reshape(TAPS, 4 * ns),
        from_lane(small[rest]),
        from_lane(small[rest + 1]).sum(axis=0),
        from_lane(small[rest + 2])[0],
        small[cfg["input_row"] : cfg["input_row"] + width // LANES].reshape(width),
        small[cfg["gain_row"] : cfg["state_row"]].reshape(inner),
    )


def solution(mesh):
    both = P(("dp", "tensor"), None)
    placed = (
        both, P("dp", "tensor"), P("dp", "tensor"), P("dp", None, "tensor"), P("dp", None),
        P("tensor", "dp"), P(), P(), P(), P(), P(), P(), P(), both,
    )
    return jax.shard_map(
        shards,
        mesh=mesh,
        in_specs=placed,
        out_specs=(
            both, both, P("dp", "tensor"), P("dp", "tensor"), P("dp", None, "tensor"), P("dp", None),
            P("tensor", "dp"), P(), P(), P(), P(), P(), P(), P(),
        ),
        check_vma=False,
    )
```

```python
import functools

import jax
import jax.numpy as jnp
from jax import lax
from jax.experimental import pallas as pl
from jax.experimental.pallas import tpu as pltpu
from jax.sharding import PartitionSpec as P

F32 = jnp.float32
BF16 = jnp.bfloat16
EPSILON = 1e-06
SPAN = 128
HALO = 16
TAPS = 4
LANES = 128
LOG2E = 1.4426950408889634
EXACT = lax.Precision.HIGHEST
LIMIT = 4 * 1024 * 1024
MB = 1024 * 1024

NN = (((1,), (0,)), ((), ()))
NT = (((1,), (1,)), ((), ()))
TN = (((0,), (0,)), ((), ()))


def mm(a, b, dims=NN, precision=None):
    return lax.dot_general(a, b, dims, preferred_element_type=F32, precision=precision)


def iota(shape, dim):
    return lax.broadcasted_iota(jnp.int32, shape, dim)


def sigmoid(v):
    return 0.5 * jnp.tanh(0.5 * v) + 0.5


def split(v, n):
    parts = []
    for _ in range(n):
        part = v.astype(BF16)
        parts.append(part)
        v = v - part.astype(F32)
    return parts


def mm_right(ones, v, n):
    total = None
    for part in split(v, n):
        term = mm(ones, part)
        total = term if total is None else total + term
    return total


def mm_left(v, ones, n, dims=(((1,), (0,)), ((), ()))):
    total = None
    for part in split(v, n):
        term = mm(part, ones, dims)
        total = term if total is None else total + term
    return total


def fold(v):
    return v.reshape(v.shape[0] // 8, 8, v.shape[1]).sum(axis=0)


def chunk_rows(c, base=0):
    return pl.ds(base + c * SPAN, SPAN)


def call(kernel, out_shape, scratch=(), us=1.0, limit=LIMIT):
    def run(*args):
        specs = [
            pl.BlockSpec(memory_space=pltpu.SMEM if i == 0 else pltpu.VMEM)
            for i in range(len(args))
        ]
        return pl.pallas_call(
            kernel,
            out_shape=out_shape,
            in_specs=specs,
            out_specs=jax.tree.map(lambda _: pl.BlockSpec(memory_space=pltpu.VMEM), out_shape),
            scratch_shapes=list(scratch),
            cost_estimate=pl.CostEstimate(
                flops=int(us * 1.1e9), bytes_accessed=int(us * 3.0e6), transcendentals=0
            ),
            compiler_params=pltpu.CompilerParams(vmem_limit_bytes=limit),
        )(*args)

    return run


def sds(shape, dtype=F32):
    return jax.ShapeDtypeStruct(shape, dtype)


def put_weights(ids, pieces, full, shares, per):
    if len(pieces) == 1:
        full[...] = pieces[0][...]
        return
    for rel, piece in enumerate(pieces):
        row = pl.multiple_of((ids[1] ^ rel) * per, per)
        for d in range(shares):
            j = (ids[0] + shares - d) % shares
            full[j, pl.ds(row, per), :] = piece[d]


def take_grads(ids, pieces, held, d, per):
    if len(pieces) == 1:
        shares = pieces[0].shape[0]
        pieces[0][(ids[0] + shares - d) % shares] = held[...]
        return
    for rel in range(2 * pieces[0].shape[0]):
        row = pl.multiple_of((ids[1] ^ rel) * per, per)
        pieces[rel % 2][rel // 2, d] = held[pl.ds(row, per), :]


def cyclic(size, d):
    return [(i, (i + d) % size) for i in range(size)]


def xor(size, bit):
    return [(i, i ^ bit) for i in range(size)]


def along(v, d, shares):
    return lax.ppermute(v, "tensor", cyclic(shares, d))


def spread_out(parts, shares):
    return [along(part, d + 1, shares) for d, part in enumerate(parts)]


def after(values, *others):
    out = lax.optimization_barrier((values,) + others)
    return out[0]


def pair_kernel(n, ids, keep, other, *refs):
    for k in range(n):
        refs[len(refs) - n + k][...] = (keep[k].astype(F32) + other[k].astype(F32)).astype(BF16)
    if len(refs) > n:
        mine, theirs, total = refs[:3]
        total[...] = mine[...] + theirs[...]


def quad_kernel(cfg, first, ids, *refs):
    n, shares, cols, ns = cfg["groups"] // 2, cfg["shares"], cfg["cols"], cfg["state"]
    parts, outs, held = refs[:n], refs[n:-1], refs[-1]
    for d in range(shares):
        q = (ids[0] + shares - d) % shares
        total = parts[0][d].astype(F32)
        for part in parts[1:]:
            total = total + part[d].astype(F32)
        if first:
            outs[d][:, :cols] = total[:, :cols].astype(BF16)
            held[q] = total[:, cols:]
        else:
            outs[d][...] = total.astype(BF16)
    if first:
        low = iota((outs[0].shape[0], LANES), 1) < ns
        for k in range(shares // 2):
            both = jnp.where(low, held[2 * k], pltpu.roll(held[2 * k + 1], ns, 1)).astype(BF16)
            for out in outs:
                out[:, cols + k * LANES : cols + (k + 1) * LANES] = both
        for d, out in enumerate(outs):
            step = held[(ids[0] + shares - d) % shares]
            out[:, cols + shares * ns :] = jnp.where(low, pltpu.roll(step, LANES - ns, 1), 0.0).astype(BF16)


def line_kernel(cfg, ids, *refs):
    shares, cols, ns = cfg["shares"], cfg["cols"], cfg["state"]
    parts, (value, step, shared, held) = refs[:shares], refs[shares:]
    for e, part in enumerate(parts):
        held[e] = part[...].astype(F32)
    total = held[(shares - ids[0]) % shares]
    for q in range(1, shares):
        total = total + held[(q + shares - ids[0]) % shares]
    value[...] = total[:, :cols]
    shared[...] = total[:, cols : cols + shares * ns]
    step[...] = total[:, cols + shares * ns :][:, : step.shape[1]]


def line2_kernel(cfg, ids, *refs):
    shares, cols = cfg["shares"], cfg["cols"]
    parts, (gate, out) = refs[:shares], refs[shares:]
    total = parts[0][...].astype(F32)
    for part in parts[1:]:
        total = total + part[...].astype(F32)
    gate[...] = total[:, :cols]
    out[...] = total[:, cols:]


def fill_spread(cfg, spread):
    own, head = cfg["own"], cfg["head"]
    block = own * head
    for j in range(cfg["shares"]):
        lane = iota((LANES, block), 0)
        place = iota((LANES, block), 1) // head
        for d in range(2):
            cols = slice(j * block, (j + 1) * block)
            spread[d, :, cols] = (lane == own * (2 * j + d) + place).astype(F32).astype(BF16)


def prep_kernel(ids, inputs, cot, gain, normed, normed_t, cot_t):
    size = SPAN // 2
    for c in range(inputs.shape[0] // size):
        at = pl.ds(c * size, size)
        wide = inputs[at, :].astype(F32)
        scale = lax.rsqrt(jnp.mean(wide * wide, axis=1, keepdims=True) + EPSILON)
        normed[at, :] = (wide * scale * gain[...]).astype(BF16)
    normed_t[...] = normed[...].T
    cot_t[...] = cot[...].T


def front_kernel(cfg, *refs):
    n = cfg["pieces"]
    ids, halo, normed, gain, vk, sk, params = refs[:7]
    pieces = refs[7 : 7 + n]
    (
        w1, ahead, vext, u_out, x_out, wide_out, side, su_out, bc_out, cct, c2, rho2, c2t, rho2t, dec, states,
        tots, spread, pay1, pay2, pay3, acc, bbt, xw,
    ) = refs[7 + n :]
    shares, own, cols, rows, ns = (cfg[k] for k in ("shares", "own", "cols", "rows", "state"))
    blocks, pages = rows // SPAN, cols // LANES
    put_weights(ids, pieces, w1, shares, cfg["per"])
    fill_spread(cfg, spread)

    edge = halo[...].astype(F32)
    scale = lax.rsqrt(jnp.mean(edge * edge, axis=1, keepdims=True) + EPSILON)
    ahead[...] = jnp.where(ids[0] > 0, edge * scale * gain[...], 0.0).astype(BF16)
    bbt[...] = jnp.zeros_like(bbt)
    cct[...] = jnp.zeros_like(cct)

    for j in range(shares):
        acc[0:HALO, :] = mm(ahead[...], w1[j])
        acc[HALO:, :] = mm(normed[...], w1[j])
        side[j] = acc[:, cols : cols + LANES]
        vext[:, j * cols : (j + 1) * cols] = acc[:, :cols].astype(BF16)
        for c in range(blocks):
            for p in range(pages + 1):
                lanes = slice(p * LANES, (p + 1) * LANES)
                here = slice(j * cols + p * LANES, j * cols + (p + 1) * LANES)
                u = None
                for m in range(TAPS):
                    tap = vk[m : m + 1, here] if p < pages else sk[j, m : m + 1, :]
                    term = tap * acc[chunk_rows(c, HALO - TAPS + 1 + m), lanes]
                    u = term if u is None else u + term
                v = u * sigmoid(u)
                if p < pages:
                    u_out[chunk_rows(c), here] = u.astype(BF16)
                    x_out[chunk_rows(c), here] = v.astype(BF16)
                else:
                    su_out[j, chunk_rows(c), :] = u
                    bc_out[j, chunk_rows(c), :] = v.astype(BF16)
                    turned = v.T[:ns].astype(BF16)
                    d = j // 2
                    target = cct if j % 2 else bbt
                    target[c, d * ns : (d + 1) * ns, d * SPAN : (d + 1) * SPAN] = turned

    lane = iota((SPAN, LANES), 1)
    is_fwd = lane % (2 * own) < own
    at0, at1 = iota((SPAN, SPAN), 0), iota((SPAN, SPAN), 1)
    both = jnp.concatenate([(at0 >= at1).astype(F32), (at0 <= at1).astype(F32)], axis=0).astype(BF16)
    rate = jnp.where(iota((1, LANES), 1) < 2 * own * shares, -jnp.exp(params[1:2, :]), 0.0)
    for c in range(blocks):
        raw = jnp.zeros((SPAN, LANES), F32)
        for j in range(shares):
            moved = pltpu.roll(side[j, chunk_rows(c, HALO), :], (2 * own * j - ns) % LANES, 1)
            raw = jnp.where((lane >= 2 * own * j) & (lane < 2 * own * (j + 1)), moved, raw)
        v = raw + params[0:1, :]
        small = jnp.exp(jnp.minimum(v, 0.0))
        dt = jnp.where(v < -15.0, small, jnp.maximum(v, 0.0) + jnp.log1p(jnp.exp(-jnp.abs(v))))
        log_dt = jnp.where(v < -15.0, v, jnp.log(jnp.maximum(dt, 1e-30)))
        ratio = jnp.where(v < -15.0, 1.0, sigmoid(v) / jnp.maximum(dt, 1e-30))
        a = dt * rate
        sums = mm_right(both, a, 3)
        cum = jnp.where(is_fwd, sums[:SPAN], sums[SPAN:])
        tot = jnp.sum(a, axis=0, keepdims=True)
        rho = cum - log_dt
        cc = cum * LOG2E
        rr = rho * LOG2E
        c2[chunk_rows(c), :] = cc
        rho2[chunk_rows(c), :] = rr
        c2t[c] = cc.T
        rho2t[c] = rr.T
        dec[0, chunk_rows(c), :] = a
        dec[1, chunk_rows(c), :] = ratio
        dec[2, chunk_rows(c), :] = jnp.exp(tot - rho)
        dec[3, chunk_rows(c), :] = jnp.exp(cum)
        tots[c : c + 1, :] = tot
    fwd1 = iota((1, LANES), 1) % (2 * own) < own
    zero = jnp.zeros((1, LANES), F32)
    lead = []
    for c in range(blocks):
        later, sooner = zero, zero
        for k in range(blocks):
            if k > c:
                later = later + tots[k : k + 1, :]
            if k < c:
                sooner = sooner + tots[k : k + 1, :]
        lead.append(jnp.exp(jnp.where(fwd1, later, sooner)))
        tots[blocks + c : blocks + c + 1, :] = jnp.where(fwd1, sooner, later)
    lead = jnp.concatenate(lead + [zero] * (8 - blocks), axis=0)
    whole = tots[0:1, :]
    for c in range(1, blocks):
        whole = whole + tots[c : c + 1, :]
    extra = jnp.concatenate([p.astype(F32) for p in split(whole, 3)] + [zero] * (HALO - 3), axis=0)
    extra = jnp.concatenate([extra, jnp.zeros((HALO, cols - LANES), F32)], axis=1).astype(BF16)
    for pay in (pay1, pay2, pay3):
        pay[shares * ns :, :] = extra

    weights = dec[2].astype(BF16)
    for d in range(2):
        wide_out[d] = mm(weights, spread[d]).astype(BF16)
    grow_f, grow_b = mm_left(lead, spread[0], 2), mm_left(lead, spread[1], 2)
    for c in range(blocks):
        for d in range(2):
            for p in range(shares * pages):
                lanes = slice(p * LANES, (p + 1) * LANES)
                product = wide_out[d, chunk_rows(c), lanes].astype(F32) * x_out[chunk_rows(c), lanes].astype(F32)
                xw[d * SPAN : (d + 1) * SPAN, lanes] = product.astype(BF16)
        states[c] = mm(bbt[c], xw[...]).astype(BF16)
    for j in range(shares):
        at = slice(j * ns, (j + 1) * ns)
        here = slice(j * cols, (j + 1) * cols)
        f, b = jnp.zeros((ns, cols), F32), jnp.zeros((ns, cols), F32)
        for c in range(blocks):
            f = f + grow_f[c : c + 1, here] * states[c, :ns, here].astype(F32)
            b = b + grow_b[c : c + 1, here] * states[c, ns:, here].astype(F32)
        for dist, pay in ((1, pay1), (2, pay2), (3, pay3)):
            pay[at, :] = jnp.where(ids[0] + dist < shares, f, b).astype(BF16)


def stack_pair(first, v):
    zero = jnp.zeros_like(v)
    return jnp.concatenate([jnp.where(first, v, zero), jnp.where(first, zero, v)], axis=0)


def within_kernel(cfg, ids, bc, c2, rho2t, x, y):
    shares, own, rows = (cfg[k] for k in ("shares", "own", "rows"))
    t, s = iota((SPAN, SPAN), 0), iota((SPAN, SPAN), 1)
    low = t > s
    first = iota((SPAN, LANES), 1) < cfg["head"]

    def block(c, _):
        at = pl.ds(pl.multiple_of(c * SPAN, SPAN), SPAN)
        g = jnp.where(low, mm(bc[1, at, :], bc[0, at, :], NT), mm(bc[3, at, :], bc[2, at, :], NT))
        g = jnp.where(t == s, 0.0, g)
        cc = c2[at, :]
        for k in range(shares * own // 2):
            j, p = k // (own // 2), k % (own // 2)
            mats = []
            for i in (2 * p, 2 * p + 1):
                f, b = 2 * own * j + i, 2 * own * j + own + i
                col = jnp.where(low, cc[:, f : f + 1], cc[:, b : b + 1])
                row = jnp.where(low, rho2t[c, f : f + 1, :], rho2t[c, b : b + 1, :])
                mats.append((jnp.exp2(col - row) * g).astype(BF16))
            lanes = slice(k * LANES, (k + 1) * LANES)
            y[at, lanes] = mm(jnp.concatenate(mats, axis=1), stack_pair(first, x[at, lanes])).astype(BF16)
        return 0

    lax.fori_loop(0, rows // SPAN, block, 0)


def gate_kernel(cfg, *refs):
    n = cfg["pieces"]
    ids, normed, cot = refs[:3]
    pieces = refs[3 : 3 + n]
    w2, gate, gn = refs[3 + n :]
    shares, cols = (cfg[k] for k in ("shares", "cols"))
    put_weights(ids, pieces, w2, shares, cfg["per"])
    for j in range(shares):
        here = slice(j * cols, (j + 1) * cols)
        gate[:, here] = mm(normed[...], w2[j, :, :cols]).astype(BF16)
        gn[:, here] = mm(cot[...], w2[j, :, cols:]).astype(BF16)


def incoming(ids, cfg, got, j, near, far):
    z, shares, ns = ids[0], cfg["shares"], cfg["state"]
    r1, r2, r3 = (part[j * ns : (j + 1) * ns, :].astype(F32) for part in got)

    def keep(test, v):
        return jnp.where(test, v, 0.0)

    before = keep(z >= 1, r1) + near[0] * keep(z >= 2, r2) + near[1] * keep(z >= 3, r3)
    behind = (
        keep(z <= shares - 2, r3)
        + far[0] * keep(z <= shares - 3, r2)
        + far[1] * keep(z <= shares - 4, r1)
    )
    return before, behind


def middle_kernel(cfg, *refs):
    (
        ids, yin, x, gate, gn, states, bc, cct, dec, tots, spread, params, ogain, r1, r2, r3,
        enter, dy, normal, dgate, dcarry, rr, dlocal, rowsum, keeps, p1, p2, p3,
        ecx, ys, acts, kept, edy, prod,
    ) = refs
    shares, cols, rows, ns = (cfg[k] for k in ("shares", "cols", "rows", "state"))
    blocks, inner = rows // SPAN, cols * shares
    pages = inner // LANES
    zero = jnp.zeros((1, LANES), F32)

    def whole(r):
        v = r[shares * ns :, :LANES].astype(F32)
        return v[0:1, :] + v[1:2, :] + v[2:3, :]

    l1, l2, l3 = whole(r1), whole(r2), whole(r3)
    lines = [tots[c : c + 1, :] for c in range(2 * blocks)] + [l1, l1 + l2, l3, l3 + l2]
    lines = jnp.exp(jnp.concatenate(lines + [zero] * (HALO - len(lines)), axis=0))
    skip_rows = jnp.concatenate([params[2:3, :]] + [zero] * 7, axis=0)
    for d in range(2):
        keeps[d] = mm_left(lines, spread[d], 2)
        ecx[d] = mm(dec[3].astype(BF16), spread[d]).astype(BF16)
    keeps[2, 0:8] = mm_left(skip_rows, spread[0], 2)
    b = 2 * blocks
    for j in range(shares):
        here = slice(j * cols, (j + 1) * cols)
        kf, kb = keeps[0, :, here], keeps[1, :, here]
        e, e_b = incoming(
            ids, cfg, (r1, r2, r3), j,
            (kf[b : b + 1, :], kf[b + 1 : b + 2, :]), (kb[b + 2 : b + 3, :], kb[b + 3 : b + 4, :]),
        )
        for c in range(blocks):
            enter[c, :ns, here] = e.astype(BF16)
            e = kf[c : c + 1, :] * e + states[c, :ns, here].astype(F32)
        for c in reversed(range(blocks)):
            enter[c, ns:, here] = e_b.astype(BF16)
            e_b = kb[c : c + 1, :] * e_b + states[c, ns:, here].astype(F32)
    rowsum[...] = jnp.zeros_like(rowsum)

    def block(c, _):
        at = pl.ds(pl.multiple_of(c * SPAN, SPAN), SPAN)
        for d in range(2):
            kept[d] = mm(bc[1 + 2 * d, at, :ns], enter[c, d * ns : (d + 1) * ns, :])
        square, dot = jnp.zeros((SPAN, LANES), F32), jnp.zeros((SPAN, LANES), F32)
        for p in range(pages):
            lanes = slice(p * LANES, (p + 1) * LANES)
            cf = kept[0, :, lanes] * ecx[0, at, lanes].astype(F32)
            cb = kept[1, :, lanes] * ecx[1, at, lanes].astype(F32)
            kept[0, :, lanes] = cf
            kept[1, :, lanes] = cb
            v = yin[at, lanes].astype(F32) + keeps[2, 0:1, lanes] * x[at, lanes].astype(F32) + cf + cb
            ys[:, lanes] = v
            g = gate[at, lanes].astype(F32)
            act = g * sigmoid(g)
            acts[:, lanes] = act
            gated = v * act
            square = square + gated * gated
            dot = dot + gn[at, lanes].astype(F32) * ogain[:, lanes] * gated
        square = jnp.sum(square, axis=1, keepdims=True)
        dot = jnp.sum(dot, axis=1, keepdims=True)
        inv = lax.rsqrt(square / inner + EPSILON)
        back = inv * inv * inv * dot / inner
        for p in range(pages):
            lanes = slice(p * LANES, (p + 1) * LANES)
            v, act, g = ys[:, lanes], acts[:, lanes], gate[at, lanes].astype(F32)
            gnv, og = gn[at, lanes].astype(F32), ogain[:, lanes]
            sig = sigmoid(g)
            gated = v * act
            scaled = gated * inv
            normal[at, lanes] = (scaled * og).astype(BF16)
            rowsum[0, :, lanes] += fold(gnv * scaled)
            dgated = inv * (gnv * og) - gated * back
            d_scan = dgated * act
            dy[at, lanes] = d_scan.astype(BF16)
            dgate[at, lanes] = (dgated * v * (sig + act * (1.0 - sig))).astype(BF16)
            rowsum[1, :, lanes] += fold(d_scan * x[at, lanes].astype(F32))
            for d in range(2):
                prod[d, at, lanes] = (d_scan * kept[d, :, lanes]).astype(BF16)
                wide = ecx[d, at, lanes].astype(F32) * d_scan
                edy[d * SPAN : (d + 1) * SPAN, lanes] = wide.astype(BF16)
        dlocal[c] = mm(cct[c], edy[...]).astype(BF16)
        for d in range(2):
            dcarry[d, at, :] = mm(edy[d * SPAN : (d + 1) * SPAN, :], enter[c, d * ns : (d + 1) * ns, :], NT)
        return 0

    lax.fori_loop(0, blocks, block, 0)
    rr[...] = mm(prod[0], spread[0], NT) + mm(prod[1], spread[1], NT)

    for j in range(shares):
        here = slice(j * cols, (j + 1) * cols)
        f, b_ = jnp.zeros((ns, cols), F32), jnp.zeros((ns, cols), F32)
        for c in range(blocks):
            f = f + keeps[0, blocks + c : blocks + c + 1, here] * dlocal[c, :ns, here].astype(F32)
            b_ = b_ + keeps[1, blocks + c : blocks + c + 1, here] * dlocal[c, ns:, here].astype(F32)
        for dist, pay in ((1, p1), (2, p2), (3, p3)):
            pay[j * ns : (j + 1) * ns, :] = jnp.where(ids[0] + dist < shares, b_, f).astype(BF16)


def output_kernel(cfg, *refs):
    ids, inputs, cot_t, normed_t, normal, dgate, w2 = refs[:7]
    mixed, gx = refs[7:9]
    pieces, (total, held, spare) = refs[9:-3], refs[-3:]
    shares, cols = (cfg[k] for k in ("shares", "cols"))
    for j in range(shares):
        here = slice(j * cols, (j + 1) * cols)
        place = held if j % 2 else spare
        place[:, :cols] = mm(normed_t[...], dgate[:, here]).astype(BF16)
        place[:, cols:] = mm(cot_t[...], normal[:, here]).astype(BF16)
        take_grads(ids, pieces, place, (ids[0] + shares - j) % shares, cfg["per"])
        part = mm(normal[:, here], w2[j, :, cols:], NT)
        back = mm(dgate[:, here], w2[j, :, :cols], NT)
        if j == 0:
            total[...] = part
            gx[...] = back
        elif j < shares - 1:
            total[...] += part
            gx[...] += back
        else:
            mixed[...] = (total[...] + part + inputs[...].astype(F32)).astype(BF16)
            gx[...] += back


def back_within_kernel(cfg, ids, bc, rho2, c2t, x, dy, dcarry, rr, keeps, dx, dbc, da, dk, das, ras):
    shares, own, rows, ns = (cfg[k] for k in ("shares", "own", "rows", "state"))
    s, t = iota((SPAN, SPAN), 0), iota((SPAN, SPAN), 1)
    up = t > s
    first = iota((SPAN, LANES), 1) < cfg["head"]
    after_t = (s >= t).astype(F32).astype(BF16)
    until_t = (s <= t).astype(F32).astype(BF16)
    tri = jnp.concatenate([after_t, until_t], axis=1)
    sums = jnp.concatenate([until_t, after_t], axis=0)
    lane = iota((SPAN, LANES), 1)
    is_fwd = iota((LANES, SPAN), 0) % (2 * own) < own

    def block(c, _):
        at = pl.ds(pl.multiple_of(c * SPAN, SPAN), SPAN)
        g = jnp.where(up, mm(bc[0, at, :], bc[1, at, :], NT), mm(bc[2, at, :], bc[3, at, :], NT))
        g = jnp.where(t == s, 0.0, g)
        rho = rho2[at, :]
        dg = jnp.zeros((SPAN, SPAN), F32)
        das[...] = jnp.zeros_like(das)
        ras[...] = jnp.zeros_like(ras)
        for k in range(shares * own // 2):
            j, p = k // (own // 2), k % (own // 2)
            lanes = slice(k * LANES, (k + 1) * LANES)
            dyp = dy[at, lanes]
            dm = mm(stack_pair(first, x[at, lanes]), dyp, NT)
            ws, zs = [], []
            for q in range(2):
                i = 2 * p + q
                f, b = 2 * own * j + i, 2 * own * j + own + i
                row = jnp.where(up, c2t[c, f : f + 1, :], c2t[c, b : b + 1, :])
                col = jnp.where(up, rho[:, f : f + 1], rho[:, b : b + 1])
                pw = jnp.exp2(row - col)
                ud = dm[q * SPAN : (q + 1) * SPAN] * pw
                dg = dg + ud
                ws.append((pw * g).astype(BF16))
                zd = ud * g
                zs.append(zd.astype(BF16))
                rf = jnp.sum(jnp.where(up, zd, 0.0), axis=0, keepdims=True)
                ras[f : f + 1, :] = rf
                ras[b : b + 1, :] = jnp.sum(zd, axis=0, keepdims=True) - rf
            back = mm(jnp.concatenate(ws, axis=1), stack_pair(first, dyp))
            dx[at, lanes] = (back + keeps[2, 0:1, lanes] * dyp.astype(F32)).astype(BF16)
            cross = mm(jnp.concatenate(zs, axis=0), tri)
            for q in range(2):
                i = 2 * p + q
                f, b = 2 * own * j + i, 2 * own * j + own + i
                part = cross[q * SPAN : (q + 1) * SPAN]
                das[f : f + 1, :] = jnp.sum(jnp.where(up, part[:, :SPAN], 0.0), axis=0, keepdims=True)
                das[b : b + 1, :] = jnp.sum(jnp.where(t < s, part[:, SPAN:], 0.0), axis=0, keepdims=True)
        df = jnp.where(up, dg, 0.0)
        db = jnp.where(t < s, dg, 0.0)
        dbc[0, at, :] = mm(df.astype(BF16), bc[1, at, :])
        dbc[1, at, :] = mm(df.T.astype(BF16), bc[0, at, :])
        dbc[2, at, :] = mm(db.astype(BF16), bc[3, at, :])
        dbc[3, at, :] = mm(db.T.astype(BF16), bc[2, at, :])
        dbc[1, at, :ns] += dcarry[0, at, :]
        dbc[3, at, :ns] += dcarry[1, at, :]
        a = das[...]
        later = jnp.where(lane < SPAN - 1, pltpu.roll(a, SPAN - 1, 1), 0.0)
        sooner = jnp.where(lane > 0, pltpu.roll(a, 1, 1), 0.0)
        kd = ras[...] - a + jnp.where(is_fwd, later, sooner)
        through = mm_right(sums, rr[at, :], 2)
        da[at, :] = a.T + jnp.where(lane % (2 * own) < own, through[:SPAN], through[SPAN:])
        dk[at, :] = kd.T
        return 0

    lax.fori_loop(0, rows // SPAN, block, 0)


def tail_kernel(cfg, *refs):
    (
        ids, x, u, dxi, wide_in, vext, side, su, bc, dbc, dec, enter, da, dk, dlocal, rowsum, keeps, spread,
        r1, r2, r3, vk, sk,
        dp, small,
        du, dsu, dst, dstate, xs, qs, held, xw, prod,
    ) = refs
    shares, own, cols, rows, ns = (cfg[k] for k in ("shares", "own", "cols", "rows", "state"))
    blocks, inner = rows // SPAN, cols * shares
    pages = inner // LANES

    du[0:HALO, :] = jnp.zeros((HALO, inner), F32)
    du[HALO + rows :, :] = jnp.zeros((HALO, inner), F32)
    dsu[...] = jnp.zeros_like(dsu)

    b = 2 * blocks
    total_x = jnp.zeros((8, LANES), F32)
    for j in range(shares):
        here = slice(j * cols, (j + 1) * cols)
        kf, kb = keeps[0, :, here], keeps[1, :, here]
        now_b, now_f = incoming(
            ids, cfg, (r1, r2, r3), j,
            (kb[b : b + 1, :], kb[b + 1 : b + 2, :]), (kf[b + 2 : b + 3, :], kf[b + 3 : b + 4, :]),
        )
        for d, order, now, kept in (
            (0, list(reversed(range(blocks))), now_f, kf),
            (1, list(range(blocks)), now_b, kb),
        ):
            part = slice(d * ns, (d + 1) * ns)
            rows_x = [None] * blocks
            for c in order:
                dstate[c, part, here] = now.astype(BF16)
                rows_x[c] = kept[c : c + 1, :] * jnp.sum(
                    enter[c, part, here].astype(F32) * now, axis=0, keepdims=True
                )
                now = kept[c : c + 1, :] * now + dlocal[c, part, here].astype(F32)
            rows_x = jnp.concatenate(rows_x + [jnp.zeros((8 - blocks, cols), F32)], axis=0)
            total_x = total_x + mm_left(rows_x, spread[d, :, here], 2, NT)
    xs[...] = total_x

    def states_part(c, _):
        at = pl.ds(pl.multiple_of(c * SPAN, SPAN), SPAN)
        moved = pl.ds(pl.multiple_of(c * SPAN + HALO, HALO), SPAN)
        for d in range(2):
            held[d] = mm(bc[2 * d, at, :ns], dstate[c, d * ns : (d + 1) * ns, :])
        for p in range(pages):
            lanes = slice(p * LANES, (p + 1) * LANES)
            xv = x[at, lanes].astype(F32)
            dx = dxi[at, lanes].astype(F32)
            for d in range(2):
                wide = wide_in[d, at, lanes].astype(F32)
                through = held[d, :, lanes] * wide
                dx = dx + through
                prod[d, at, lanes] = (through * xv).astype(BF16)
                xw[d, :, lanes] = (wide * xv).astype(BF16)
            uv = u[at, lanes].astype(F32)
            sig = sigmoid(uv)
            du[moved, lanes] = dx * (sig + uv * sig * (1.0 - sig))
        for d in range(2):
            dst[2 * d, at, :] = dbc[2 * d, at, :]
            dst[2 * d, at, :ns] += mm(xw[d], dstate[c, d * ns : (d + 1) * ns, :], NT)
            dst[2 * d + 1, at, :] = dbc[2 * d + 1, at, :]
        return 0

    lax.fori_loop(0, blocks, states_part, 0)
    qs[...] = mm(prod[0], spread[0], NT) + mm(prod[1], spread[1], NT)
    parts = [(0, HALO)] + [(HALO + c * SPAN, SPAN) for c in range(blocks)]
    per_share = cols // LANES

    for p in range(pages):
        lanes = slice(p * LANES, (p + 1) * LANES)
        near = slice((p % per_share) * LANES, (p % per_share + 1) * LANES)
        sums = [jnp.zeros((8, LANES), F32) for _ in range(TAPS)]
        for start, size in parts:
            old = vext[pl.ds(start, size), lanes].astype(F32)
            dv = None
            for m in range(TAPS):
                shifted = du[pl.ds(start + TAPS - 1 - m, size), lanes]
                term = vk[m : m + 1, lanes] * shifted
                dv = term if dv is None else dv + term
                sums[m] = sums[m] + fold(old * shifted)
            dp[p // per_share, pl.ds(start, size), near] = dv.astype(BF16)
        for m in range(TAPS):
            small[m * pages + p : m * pages + p + 1, :] = jnp.sum(sums[m], axis=0, keepdims=True)
        row = cfg["gain_row"] + p
        small[row : row + 1, :] = jnp.sum(rowsum[0, :, lanes], axis=0, keepdims=True)

    lane = iota((SPAN, LANES), 1)
    is_fwd = lane % (2 * own) < own
    at0, at1 = iota((SPAN, SPAN), 0), iota((SPAN, SPAN), 1)
    both = jnp.concatenate([(at0 > at1).astype(F32), (at0 < at1).astype(F32)], axis=0).astype(BF16)
    dbias = jnp.zeros((1, LANES), F32)
    ddecay = jnp.zeros((1, LANES), F32)
    steps = []
    for c in range(blocks):
        at = chunk_rows(c)
        qv = qs[at, :]
        sums = mm_right(both, qv, 2)
        total = da[at, :] + xs[c : c + 1, :] + jnp.where(is_fwd, sums[:SPAN], sums[SPAN:])
        through = total * dec[0, at, :]
        step = (dk[at, :] + qv + through) * dec[1, at, :]
        step = jnp.where(lane < 2 * own * shares, step, 0.0)
        steps.append(step)
        dbias = dbias + jnp.sum(step, axis=0, keepdims=True)
        ddecay = ddecay + jnp.sum(through, axis=0, keepdims=True)
    base = cfg["rest_row"]
    small[base : base + 1, :] = dbias
    small[base + 1 : base + 2, :] = ddecay
    skips = mm_left(rowsum[1], spread[0], 2, NT)
    small[base + 2 : base + 3, :] = jnp.sum(skips, axis=0, keepdims=True)
    small[base + 3 : base + 8, :] = jnp.zeros((5, LANES), F32)

    for k in range(4):
        for c in range(blocks):
            at = chunk_rows(c)
            uv = su[k, at, :]
            sig = sigmoid(uv)
            dsu[k, chunk_rows(c, HALO), :] = dst[k, at, :] * sig * (1.0 + uv * (1.0 - sig))
        sums = [jnp.zeros((8, LANES), F32) for _ in range(TAPS)]
        for start, size in parts:
            old = side[k, pl.ds(start, size), :]
            dv = None
            for m in range(TAPS):
                shifted = dsu[k, pl.ds(start + TAPS - 1 - m, size), :]
                term = sk[k, m : m + 1, :] * shifted
                dv = term if dv is None else dv + term
                sums[m] = sums[m] + fold(old * shifted)
            if start >= HALO:
                moved = pltpu.roll(steps[(start - HALO) // SPAN], (ns - 2 * own * k) % LANES, 1)
                dv = dv + jnp.where((lane >= ns) & (lane < ns + 2 * own), moved, 0.0)
            dp[k, pl.ds(start, size), cols : cols + LANES] = dv.astype(BF16)
        for m in range(TAPS):
            row = cfg["state_row"] + m * 4 + k
            small[row : row + 1, :] = jnp.sum(sums[m], axis=0, keepdims=True)
    small[cfg["input_row"] :, :] = jnp.zeros_like(small[cfg["input_row"] :, :])


def last_kernel(cfg, *refs):
    ids, halo, inputs, ahead, normed_t, dp, w1, gx, small_in = refs[:9]
    gn, small = refs[9:11]
    pieces, (held, spare) = refs[11:-2], refs[-2:]
    shares, rows, width = cfg["shares"], cfg["rows"], inputs.shape[1]
    for j in range(shares):
        place = held if j % 2 else spare
        grad = mm(normed_t[...], dp[j, HALO:, :]) + mm(ahead[...], dp[j, :HALO, :], TN)
        place[...] = grad.astype(BF16)
        take_grads(ids, pieces, place, (ids[0] + shares - j) % shares, cfg["per"])
        edge = mm(dp[j, :HALO, :], w1[j], NT)
        back = mm(dp[j, HALO:, :], w1[j], NT)
        if j == 0:
            gn[:HALO, :] = edge
            gn[HALO:, :] = back + gx[...]
        else:
            gn[:HALO, :] += edge
            gn[HALO:, :] += back

    def plain(block):
        wide = block.astype(F32)
        return wide * lax.rsqrt(jnp.mean(wide * wide, axis=1, keepdims=True) + EPSILON)

    total = fold(jnp.where(ids[0] > 0, gn[0:HALO, :] * plain(halo[...]), 0.0))
    for c in range(rows // SPAN):
        total = total + fold(gn[chunk_rows(c, HALO), :] * plain(inputs[chunk_rows(c), :]))
    total = jnp.sum(total, axis=0, keepdims=True)
    small[...] = small_in[...]
    for k in range(width // LANES):
        row = cfg["input_row"] + k
        small[row : row + 1, :] = total[:, k * LANES : (k + 1) * LANES]


def finish_kernel(cfg, ids, inputs, cot, gain, gn, edge, out):
    rows = cfg["rows"]
    size = SPAN // 2
    for c in range(rows // size):
        at = pl.ds(c * size, size)
        wide = inputs[at, :].astype(F32)
        g = gn[pl.ds(HALO + c * size, size), :]
        if c == rows // size - 1:
            g = jnp.concatenate([g[: size - HALO], g[size - HALO :] + edge[...]], axis=0)
        scale = lax.rsqrt(jnp.mean(wide * wide, axis=1, keepdims=True) + EPSILON)
        f = g * gain[...]
        mean = jnp.mean(f * wide, axis=1, keepdims=True)
        grad = cot[at, :].astype(F32) + scale * f - wide * (scale * scale * scale) * mean
        out[at, :] = grad.astype(BF16)


def gather_line(pack, shares):
    return jnp.stack([pack] + [along(pack, d, shares) for d in range(1, shares)])


def gather_layer(held, groups):
    return [held] + [lax.ppermute(held, "dp", xor(groups, 2 * k)) for k in range(1, groups // 2)]


def gather_pair(near, groups):
    pieces = []
    for block in near:
        pieces += [block, lax.ppermute(block, "dp", xor(groups, 1))]
    return pieces


def gather_any(pack):
    rows = lax.all_gather(pack, "dp", axis=0, tiled=True)
    return [lax.all_gather(rows, "tensor", axis=0, tiled=False)]


def scatter_any(pieces):
    part = lax.psum_scatter(pieces[0].astype(F32), "dp", scatter_dimension=1, tiled=True)
    return lax.psum_scatter(part, "tensor", scatter_dimension=0, tiled=False)


def scatter_pair(cfg, ids, keep, send, *small):
    groups, shares, per, c = cfg["groups"], cfg["shares"], cfg["per"], keep.shape[-1]
    others = [lax.ppermute(v, "dp", xor(groups, 1)) for v in (send,) + small]
    n = groups // 2
    shapes = tuple(sds(v.shape) for v in small) + tuple(sds((shares, per, c), BF16) for _ in range(n))
    sums = [v for pair in zip(small, others[1:]) for v in pair]
    return call(functools.partial(pair_kernel, n), shapes, us=1.5)(ids, keep, others[0], *sums)


def scatter_layer(groups, pairs):
    return [pairs[0]] + [lax.ppermute(pairs[k], "dp", xor(groups, 2 * k)) for k in range(1, groups // 2)]


def layer_sum(cfg, ids, parts, first):
    shares, per, cols = (cfg[k] for k in ("shares", "per", "cols"))
    return call(
        functools.partial(quad_kernel, cfg, first),
        (sds((per, 2 * cols), BF16),) * shares,
        scratch=[pltpu.VMEM((shares, per, LANES), F32)],
        us=15.0 if first else 1.5,
    )(ids, *parts)


def scatter_line(shares, blocks):
    return [blocks[0]] + [along(blocks[d], shares - d, shares) for d in range(1, shares)]


def shards(
    inputs, gate_weight, value_weight, step_weight, shared_weight, output_weight, value_kernel,
    shared_kernel, step_bias, decay_log, skip_gain, input_gain, output_gain, cotangent,
):
    shares, groups = lax.axis_size("tensor"), lax.axis_size("dp")
    z, g = lax.axis_index("tensor"), lax.axis_index("dp")
    rows, width = inputs.shape
    per, cols = gate_weight.shape
    own = step_weight.shape[2]
    heads = own * shares
    ns = shared_weight.shape[1] // 4
    inner = cols * shares
    blocks, pages = rows // SPAN, cols // LANES
    fast = groups == 8 and per % 32 == 0
    cfg = dict(
        shares=shares, groups=groups, own=own, head=cols // own, cols=cols, rows=rows, state=ns, per=per,
        pieces=groups if fast else 1,
    )
    cfg["gain_row"] = TAPS * shares * pages
    cfg["state_row"] = cfg["gain_row"] + shares * pages
    cfg["rest_row"] = cfg["state_row"] + 4 * TAPS
    cfg["input_row"] = cfg["rest_row"] + 8
    small_rows = -(-(cfg["input_row"] + width // LANES) // 8) * 8
    ids = jnp.stack([z, g]).astype(jnp.int32)
    ext = HALO + rows
    pk = cols + LANES

    edge_rows = inputs[rows - HALO :]
    shared_own = lax.dynamic_slice_in_dim(shared_weight, z * ns, ns, 1)
    flat_step = step_weight.reshape(per, 2 * own)
    blank = jnp.zeros((per, LANES - ns - 2 * own), BF16)
    pack1 = jnp.concatenate([value_weight, shared_own, flat_step, blank], axis=1)
    pack2 = jnp.concatenate([gate_weight, output_weight.T], axis=1)

    def by_lane(v):
        v = v.reshape(-1, 2, shares, own).transpose(0, 2, 1, 3).reshape(-1, 2 * heads)
        return jnp.pad(v, ((0, 8 - v.shape[0]), (0, LANES - 2 * heads)))

    params = by_lane(
        jnp.stack([step_bias, jnp.broadcast_to(decay_log, (2, heads)), jnp.broadcast_to(skip_gain, (2, heads))])
    )
    sk = jnp.pad(
        shared_kernel.reshape(TAPS, 4, ns).transpose(1, 0, 2), ((0, 0), (0, 8 - TAPS), (0, LANES - ns))
    )
    ogain = output_gain.reshape(1, inner)
    gain = input_gain.reshape(1, width)

    if fast:
        line1 = gather_line(pack1, shares)
        pack2 = jnp.concatenate([pack2, edge_rows], axis=0)
        line2 = [pack2] + [along(after(pack2, line1), d, shares) for d in range(1, shares)]
        halo = line2[1][per:]
        line2 = jnp.stack([block[:per] for block in line2])
        near1 = gather_layer(line1, groups)
        near1, params, sk, ogain, gain, ids = lax.optimization_barrier((near1, params, sk, ogain, gain, ids))
        parts1 = gather_pair(near1, groups)
        near2 = gather_layer(after(line2, *near1), groups)
    else:
        parts1, parts2 = gather_any(pack1), gather_any(pack2)
        halo = along(edge_rows, 1, shares)

    normed, normed_t, cot_t = call(
        prep_kernel,
        (sds((rows, width), BF16), sds((width, rows), BF16), sds((width, rows), BF16)),
        us=3.0,
    )(ids, inputs, cotangent, gain)
    full = sds((rows, inner), BF16)
    (
        w1, ahead, vext, u, x, wide, side, su, bc, cct, c2, rho2, c2t, rho2t, dec, states, tots, spread,
        *pays,
    ) = call(
        functools.partial(front_kernel, cfg),
        (
            sds((shares, width, pk), BF16),
            sds((HALO, width), BF16),
            sds((ext, inner), BF16),
            full,
            full,
            sds((2, rows, inner), BF16),
            sds((shares, ext, LANES)),
            sds((4, rows, LANES)),
            sds((4, rows, LANES), BF16),
            sds((blocks, 2 * ns, 2 * SPAN), BF16),
            sds((rows, LANES)),
            sds((rows, LANES)),
            sds((blocks, LANES, SPAN)),
            sds((blocks, LANES, SPAN)),
            sds((4, rows, LANES)),
            sds((blocks, 2 * ns, inner), BF16),
            sds((2 * blocks, LANES)),
            sds((2, LANES, inner), BF16),
            *[sds((shares * ns + HALO, cols), BF16)] * 3,
        ),
        scratch=[
            pltpu.VMEM((ext, pk), F32),
            pltpu.VMEM((blocks, 2 * ns, 2 * SPAN), BF16),
            pltpu.VMEM((2 * SPAN, inner), BF16),
        ],
        us=12.0,
        limit=9 * MB,
    )(ids, halo, normed, gain, value_kernel, sk, params, *parts1)
    got = spread_out(pays, shares)

    yin = call(functools.partial(within_kernel, cfg), full, us=5.0)(
        ids, bc, c2, rho2t, x
    )
    if fast:
        parts2 = gather_pair(after(near2, yin, *got), groups)
    w2, gate, gn_out = call(
        functools.partial(gate_kernel, cfg),
        (sds((shares, width, 2 * cols), BF16), full, full),
        us=6.0,
    )(ids, normed, cotangent, *parts2)

    enter, dy, normal, dgate, dcarry, rr, dlocal, rowsum, keeps, *pays = call(
        functools.partial(middle_kernel, cfg),
        (
            sds((blocks, 2 * ns, inner), BF16),
            full,
            full,
            full,
            sds((2, rows, ns)),
            sds((rows, LANES)),
            sds((blocks, 2 * ns, inner), BF16),
            sds((2, 8, inner)),
            sds((3, HALO, inner)),
            *[sds((shares * ns, cols), BF16)] * 3,
        ),
        scratch=[
            pltpu.VMEM((2, rows, inner), BF16),
            pltpu.VMEM((SPAN, inner), F32),
            pltpu.VMEM((SPAN, inner), F32),
            pltpu.VMEM((2, SPAN, inner), F32),
            pltpu.VMEM((2 * SPAN, inner), BF16),
            pltpu.VMEM((2, rows, inner), BF16),
        ],
        us=12.0,
        limit=16 * MB,
    )(ids, yin, x, gate, gn_out, states, bc, cct, dec, tots, spread, params, ogain, *got)
    got = spread_out(pays, shares)

    def piece_shapes(c):
        if fast:
            return (sds((groups // 2, shares, per, c), BF16),) * 2
        return (sds((shares, width, c), BF16),)

    mixed, gx, *grads2 = call(
        functools.partial(output_kernel, cfg),
        (sds((rows, width), BF16), sds((rows, width))) + piece_shapes(2 * cols),
        scratch=[pltpu.VMEM((rows, width), F32)] + [pltpu.VMEM((width, 2 * cols), BF16)] * 2,
        us=7.0,
        limit=6 * MB,
    )(ids, inputs, cot_t, normed_t, normal, dgate, w2)
    dy_late = dy
    if fast:
        pairs2 = scatter_pair(cfg, ids, *grads2)
        dy_late = after(dy, pairs2)

    dxi, dbc, da, dk = call(
        functools.partial(back_within_kernel, cfg),
        (full, sds((4, rows, LANES)), sds((rows, LANES)), sds((rows, LANES))),
        scratch=[pltpu.VMEM((LANES, SPAN), F32), pltpu.VMEM((LANES, SPAN), F32)],
        us=9.0,
    )(ids, bc, rho2, c2t, x, dy_late, dcarry, rr, keeps)
    if fast:
        layer2 = scatter_layer(groups, pairs2)

    dp, small = call(
        functools.partial(tail_kernel, cfg),
        (sds((shares, ext, pk), BF16), sds((small_rows, LANES))),
        scratch=[
            pltpu.VMEM((ext + HALO, inner), F32),
            pltpu.VMEM((4, ext + HALO, LANES), F32),
            pltpu.VMEM((4, rows, LANES), F32),
            pltpu.VMEM((blocks, 2 * ns, inner), BF16),
            pltpu.VMEM((8, LANES), F32),
            pltpu.VMEM((rows, LANES), F32),
            pltpu.VMEM((2, SPAN, inner), F32),
            pltpu.VMEM((2, SPAN, inner), BF16),
            pltpu.VMEM((2, rows, inner), BF16),
        ],
        us=13.0,
        limit=17 * MB,
    )(
        ids, x, u, dxi, wide, vext, side, su, bc, dbc, dec, enter, da, dk, dlocal, rowsum, keeps, spread,
        *got, value_kernel, sk,
    )
    gn, small, *grads1 = call(
        functools.partial(last_kernel, cfg),
        (sds((ext, width)), sds((small_rows, LANES))) + piece_shapes(pk),
        scratch=[pltpu.VMEM((width, pk), BF16)] * 2,
        us=6.0,
        limit=8 * MB,
    )(ids, halo, inputs, ahead, normed_t, dp, w1, gx, small)
    first_rows = gn[:HALO]
    if fast:
        small, *pairs1 = scatter_pair(cfg, ids, *after(grads1, *layer2), small)
        blocks2 = layer_sum(cfg, ids, layer2, False)
        layer1 = scatter_layer(groups, pairs1)
        line2 = scatter_line(shares, blocks2)
        small, first_rows, line2 = after((small, first_rows, line2), layer1[1])
        grad_gate, grad_output = call(
            functools.partial(line2_kernel, cfg), (sds((per, cols)), sds((per, cols))), us=1.0
        )(ids, *line2)
        grad_value, grad_step, grad_shared = call(
            functools.partial(line_kernel, cfg),
            (sds((per, cols)), sds((per, 2 * own)), sds((per, shares * ns))),
            scratch=[pltpu.VMEM((shares, per, 2 * cols), F32)],
            us=15.0,
        )(ids, *scatter_line(shares, layer_sum(cfg, ids, layer1, True)))

        for axis, size, bits in (("dp", groups, range(1, groups.bit_length() - 1)), ("tensor", shares, range(2))):
            for bit in bits:
                small = small + lax.ppermute(small, axis, xor(size, 1 << bit))
    else:
        out1, out2 = scatter_any(grads1), scatter_any(grads2)
        grad_gate, grad_output = out2[:, :cols], out2[:, cols:]
        grad_value, grad_step = out1[:, :cols], out1[:, cols + ns : cols + ns + 2 * own]
        grad_shared = lax.all_gather(out1[:, cols : cols + ns], "tensor", axis=1, tiled=True)
        small = lax.psum(small, ("dp", "tensor"))

    edge = lax.ppermute(first_rows, "tensor", [(i + 1, i) for i in range(shares - 1)])
    grad_input = call(functools.partial(finish_kernel, cfg), sds((rows, width), BF16), us=2.0)(
        ids, inputs, cotangent, gain, gn, edge
    )

    def from_lane(v):
        return v[: 2 * heads].reshape(shares, 2, own).transpose(1, 0, 2).reshape(2, heads)

    rest = cfg["rest_row"]
    return (
        mixed,
        grad_input,
        grad_gate,
        grad_value,
        grad_step.reshape(per, 2, own),
        grad_shared,
        grad_output.T,
        small[: cfg["gain_row"]].reshape(TAPS, inner),
        small[cfg["state_row"] : rest].reshape(TAPS, 4, LANES)[:, :, :ns].reshape(TAPS, 4 * ns),
        from_lane(small[rest]),
        from_lane(small[rest + 1]).sum(axis=0),
        from_lane(small[rest + 2])[0],
        small[cfg["input_row"] : cfg["input_row"] + width // LANES].reshape(width),
        small[cfg["gain_row"] : cfg["state_row"]].reshape(inner),
    )


def solution(mesh):
    both = P(("dp", "tensor"), None)
    placed = (
        both, P("dp", "tensor"), P("dp", "tensor"), P("dp", None, "tensor"), P("dp", None),
        P("tensor", "dp"), P(), P(), P(), P(), P(), P(), P(), both,
    )
    return jax.shard_map(
        shards,
        mesh=mesh,
        in_specs=placed,
        out_specs=(
            both, both, P("dp", "tensor"), P("dp", "tensor"), P("dp", None, "tensor"), P("dp", None),
            P("tensor", "dp"), P(), P(), P(), P(), P(), P(), P(),
        ),
        check_vma=False,
    )
```

```python
import functools

import jax
import jax.numpy as jnp
from jax import lax
from jax.experimental import pallas as pl
from jax.experimental.pallas import tpu as pltpu
from jax.sharding import PartitionSpec as P

F32 = jnp.float32
BF16 = jnp.bfloat16
EPSILON = 1e-06
SPAN = 128
HALO = 16
TAPS = 4
LANES = 128
LOG2E = 1.4426950408889634
EXACT = lax.Precision.HIGHEST
LIMIT = 4 * 1024 * 1024
MB = 1024 * 1024

NN = (((1,), (0,)), ((), ()))
NT = (((1,), (1,)), ((), ()))
TN = (((0,), (0,)), ((), ()))


def mm(a, b, dims=NN, precision=None):
    return lax.dot_general(a, b, dims, preferred_element_type=F32, precision=precision)


def iota(shape, dim):
    return lax.broadcasted_iota(jnp.int32, shape, dim)


def sigmoid(v):
    return 0.5 * jnp.tanh(0.5 * v) + 0.5


def split(v, n):
    parts = []
    for _ in range(n):
        part = v.astype(BF16)
        parts.append(part)
        v = v - part.astype(F32)
    return parts


def mm_right(ones, v, n):
    total = None
    for part in split(v, n):
        term = mm(ones, part)
        total = term if total is None else total + term
    return total


def mm_left(v, ones, n, dims=(((1,), (0,)), ((), ()))):
    total = None
    for part in split(v, n):
        term = mm(part, ones, dims)
        total = term if total is None else total + term
    return total


def fold(v):
    return v.reshape(v.shape[0] // 8, 8, v.shape[1]).sum(axis=0)


def chunk_rows(c, base=0):
    return pl.ds(base + c * SPAN, SPAN)


def call(kernel, out_shape, scratch=(), us=1.0, limit=LIMIT):
    def run(*args):
        specs = [
            pl.BlockSpec(memory_space=pltpu.SMEM if i == 0 else pltpu.VMEM)
            for i in range(len(args))
        ]
        return pl.pallas_call(
            kernel,
            out_shape=out_shape,
            in_specs=specs,
            out_specs=jax.tree.map(lambda _: pl.BlockSpec(memory_space=pltpu.VMEM), out_shape),
            scratch_shapes=list(scratch),
            cost_estimate=pl.CostEstimate(
                flops=int(us * 1.1e9), bytes_accessed=int(us * 3.0e6), transcendentals=0
            ),
            compiler_params=pltpu.CompilerParams(vmem_limit_bytes=limit),
        )(*args)

    return run


def sds(shape, dtype=F32):
    return jax.ShapeDtypeStruct(shape, dtype)


def put_weights(ids, pieces, outs, shares, per):
    for rel, piece in enumerate(pieces):
        for d in range(shares):
            start = 0
            for out in outs:
                width = out.shape[1] // shares
                if len(pieces) == 1:
                    out[:, d * width : (d + 1) * width] = piece[d, :, start : start + width]
                else:
                    row = pl.multiple_of((ids[1] ^ rel) * per, per)
                    col = pl.multiple_of((ids[0] + shares - d) % shares * width, LANES)
                    out[pl.ds(row, per), pl.ds(col, width)] = piece[d, :, start : start + width]
                start += width


def take_grads(ids, pieces, held, shares, per):
    n = 2 * pieces[0].shape[0] if len(pieces) > 1 else 1
    for rel in range(n):
        for d in range(shares):
            start = 0
            for part in held:
                width = part.shape[1] // shares
                if n == 1:
                    pieces[0][d, :, start : start + width] = part[:, d * width : (d + 1) * width]
                else:
                    row = pl.multiple_of((ids[1] ^ rel) * per, per)
                    col = pl.multiple_of((ids[0] + shares - d) % shares * width, LANES)
                    pieces[rel % 2][rel // 2, d, :, start : start + width] = part[pl.ds(row, per), pl.ds(col, width)]
                start += width


def blocks_of(total, size):
    return [slice(i, min(i + size, total)) for i in range(0, total, size)]


def cyclic(size, d):
    return [(i, (i + d) % size) for i in range(size)]


def xor(size, bit):
    return [(i, i ^ bit) for i in range(size)]


def along(v, d, shares):
    return lax.ppermute(v, "tensor", cyclic(shares, d))


def spread_out(parts, shares):
    return [along(part, d + 1, shares) for d, part in enumerate(parts)]


def after(values, *others):
    out = lax.optimization_barrier((values,) + others)
    return out[0]


def pair_kernel(n, ids, keep, other, *refs):
    for k in range(n):
        refs[len(refs) - n + k][...] = (keep[k].astype(F32) + other[k].astype(F32)).astype(BF16)
    if len(refs) > n:
        mine, theirs, total = refs[:3]
        total[...] = mine[...] + theirs[...]


def quad_kernel(cfg, first, ids, *refs):
    n, shares, cols, ns = cfg["groups"] // 2, cfg["shares"], cfg["cols"], cfg["state"]
    parts, outs, held = refs[:n], refs[n:-1], refs[-1]
    for d in range(shares):
        q = (ids[0] + shares - d) % shares
        total = parts[0][d].astype(F32)
        for part in parts[1:]:
            total = total + part[d].astype(F32)
        if first:
            outs[d][:, :cols] = total[:, :cols].astype(BF16)
            held[q] = total[:, cols:]
        else:
            outs[d][...] = total.astype(BF16)
    if first:
        low = iota((outs[0].shape[0], LANES), 1) < ns
        for k in range(shares // 2):
            both = jnp.where(low, held[2 * k], pltpu.roll(held[2 * k + 1], ns, 1)).astype(BF16)
            for out in outs:
                out[:, cols + k * LANES : cols + (k + 1) * LANES] = both
        for d, out in enumerate(outs):
            step = held[(ids[0] + shares - d) % shares]
            out[:, cols + shares * ns :] = jnp.where(low, pltpu.roll(step, LANES - ns, 1), 0.0).astype(BF16)


def line_kernel(cfg, ids, *refs):
    shares, cols, ns = cfg["shares"], cfg["cols"], cfg["state"]
    parts, (value, step, shared, held) = refs[:shares], refs[shares:]
    for e, part in enumerate(parts):
        held[e] = part[...].astype(F32)
    total = held[(shares - ids[0]) % shares]
    for q in range(1, shares):
        total = total + held[(q + shares - ids[0]) % shares]
    value[...] = total[:, :cols]
    shared[...] = total[:, cols : cols + shares * ns]
    step[...] = total[:, cols + shares * ns :][:, : step.shape[1]]


def line2_kernel(cfg, ids, *refs):
    shares, cols = cfg["shares"], cfg["cols"]
    parts, (gate, out) = refs[:shares], refs[shares:]
    total = parts[0][...].astype(F32)
    for part in parts[1:]:
        total = total + part[...].astype(F32)
    gate[...] = total[:, :cols]
    out[...] = total[:, cols:]


def fill_spread(cfg, spread):
    own, head = cfg["own"], cfg["head"]
    block = own * head
    for j in range(cfg["shares"]):
        lane = iota((LANES, block), 0)
        place = iota((LANES, block), 1) // head
        for d in range(2):
            cols = slice(j * block, (j + 1) * block)
            spread[d, :, cols] = (lane == own * (2 * j + d) + place).astype(F32).astype(BF16)


def prep_kernel(cfg, ids, inputs, cot, gain, bias, decay, skip, taps, normed, normed_t, cot_t, params, sk, raw):
    own, ns = cfg["own"], cfg["state"]
    heads = own * cfg["shares"]
    size = SPAN // 2
    for c in range(inputs.shape[0] // size):
        at = pl.ds(c * size, size)
        wide = inputs[at, :].astype(F32)
        scale = lax.rsqrt(jnp.mean(wide * wide, axis=1, keepdims=True) + EPSILON)
        normed[at, :] = (wide * scale * gain[...]).astype(BF16)
    normed_t[...] = normed[...].T
    cot_t[...] = cot[...].T
    raw[...] = jnp.zeros_like(raw)
    raw[0:2, :heads] = bias[...]
    raw[2:3, :heads] = decay[...]
    raw[3:4, :heads] = skip[...]
    h, lane = iota((LANES, LANES), 0), iota((LANES, LANES), 1)
    fwd, bwd = (
        mm_left(
            raw[...],
            ((h < heads) & (lane == 2 * own * (h // own) + own * d + h % own)).astype(F32).astype(BF16),
            3,
        )
        for d in range(2)
    )
    params[...] = jnp.zeros_like(params)
    params[0:1, :] = fwd[0:1, :] + bwd[1:2, :]
    params[1:2, :] = fwd[2:3, :] + bwd[2:3, :]
    params[2:3, :] = fwd[3:4, :] + bwd[3:4, :]
    low = iota((8, LANES), 1) < ns
    for k in range(4):
        raw[...] = jnp.zeros_like(raw)
        raw[0:TAPS, :] = taps[:, k // 2 * LANES : (k // 2 + 1) * LANES]
        v = raw[...]
        sk[k] = jnp.where(low, pltpu.roll(v, LANES - ns, 1) if k % 2 else v, 0.0)


def small_kernel(cfg, ids, mine, theirs, vkernel, skernel, bias, decay, skip, ingain, outgain, held):
    own, ns, shares = cfg["own"], cfg["state"], cfg["shares"]
    heads = own * shares
    held[...] = mine[...] + theirs[...]
    n = outgain.shape[1] // LANES
    for k in range(n):
        lanes = slice(k * LANES, (k + 1) * LANES)
        for m in range(TAPS):
            vkernel[m : m + 1, lanes] = held[m * n + k : m * n + k + 1, :]
        outgain[:, lanes] = held[cfg["gain_row"] + k : cfg["gain_row"] + k + 1, :]
    for k in range(ingain.shape[1] // LANES):
        row = cfg["input_row"] + k
        ingain[:, k * LANES : (k + 1) * LANES] = held[row : row + 1, :]
    low = iota((1, LANES), 1) < ns
    for m in range(TAPS):
        for k in range(2):
            row = cfg["state_row"] + 4 * m + 2 * k
            both = held[row : row + 2, :]
            odd = jnp.concatenate([both] * 4, axis=0)
            odd = pltpu.roll(odd, ns, 1)[1:2, :]
            skernel[m : m + 1, k * LANES : (k + 1) * LANES] = jnp.where(low, both[0:1, :], odd)
    rest = held[cfg["rest_row"] : cfg["rest_row"] + 8, :]
    lane, h = iota((LANES, LANES), 0), iota((LANES, LANES), 1)
    fwd, bwd = (
        mm_left(
            rest,
            ((h < heads) & (lane == 2 * own * (h // own) + own * d + h % own)).astype(F32).astype(BF16),
            3,
        )
        for d in range(2)
    )
    bias[0:1, :] = fwd[0:1, :heads]
    bias[1:2, :] = bwd[0:1, :heads]
    decay[...] = fwd[1:2, :heads] + bwd[1:2, :heads]
    skip[...] = fwd[2:3, :heads]


def front_kernel(cfg, *refs):
    n = cfg["pieces"]
    ids, halo, normed, gain, vk, sk, params = refs[:7]
    pieces = refs[7 : 7 + n]
    (
        w1, ws, ahead, vext, u_out, x_out, wide_out, side, su_out, bc_out, cct, c2, rho2, c2t, rho2t, dec, states,
        tots, spread, pay1, pay2, pay3, acc, bbt, xw,
    ) = refs[7 + n :]
    shares, own, cols, rows, ns = (cfg[k] for k in ("shares", "own", "cols", "rows", "state"))
    blocks, pages = rows // SPAN, cols // LANES
    put_weights(ids, pieces, (w1, ws), shares, cfg["per"])
    fill_spread(cfg, spread)

    edge = halo[...].astype(F32)
    scale = lax.rsqrt(jnp.mean(edge * edge, axis=1, keepdims=True) + EPSILON)
    ahead[...] = jnp.where(ids[0] > 0, edge * scale * gain[...], 0.0).astype(BF16)
    bbt[...] = jnp.zeros_like(bbt)
    cct[...] = jnp.zeros_like(cct)

    for part in blocks_of(shares * cols, 512):
        acc[0:HALO, part] = mm(ahead[...], w1[:, part])
        acc[HALO:, part] = mm(normed[...], w1[:, part])
    sides, edge = mm(normed[...], ws[...]), mm(ahead[...], ws[...])
    for j in range(shares):
        side[j, :HALO, :] = edge[:, j * LANES : (j + 1) * LANES]
        side[j, HALO:, :] = sides[:, j * LANES : (j + 1) * LANES]
    for j in range(shares):
        here = slice(j * cols, (j + 1) * cols)
        for c in range(blocks):
            vext[chunk_rows(c), here] = acc[chunk_rows(c), here].astype(BF16)
        vext[blocks * SPAN :, here] = acc[blocks * SPAN :, here].astype(BF16)
        for c in range(blocks):
            for p in range(pages + 1):
                here = slice(j * cols + p * LANES, j * cols + (p + 1) * LANES)
                u = None
                for m in range(TAPS):
                    rows_m = chunk_rows(c, HALO - TAPS + 1 + m)
                    if p < pages:
                        term = vk[m : m + 1, here] * acc[rows_m, here]
                    else:
                        term = sk[j, m : m + 1, :] * side[j, rows_m, :]
                    u = term if u is None else u + term
                v = u * sigmoid(u)
                if p < pages:
                    u_out[chunk_rows(c), here] = u.astype(BF16)
                    x_out[chunk_rows(c), here] = v.astype(BF16)
                else:
                    su_out[j, chunk_rows(c), :] = u
                    bc_out[j, chunk_rows(c), :] = v.astype(BF16)
                    turned = v.T[:ns].astype(BF16)
                    d = j // 2
                    target = cct if j % 2 else bbt
                    target[c, d * ns : (d + 1) * ns, d * SPAN : (d + 1) * SPAN] = turned

    lane = iota((SPAN, LANES), 1)
    is_fwd = lane % (2 * own) < own
    at0, at1 = iota((SPAN, SPAN), 0), iota((SPAN, SPAN), 1)
    both = jnp.concatenate([(at0 >= at1).astype(F32), (at0 <= at1).astype(F32)], axis=0).astype(BF16)
    rate = jnp.where(iota((1, LANES), 1) < 2 * own * shares, -jnp.exp(params[1:2, :]), 0.0)
    for c in range(blocks):
        raw = jnp.zeros((SPAN, LANES), F32)
        for j in range(shares):
            moved = pltpu.roll(side[j, chunk_rows(c, HALO), :], (2 * own * j - ns) % LANES, 1)
            raw = jnp.where((lane >= 2 * own * j) & (lane < 2 * own * (j + 1)), moved, raw)
        v = raw + params[0:1, :]
        small = jnp.exp(jnp.minimum(v, 0.0))
        dt = jnp.where(v < -15.0, small, jnp.maximum(v, 0.0) + jnp.log1p(jnp.exp(-jnp.abs(v))))
        log_dt = jnp.where(v < -15.0, v, jnp.log(jnp.maximum(dt, 1e-30)))
        ratio = jnp.where(v < -15.0, 1.0, sigmoid(v) / jnp.maximum(dt, 1e-30))
        a = dt * rate
        sums = mm_right(both, a, 3)
        cum = jnp.where(is_fwd, sums[:SPAN], sums[SPAN:])
        tot = jnp.sum(a, axis=0, keepdims=True)
        rho = cum - log_dt
        cc = cum * LOG2E
        rr = rho * LOG2E
        c2[chunk_rows(c), :] = cc
        rho2[chunk_rows(c), :] = rr
        c2t[c] = cc.T
        rho2t[c] = rr.T
        dec[0, chunk_rows(c), :] = a
        dec[1, chunk_rows(c), :] = ratio
        dec[2, chunk_rows(c), :] = jnp.exp(tot - rho)
        dec[3, chunk_rows(c), :] = jnp.exp(cum)
        tots[c : c + 1, :] = tot
    fwd1 = iota((1, LANES), 1) % (2 * own) < own
    zero = jnp.zeros((1, LANES), F32)
    lead = []
    for c in range(blocks):
        later, sooner = zero, zero
        for k in range(blocks):
            if k > c:
                later = later + tots[k : k + 1, :]
            if k < c:
                sooner = sooner + tots[k : k + 1, :]
        lead.append(jnp.exp(jnp.where(fwd1, later, sooner)))
        tots[blocks + c : blocks + c + 1, :] = jnp.where(fwd1, sooner, later)
    lead = jnp.concatenate(lead + [zero] * (8 - blocks), axis=0)
    whole = tots[0:1, :]
    for c in range(1, blocks):
        whole = whole + tots[c : c + 1, :]
    extra = jnp.concatenate([p.astype(F32) for p in split(whole, 3)] + [zero] * (HALO - 3), axis=0)
    extra = jnp.concatenate([extra, jnp.zeros((HALO, cols - LANES), F32)], axis=1).astype(BF16)
    for pay in (pay1, pay2, pay3):
        pay[shares * ns :, :] = extra

    weights = dec[2].astype(BF16)
    for d in range(2):
        wide_out[d] = mm(weights, spread[d]).astype(BF16)
    grow_f, grow_b = mm_left(lead, spread[0], 2), mm_left(lead, spread[1], 2)
    for c in range(blocks):
        for d in range(2):
            for p in range(shares * pages):
                lanes = slice(p * LANES, (p + 1) * LANES)
                product = wide_out[d, chunk_rows(c), lanes].astype(F32) * x_out[chunk_rows(c), lanes].astype(F32)
                xw[d * SPAN : (d + 1) * SPAN, lanes] = product.astype(BF16)
        states[c] = mm(bbt[c], xw[...]).astype(BF16)
    for j in range(shares):
        at = slice(j * ns, (j + 1) * ns)
        here = slice(j * cols, (j + 1) * cols)
        f, b = jnp.zeros((ns, cols), F32), jnp.zeros((ns, cols), F32)
        for c in range(blocks):
            f = f + grow_f[c : c + 1, here] * states[c, :ns, here].astype(F32)
            b = b + grow_b[c : c + 1, here] * states[c, ns:, here].astype(F32)
        for dist, pay in ((1, pay1), (2, pay2), (3, pay3)):
            pay[at, :] = jnp.where(ids[0] + dist < shares, f, b).astype(BF16)


def stack_pair(first, v):
    zero = jnp.zeros_like(v)
    return jnp.concatenate([jnp.where(first, v, zero), jnp.where(first, zero, v)], axis=0)


def within_kernel(cfg, ids, bc, c2, rho2t, x, y):
    shares, own, rows = (cfg[k] for k in ("shares", "own", "rows"))
    t, s = iota((SPAN, SPAN), 0), iota((SPAN, SPAN), 1)
    low = t > s
    first = iota((SPAN, LANES), 1) < cfg["head"]

    def block(c, _):
        at = pl.ds(pl.multiple_of(c * SPAN, SPAN), SPAN)
        g = jnp.where(low, mm(bc[1, at, :], bc[0, at, :], NT), mm(bc[3, at, :], bc[2, at, :], NT))
        g = jnp.where(t == s, 0.0, g)
        cc = c2[at, :]
        for k in range(shares * own // 2):
            j, p = k // (own // 2), k % (own // 2)
            mats = []
            for i in (2 * p, 2 * p + 1):
                f, b = 2 * own * j + i, 2 * own * j + own + i
                col = jnp.where(low, cc[:, f : f + 1], cc[:, b : b + 1])
                row = jnp.where(low, rho2t[c, f : f + 1, :], rho2t[c, b : b + 1, :])
                mats.append((jnp.exp2(col - row) * g).astype(BF16))
            lanes = slice(k * LANES, (k + 1) * LANES)
            y[at, lanes] = mm(jnp.concatenate(mats, axis=1), stack_pair(first, x[at, lanes])).astype(BF16)
        return 0

    lax.fori_loop(0, rows // SPAN, block, 0)


def gate_kernel(cfg, *refs):
    n = cfg["pieces"]
    ids, normed, cot = refs[:3]
    pieces = refs[3 : 3 + n]
    wg, wo, gate, gn = refs[3 + n :]
    put_weights(ids, pieces, (wg, wo), cfg["shares"], cfg["per"])
    for part in blocks_of(gate.shape[1], 512):
        gate[:, part] = mm(normed[...], wg[:, part]).astype(BF16)
        gn[:, part] = mm(cot[...], wo[:, part]).astype(BF16)


def incoming(ids, cfg, got, j, near, far):
    z, shares, ns = ids[0], cfg["shares"], cfg["state"]
    r1, r2, r3 = (part[j * ns : (j + 1) * ns, :].astype(F32) for part in got)

    def keep(test, v):
        return jnp.where(test, v, 0.0)

    before = keep(z >= 1, r1) + near[0] * keep(z >= 2, r2) + near[1] * keep(z >= 3, r3)
    behind = (
        keep(z <= shares - 2, r3)
        + far[0] * keep(z <= shares - 3, r2)
        + far[1] * keep(z <= shares - 4, r1)
    )
    return before, behind


def middle_kernel(cfg, *refs):
    (
        ids, yin, x, gate, gn, states, bc, cct, dec, tots, spread, params, ogain, r1, r2, r3,
        enter, dy, normal, dgate, dcarry, rr, dlocal, rowsum, keeps, p1, p2, p3,
        ecx, ys, acts, kept, edy, prod,
    ) = refs
    shares, cols, rows, ns = (cfg[k] for k in ("shares", "cols", "rows", "state"))
    blocks, inner = rows // SPAN, cols * shares
    pages = inner // LANES
    zero = jnp.zeros((1, LANES), F32)

    def whole(r):
        v = r[shares * ns :, :LANES].astype(F32)
        return v[0:1, :] + v[1:2, :] + v[2:3, :]

    l1, l2, l3 = whole(r1), whole(r2), whole(r3)
    lines = [tots[c : c + 1, :] for c in range(2 * blocks)] + [l1, l1 + l2, l3, l3 + l2]
    lines = jnp.exp(jnp.concatenate(lines + [zero] * (HALO - len(lines)), axis=0))
    skip_rows = jnp.concatenate([params[2:3, :]] + [zero] * 7, axis=0)
    for d in range(2):
        keeps[d] = mm_left(lines, spread[d], 2)
        ecx[d] = mm(dec[3].astype(BF16), spread[d]).astype(BF16)
    keeps[2, 0:8] = mm_left(skip_rows, spread[0], 2)
    b = 2 * blocks
    for j in range(shares):
        here = slice(j * cols, (j + 1) * cols)
        kf, kb = keeps[0, :, here], keeps[1, :, here]
        e, e_b = incoming(
            ids, cfg, (r1, r2, r3), j,
            (kf[b : b + 1, :], kf[b + 1 : b + 2, :]), (kb[b + 2 : b + 3, :], kb[b + 3 : b + 4, :]),
        )
        for c in range(blocks):
            enter[c, :ns, here] = e.astype(BF16)
            e = kf[c : c + 1, :] * e + states[c, :ns, here].astype(F32)
        for c in reversed(range(blocks)):
            enter[c, ns:, here] = e_b.astype(BF16)
            e_b = kb[c : c + 1, :] * e_b + states[c, ns:, here].astype(F32)
    rowsum[...] = jnp.zeros_like(rowsum)

    def block(c, _):
        at = pl.ds(pl.multiple_of(c * SPAN, SPAN), SPAN)
        for d in range(2):
            kept[d] = mm(bc[1 + 2 * d, at, :ns], enter[c, d * ns : (d + 1) * ns, :])
        square, dot = jnp.zeros((SPAN, LANES), F32), jnp.zeros((SPAN, LANES), F32)
        for p in range(pages):
            lanes = slice(p * LANES, (p + 1) * LANES)
            cf = kept[0, :, lanes] * ecx[0, at, lanes].astype(F32)
            cb = kept[1, :, lanes] * ecx[1, at, lanes].astype(F32)
            kept[0, :, lanes] = cf
            kept[1, :, lanes] = cb
            v = yin[at, lanes].astype(F32) + keeps[2, 0:1, lanes] * x[at, lanes].astype(F32) + cf + cb
            ys[:, lanes] = v
            g = gate[at, lanes].astype(F32)
            act = g * sigmoid(g)
            acts[:, lanes] = act
            gated = v * act
            square = square + gated * gated
            dot = dot + gn[at, lanes].astype(F32) * ogain[:, lanes] * gated
        square = jnp.sum(square, axis=1, keepdims=True)
        dot = jnp.sum(dot, axis=1, keepdims=True)
        inv = lax.rsqrt(square / inner + EPSILON)
        back = inv * inv * inv * dot / inner
        for p in range(pages):
            lanes = slice(p * LANES, (p + 1) * LANES)
            v, act, g = ys[:, lanes], acts[:, lanes], gate[at, lanes].astype(F32)
            gnv, og = gn[at, lanes].astype(F32), ogain[:, lanes]
            sig = sigmoid(g)
            gated = v * act
            scaled = gated * inv
            normal[at, lanes] = (scaled * og).astype(BF16)
            rowsum[0, :, lanes] += fold(gnv * scaled)
            dgated = inv * (gnv * og) - gated * back
            d_scan = dgated * act
            dy[at, lanes] = d_scan.astype(BF16)
            dgate[at, lanes] = (dgated * v * (sig + act * (1.0 - sig))).astype(BF16)
            rowsum[1, :, lanes] += fold(d_scan * x[at, lanes].astype(F32))
            for d in range(2):
                prod[d, at, lanes] = (d_scan * kept[d, :, lanes]).astype(BF16)
                wide = ecx[d, at, lanes].astype(F32) * d_scan
                edy[d * SPAN : (d + 1) * SPAN, lanes] = wide.astype(BF16)
        dlocal[c] = mm(cct[c], edy[...]).astype(BF16)
        for d in range(2):
            dcarry[d, at, :] = mm(edy[d * SPAN : (d + 1) * SPAN, :], enter[c, d * ns : (d + 1) * ns, :], NT)
        return 0

    lax.fori_loop(0, blocks, block, 0)
    rr[...] = mm(prod[0], spread[0], NT) + mm(prod[1], spread[1], NT)

    for j in range(shares):
        here = slice(j * cols, (j + 1) * cols)
        f, b_ = jnp.zeros((ns, cols), F32), jnp.zeros((ns, cols), F32)
        for c in range(blocks):
            f = f + keeps[0, blocks + c : blocks + c + 1, here] * dlocal[c, :ns, here].astype(F32)
            b_ = b_ + keeps[1, blocks + c : blocks + c + 1, here] * dlocal[c, ns:, here].astype(F32)
        for dist, pay in ((1, p1), (2, p2), (3, p3)):
            pay[j * ns : (j + 1) * ns, :] = jnp.where(ids[0] + dist < shares, b_, f).astype(BF16)


def output_kernel(cfg, *refs):
    ids, inputs, cot_t, normed_t, normal, dgate, wg, wo = refs[:8]
    mixed, gx = refs[8:10]
    pieces, held = refs[10:-2], refs[-2:]
    for part in blocks_of(normal.shape[1], 512):
        held[0][:, part] = mm(normed_t[...], dgate[:, part]).astype(BF16)
        held[1][:, part] = mm(cot_t[...], normal[:, part]).astype(BF16)
    take_grads(ids, pieces, held, cfg["shares"], cfg["per"])
    for part in blocks_of(inputs.shape[1], 256):
        mixed[:, part] = (mm(normal[...], wo[part, :], NT) + inputs[:, part].astype(F32)).astype(BF16)
        gx[:, part] = mm(dgate[...], wg[part, :], NT)


def back_within_kernel(cfg, ids, bc, rho2, c2t, x, dy, dcarry, rr, keeps, dx, dbc, da, dk, das, ras):
    shares, own, rows, ns = (cfg[k] for k in ("shares", "own", "rows", "state"))
    s, t = iota((SPAN, SPAN), 0), iota((SPAN, SPAN), 1)
    up = t > s
    first = iota((SPAN, LANES), 1) < cfg["head"]
    after_t = (s >= t).astype(F32).astype(BF16)
    until_t = (s <= t).astype(F32).astype(BF16)
    tri = jnp.concatenate([after_t, until_t], axis=1)
    sums = jnp.concatenate([until_t, after_t], axis=0)
    lane = iota((SPAN, LANES), 1)
    is_fwd = iota((LANES, SPAN), 0) % (2 * own) < own

    def block(c, _):
        at = pl.ds(pl.multiple_of(c * SPAN, SPAN), SPAN)
        g = jnp.where(up, mm(bc[0, at, :], bc[1, at, :], NT), mm(bc[2, at, :], bc[3, at, :], NT))
        g = jnp.where(t == s, 0.0, g)
        rho = rho2[at, :]
        dg = jnp.zeros((SPAN, SPAN), F32)
        das[...] = jnp.zeros_like(das)
        ras[...] = jnp.zeros_like(ras)
        for k in range(shares * own // 2):
            j, p = k // (own // 2), k % (own // 2)
            lanes = slice(k * LANES, (k + 1) * LANES)
            dyp = dy[at, lanes]
            dm = mm(stack_pair(first, x[at, lanes]), dyp, NT)
            ws, zs = [], []
            for q in range(2):
                i = 2 * p + q
                f, b = 2 * own * j + i, 2 * own * j + own + i
                row = jnp.where(up, c2t[c, f : f + 1, :], c2t[c, b : b + 1, :])
                col = jnp.where(up, rho[:, f : f + 1], rho[:, b : b + 1])
                pw = jnp.exp2(row - col)
                ud = dm[q * SPAN : (q + 1) * SPAN] * pw
                dg = dg + ud
                ws.append((pw * g).astype(BF16))
                zd = ud * g
                zs.append(zd.astype(BF16))
                rf = jnp.sum(jnp.where(up, zd, 0.0), axis=0, keepdims=True)
                ras[f : f + 1, :] = rf
                ras[b : b + 1, :] = jnp.sum(zd, axis=0, keepdims=True) - rf
            back = mm(jnp.concatenate(ws, axis=1), stack_pair(first, dyp))
            dx[at, lanes] = (back + keeps[2, 0:1, lanes] * dyp.astype(F32)).astype(BF16)
            cross = mm(jnp.concatenate(zs, axis=0), tri)
            for q in range(2):
                i = 2 * p + q
                f, b = 2 * own * j + i, 2 * own * j + own + i
                part = cross[q * SPAN : (q + 1) * SPAN]
                das[f : f + 1, :] = jnp.sum(jnp.where(up, part[:, :SPAN], 0.0), axis=0, keepdims=True)
                das[b : b + 1, :] = jnp.sum(jnp.where(t < s, part[:, SPAN:], 0.0), axis=0, keepdims=True)
        df = jnp.where(up, dg, 0.0)
        db = jnp.where(t < s, dg, 0.0)
        dbc[0, at, :] = mm(df.astype(BF16), bc[1, at, :])
        dbc[1, at, :] = mm(df.T.astype(BF16), bc[0, at, :])
        dbc[2, at, :] = mm(db.astype(BF16), bc[3, at, :])
        dbc[3, at, :] = mm(db.T.astype(BF16), bc[2, at, :])
        dbc[1, at, :ns] += dcarry[0, at, :]
        dbc[3, at, :ns] += dcarry[1, at, :]
        a = das[...]
        later = jnp.where(lane < SPAN - 1, pltpu.roll(a, SPAN - 1, 1), 0.0)
        sooner = jnp.where(lane > 0, pltpu.roll(a, 1, 1), 0.0)
        kd = ras[...] - a + jnp.where(is_fwd, later, sooner)
        through = mm_right(sums, rr[at, :], 2)
        da[at, :] = a.T + jnp.where(lane % (2 * own) < own, through[:SPAN], through[SPAN:])
        dk[at, :] = kd.T
        return 0

    lax.fori_loop(0, rows // SPAN, block, 0)


def tail_kernel(cfg, *refs):
    (
        ids, x, u, dxi, wide_in, vext, side, su, bc, dbc, dec, enter, da, dk, dlocal, rowsum, keeps, spread,
        r1, r2, r3, vk, sk,
        dp, dps, small,
        du, dsu, dst, dstate, xs, qs, held, xw, prod,
    ) = refs
    shares, own, cols, rows, ns = (cfg[k] for k in ("shares", "own", "cols", "rows", "state"))
    blocks, inner = rows // SPAN, cols * shares
    pages = inner // LANES

    du[0:HALO, :] = jnp.zeros((HALO, inner), F32)
    du[HALO + rows :, :] = jnp.zeros((HALO, inner), F32)
    dsu[...] = jnp.zeros_like(dsu)

    b = 2 * blocks
    total_x = jnp.zeros((8, LANES), F32)
    for j in range(shares):
        here = slice(j * cols, (j + 1) * cols)
        kf, kb = keeps[0, :, here], keeps[1, :, here]
        now_b, now_f = incoming(
            ids, cfg, (r1, r2, r3), j,
            (kb[b : b + 1, :], kb[b + 1 : b + 2, :]), (kf[b + 2 : b + 3, :], kf[b + 3 : b + 4, :]),
        )
        for d, order, now, kept in (
            (0, list(reversed(range(blocks))), now_f, kf),
            (1, list(range(blocks)), now_b, kb),
        ):
            part = slice(d * ns, (d + 1) * ns)
            rows_x = [None] * blocks
            for c in order:
                dstate[c, part, here] = now.astype(BF16)
                rows_x[c] = kept[c : c + 1, :] * jnp.sum(
                    enter[c, part, here].astype(F32) * now, axis=0, keepdims=True
                )
                now = kept[c : c + 1, :] * now + dlocal[c, part, here].astype(F32)
            rows_x = jnp.concatenate(rows_x + [jnp.zeros((8 - blocks, cols), F32)], axis=0)
            total_x = total_x + mm_left(rows_x, spread[d, :, here], 2, NT)
    xs[...] = total_x

    def states_part(c, _):
        at = pl.ds(pl.multiple_of(c * SPAN, SPAN), SPAN)
        moved = pl.ds(pl.multiple_of(c * SPAN + HALO, HALO), SPAN)
        for d in range(2):
            held[d] = mm(bc[2 * d, at, :ns], dstate[c, d * ns : (d + 1) * ns, :])
        for p in range(pages):
            lanes = slice(p * LANES, (p + 1) * LANES)
            xv = x[at, lanes].astype(F32)
            dx = dxi[at, lanes].astype(F32)
            for d in range(2):
                wide = wide_in[d, at, lanes].astype(F32)
                through = held[d, :, lanes] * wide
                dx = dx + through
                prod[d, at, lanes] = (through * xv).astype(BF16)
                xw[d, :, lanes] = (wide * xv).astype(BF16)
            uv = u[at, lanes].astype(F32)
            sig = sigmoid(uv)
            du[moved, lanes] = dx * (sig + uv * sig * (1.0 - sig))
        for d in range(2):
            dst[2 * d, at, :] = dbc[2 * d, at, :]
            dst[2 * d, at, :ns] += mm(xw[d], dstate[c, d * ns : (d + 1) * ns, :], NT)
            dst[2 * d + 1, at, :] = dbc[2 * d + 1, at, :]
        return 0

    lax.fori_loop(0, blocks, states_part, 0)
    qs[...] = mm(prod[0], spread[0], NT) + mm(prod[1], spread[1], NT)
    parts = [(0, HALO)] + [(HALO + c * SPAN, SPAN) for c in range(blocks)]

    for p in range(pages):
        lanes = slice(p * LANES, (p + 1) * LANES)
        sums = [jnp.zeros((8, LANES), F32) for _ in range(TAPS)]
        for start, size in parts:
            old = vext[pl.ds(start, size), lanes].astype(F32)
            dv = None
            for m in range(TAPS):
                shifted = du[pl.ds(start + TAPS - 1 - m, size), lanes]
                term = vk[m : m + 1, lanes] * shifted
                dv = term if dv is None else dv + term
                sums[m] = sums[m] + fold(old * shifted)
            dp[pl.ds(start, size), lanes] = dv.astype(BF16)
        for m in range(TAPS):
            small[m * pages + p : m * pages + p + 1, :] = jnp.sum(sums[m], axis=0, keepdims=True)
        row = cfg["gain_row"] + p
        small[row : row + 1, :] = jnp.sum(rowsum[0, :, lanes], axis=0, keepdims=True)

    lane = iota((SPAN, LANES), 1)
    is_fwd = lane % (2 * own) < own
    at0, at1 = iota((SPAN, SPAN), 0), iota((SPAN, SPAN), 1)
    both = jnp.concatenate([(at0 > at1).astype(F32), (at0 < at1).astype(F32)], axis=0).astype(BF16)
    dbias = jnp.zeros((1, LANES), F32)
    ddecay = jnp.zeros((1, LANES), F32)
    steps = []
    for c in range(blocks):
        at = chunk_rows(c)
        qv = qs[at, :]
        sums = mm_right(both, qv, 2)
        total = da[at, :] + xs[c : c + 1, :] + jnp.where(is_fwd, sums[:SPAN], sums[SPAN:])
        through = total * dec[0, at, :]
        step = (dk[at, :] + qv + through) * dec[1, at, :]
        step = jnp.where(lane < 2 * own * shares, step, 0.0)
        steps.append(step)
        dbias = dbias + jnp.sum(step, axis=0, keepdims=True)
        ddecay = ddecay + jnp.sum(through, axis=0, keepdims=True)
    base = cfg["rest_row"]
    small[base : base + 1, :] = dbias
    small[base + 1 : base + 2, :] = ddecay
    skips = mm_left(rowsum[1], spread[0], 2, NT)
    small[base + 2 : base + 3, :] = jnp.sum(skips, axis=0, keepdims=True)
    small[base + 3 : base + 8, :] = jnp.zeros((5, LANES), F32)

    for k in range(4):
        for c in range(blocks):
            at = chunk_rows(c)
            uv = su[k, at, :]
            sig = sigmoid(uv)
            dsu[k, chunk_rows(c, HALO), :] = dst[k, at, :] * sig * (1.0 + uv * (1.0 - sig))
        sums = [jnp.zeros((8, LANES), F32) for _ in range(TAPS)]
        for start, size in parts:
            old = side[k, pl.ds(start, size), :]
            dv = None
            for m in range(TAPS):
                shifted = dsu[k, pl.ds(start + TAPS - 1 - m, size), :]
                term = sk[k, m : m + 1, :] * shifted
                dv = term if dv is None else dv + term
                sums[m] = sums[m] + fold(old * shifted)
            if start >= HALO:
                moved = pltpu.roll(steps[(start - HALO) // SPAN], (ns - 2 * own * k) % LANES, 1)
                dv = dv + jnp.where((lane >= ns) & (lane < ns + 2 * own), moved, 0.0)
            dps[pl.ds(start, size), k * LANES : (k + 1) * LANES] = dv.astype(BF16)
        for m in range(TAPS):
            row = cfg["state_row"] + m * 4 + k
            small[row : row + 1, :] = jnp.sum(sums[m], axis=0, keepdims=True)
    small[cfg["input_row"] :, :] = jnp.zeros_like(small[cfg["input_row"] :, :])


def last_kernel(cfg, *refs):
    ids, halo, inputs, ahead, normed_t, dp, dps, w1, ws, gx, small_in = refs[:11]
    gn, small = refs[11:13]
    pieces, held = refs[13:-2], refs[-2:]
    shares, rows, width = cfg["shares"], cfg["rows"], inputs.shape[1]
    for grad, out in ((dp, held[0]), (dps, held[1])):
        for part in blocks_of(grad.shape[1], 512):
            total = mm(normed_t[...], grad[HALO:, part]) + mm(ahead[...], grad[:HALO, part], TN)
            out[:, part] = total.astype(BF16)
    take_grads(ids, pieces, held, shares, cfg["per"])
    for part in blocks_of(width, 256):
        gn[:HALO, part] = mm(dp[:HALO, :], w1[part, :], NT) + mm(dps[:HALO, :], ws[part, :], NT)
        back = mm(dp[HALO:, :], w1[part, :], NT) + mm(dps[HALO:, :], ws[part, :], NT)
        gn[HALO:, part] = back + gx[:, part]

    def plain(block):
        wide = block.astype(F32)
        return wide * lax.rsqrt(jnp.mean(wide * wide, axis=1, keepdims=True) + EPSILON)

    total = fold(jnp.where(ids[0] > 0, gn[0:HALO, :] * plain(halo[...]), 0.0))
    for c in range(rows // SPAN):
        total = total + fold(gn[chunk_rows(c, HALO), :] * plain(inputs[chunk_rows(c), :]))
    total = jnp.sum(total, axis=0, keepdims=True)
    small[...] = small_in[...]
    for k in range(width // LANES):
        row = cfg["input_row"] + k
        small[row : row + 1, :] = total[:, k * LANES : (k + 1) * LANES]


def finish_kernel(cfg, ids, inputs, cot, gain, gn, edge, out):
    rows = cfg["rows"]
    size = SPAN // 2
    for c in range(rows // size):
        at = pl.ds(c * size, size)
        wide = inputs[at, :].astype(F32)
        g = gn[pl.ds(HALO + c * size, size), :]
        if c == rows // size - 1:
            g = jnp.concatenate([g[: size - HALO], g[size - HALO :] + edge[...]], axis=0)
        scale = lax.rsqrt(jnp.mean(wide * wide, axis=1, keepdims=True) + EPSILON)
        f = g * gain[...]
        mean = jnp.mean(f * wide, axis=1, keepdims=True)
        grad = cot[at, :].astype(F32) + scale * f - wide * (scale * scale * scale) * mean
        out[at, :] = grad.astype(BF16)


def gather_line(pack, shares):
    return jnp.stack([pack] + [along(pack, d, shares) for d in range(1, shares)])


def gather_layer(held, groups):
    return [held] + [lax.ppermute(held, "dp", xor(groups, 2 * k)) for k in range(1, groups // 2)]


def gather_pair(near, groups):
    pieces = []
    for block in near:
        pieces += [block, lax.ppermute(block, "dp", xor(groups, 1))]
    return pieces


def gather_any(pack):
    rows = lax.all_gather(pack, "dp", axis=0, tiled=True)
    return [lax.all_gather(rows, "tensor", axis=0, tiled=False)]


def scatter_any(pieces):
    part = lax.psum_scatter(pieces[0].astype(F32), "dp", scatter_dimension=1, tiled=True)
    return lax.psum_scatter(part, "tensor", scatter_dimension=0, tiled=False)


def scatter_pair(cfg, ids, keep, send, *small):
    groups, shares, per, c = cfg["groups"], cfg["shares"], cfg["per"], keep.shape[-1]
    others = [lax.ppermute(v, "dp", xor(groups, 1)) for v in (send,) + small]
    n = groups // 2
    shapes = tuple(sds(v.shape) for v in small) + tuple(sds((shares, per, c), BF16) for _ in range(n))
    sums = [v for pair in zip(small, others[1:]) for v in pair]
    return call(functools.partial(pair_kernel, n), shapes, us=1.5)(ids, keep, others[0], *sums)


def scatter_layer(groups, pairs):
    return [pairs[0]] + [lax.ppermute(pairs[k], "dp", xor(groups, 2 * k)) for k in range(1, groups // 2)]


def layer_sum(cfg, ids, parts, first):
    shares, per, cols = (cfg[k] for k in ("shares", "per", "cols"))
    return call(
        functools.partial(quad_kernel, cfg, first),
        (sds((per, 2 * cols), BF16),) * shares,
        scratch=[pltpu.VMEM((shares, per, LANES), F32)],
        us=15.0 if first else 1.5,
    )(ids, *parts)


def scatter_line(shares, blocks):
    return [blocks[0]] + [along(blocks[d], shares - d, shares) for d in range(1, shares)]


def shards(
    inputs, gate_weight, value_weight, step_weight, shared_weight, output_weight, value_kernel,
    shared_kernel, step_bias, decay_log, skip_gain, input_gain, output_gain, cotangent,
):
    shares, groups = lax.axis_size("tensor"), lax.axis_size("dp")
    z, g = lax.axis_index("tensor"), lax.axis_index("dp")
    rows, width = inputs.shape
    per, cols = gate_weight.shape
    own = step_weight.shape[2]
    heads = own * shares
    ns = shared_weight.shape[1] // 4
    inner = cols * shares
    blocks, pages = rows // SPAN, cols // LANES
    fast = groups == 8 and per % 32 == 0
    cfg = dict(
        shares=shares, groups=groups, own=own, head=cols // own, cols=cols, rows=rows, state=ns, per=per,
        pieces=groups if fast else 1,
    )
    cfg["gain_row"] = TAPS * shares * pages
    cfg["state_row"] = cfg["gain_row"] + shares * pages
    cfg["rest_row"] = cfg["state_row"] + 4 * TAPS
    cfg["input_row"] = cfg["rest_row"] + 8
    small_rows = -(-(cfg["input_row"] + width // LANES) // 8) * 8
    ids = (z + jnp.arange(2) * (g - z)).astype(jnp.int32)
    ext = HALO + rows
    pk = cols + LANES

    edge_rows = inputs[rows - HALO :]
    shared_own = lax.dynamic_slice_in_dim(shared_weight, z * ns, ns, 1)
    blank = jnp.zeros((per, LANES - ns - 2 * own), BF16)
    pack1 = jnp.concatenate([value_weight, shared_own, step_weight[:, 0], step_weight[:, 1], blank], axis=1)
    pack2 = jnp.concatenate([gate_weight, output_weight.T], axis=1)

    ogain = output_gain.reshape(1, inner)
    gain = input_gain.reshape(1, width)
    normed, normed_t, cot_t, params, sk = call(
        functools.partial(prep_kernel, cfg),
        (
            sds((rows, width), BF16), sds((width, rows), BF16), sds((width, rows), BF16), sds((8, LANES)),
            sds((4, 8, LANES)),
        ),
        scratch=[pltpu.VMEM((8, LANES), F32)],
        us=3.0,
    )(
        ids, inputs, cotangent, gain, step_bias, decay_log.reshape(1, heads), skip_gain.reshape(1, heads),
        shared_kernel,
    )

    if fast:
        line1 = gather_line(pack1, shares)
        pack2 = jnp.concatenate([pack2, edge_rows], axis=0)
        line2 = [pack2] + [along(after(pack2, line1), d, shares) for d in range(1, shares)]
        halo = line2[1][per:]
        near1 = gather_layer(line1, groups)
        line2 = after(line2, *near1)
        line2 = jnp.stack([block[:per] for block in line2])
        near1, params, sk, ogain, gain, ids, normed, normed_t, cot_t = lax.optimization_barrier(
            (near1, params, sk, ogain, gain, ids, normed, normed_t, cot_t)
        )
        parts1 = gather_pair(near1, groups)
        near2 = gather_layer(after(line2, *near1), groups)
    else:
        parts1, parts2 = gather_any(pack1), gather_any(pack2)
        halo = along(edge_rows, 1, shares)

    full = sds((rows, inner), BF16)
    (
        w1, ws, ahead, vext, u, x, wide, side, su, bc, cct, c2, rho2, c2t, rho2t, dec, states, tots, spread,
        *pays,
    ) = call(
        functools.partial(front_kernel, cfg),
        (
            sds((width, inner), BF16),
            sds((width, shares * LANES), BF16),
            sds((HALO, width), BF16),
            sds((ext, inner), BF16),
            full,
            full,
            sds((2, rows, inner), BF16),
            sds((shares, ext, LANES)),
            sds((4, rows, LANES)),
            sds((4, rows, LANES), BF16),
            sds((blocks, 2 * ns, 2 * SPAN), BF16),
            sds((rows, LANES)),
            sds((rows, LANES)),
            sds((blocks, LANES, SPAN)),
            sds((blocks, LANES, SPAN)),
            sds((4, rows, LANES)),
            sds((blocks, 2 * ns, inner), BF16),
            sds((2 * blocks, LANES)),
            sds((2, LANES, inner), BF16),
            *[sds((shares * ns + HALO, cols), BF16)] * 3,
        ),
        scratch=[
            pltpu.VMEM((ext, inner), F32),
            pltpu.VMEM((blocks, 2 * ns, 2 * SPAN), BF16),
            pltpu.VMEM((2 * SPAN, inner), BF16),
        ],
        us=12.0,
        limit=13 * MB,
    )(ids, halo, normed, gain, value_kernel, sk, params, *parts1)
    got = spread_out(pays, shares)

    yin = call(functools.partial(within_kernel, cfg), full, us=5.0)(
        ids, bc, c2, rho2t, x
    )
    if fast:
        parts2 = gather_pair(after(near2, yin, got[1], got[2]), groups)
    wg, wo, gate, gn_out = call(
        functools.partial(gate_kernel, cfg),
        (sds((width, inner), BF16), sds((width, inner), BF16), full, full),
        us=6.0,
    )(ids, normed, cotangent, *parts2)

    enter, dy, normal, dgate, dcarry, rr, dlocal, rowsum, keeps, *pays = call(
        functools.partial(middle_kernel, cfg),
        (
            sds((blocks, 2 * ns, inner), BF16),
            full,
            full,
            full,
            sds((2, rows, ns)),
            sds((rows, LANES)),
            sds((blocks, 2 * ns, inner), BF16),
            sds((2, 8, inner)),
            sds((3, HALO, inner)),
            *[sds((shares * ns, cols), BF16)] * 3,
        ),
        scratch=[
            pltpu.VMEM((2, rows, inner), BF16),
            pltpu.VMEM((SPAN, inner), F32),
            pltpu.VMEM((SPAN, inner), F32),
            pltpu.VMEM((2, SPAN, inner), F32),
            pltpu.VMEM((2 * SPAN, inner), BF16),
            pltpu.VMEM((2, rows, inner), BF16),
        ],
        us=12.0,
        limit=16 * MB,
    )(ids, yin, x, gate, gn_out, states, bc, cct, dec, tots, spread, params, ogain, *got)
    got = spread_out(pays, shares)

    def piece_shapes(c):
        if fast:
            return (sds((groups // 2, shares, per, c), BF16),) * 2
        return (sds((shares, width, c), BF16),)

    mixed, gx, *grads2 = call(
        functools.partial(output_kernel, cfg),
        (sds((rows, width), BF16), sds((rows, width))) + piece_shapes(2 * cols),
        scratch=[pltpu.VMEM((width, inner), BF16)] * 2,
        us=7.0,
        limit=9 * MB,
    )(ids, inputs, cot_t, normed_t, normal, dgate, wg, wo)
    dy_late = dy
    if fast:
        pairs2 = scatter_pair(cfg, ids, *grads2)
        dy_late = after(dy, pairs2)

    dxi, dbc, da, dk = call(
        functools.partial(back_within_kernel, cfg),
        (full, sds((4, rows, LANES)), sds((rows, LANES)), sds((rows, LANES))),
        scratch=[pltpu.VMEM((LANES, SPAN), F32), pltpu.VMEM((LANES, SPAN), F32)],
        us=9.0,
    )(ids, bc, rho2, c2t, x, dy_late, dcarry, rr, keeps)
    if fast:
        layer2 = scatter_layer(groups, pairs2)

    dp, dps, small = call(
        functools.partial(tail_kernel, cfg),
        (sds((ext, inner), BF16), sds((ext, shares * LANES), BF16), sds((small_rows, LANES))),
        scratch=[
            pltpu.VMEM((ext + HALO, inner), F32),
            pltpu.VMEM((4, ext + HALO, LANES), F32),
            pltpu.VMEM((4, rows, LANES), F32),
            pltpu.VMEM((blocks, 2 * ns, inner), BF16),
            pltpu.VMEM((8, LANES), F32),
            pltpu.VMEM((rows, LANES), F32),
            pltpu.VMEM((2, SPAN, inner), F32),
            pltpu.VMEM((2, SPAN, inner), BF16),
            pltpu.VMEM((2, rows, inner), BF16),
        ],
        us=13.0,
        limit=17 * MB,
    )(
        ids, x, u, dxi, wide, vext, side, su, bc, dbc, dec, enter, da, dk, dlocal, rowsum, keeps, spread,
        *got, value_kernel, sk,
    )
    gn, small, *grads1 = call(
        functools.partial(last_kernel, cfg),
        (sds((ext, width)), sds((small_rows, LANES))) + piece_shapes(pk),
        scratch=[pltpu.VMEM((width, inner), BF16), pltpu.VMEM((width, shares * LANES), BF16)],
        us=6.0,
        limit=9 * MB,
    )(ids, halo, inputs, ahead, normed_t, dp, dps, w1, ws, gx, small)
    first_rows = gn[:HALO]
    if fast:
        small, *pairs1 = scatter_pair(cfg, ids, *after(grads1, *layer2), small)
        blocks2 = layer_sum(cfg, ids, layer2, False)
        layer1 = scatter_layer(groups, pairs1)
        line2 = scatter_line(shares, blocks2)
        small, first_rows, line2 = after((small, first_rows, line2), layer1[1])
        grad_gate, grad_output = call(
            functools.partial(line2_kernel, cfg), (sds((per, cols)), sds((per, cols))), us=1.0
        )(ids, *line2)
        grad_value, grad_step, grad_shared = call(
            functools.partial(line_kernel, cfg),
            (sds((per, cols)), sds((per, 2 * own)), sds((per, shares * ns))),
            scratch=[pltpu.VMEM((shares, per, 2 * cols), F32)],
            us=15.0,
        )(ids, *scatter_line(shares, layer_sum(cfg, ids, layer1, True)))

        steps = [("dp", groups, b) for b in range(1, groups.bit_length() - 1)]
        steps += [("tensor", shares, b) for b in range(shares.bit_length() - 1)]
        for axis, size, b in steps:
            mine, theirs = small, lax.ppermute(small, axis, xor(size, 1 << b))
            small = mine + theirs
    else:
        out1, out2 = scatter_any(grads1), scatter_any(grads2)
        grad_gate, grad_output = out2[:, :cols], out2[:, cols:]
        grad_value, grad_step = out1[:, :cols], out1[:, cols + ns : cols + ns + 2 * own]
        grad_shared = lax.all_gather(out1[:, cols : cols + ns], "tensor", axis=1, tiled=True)
        mine = lax.psum(small, ("dp", "tensor"))
        theirs = jnp.zeros_like(mine)

    edge = lax.ppermute(first_rows, "tensor", [(i + 1, i) for i in range(shares - 1)])
    grad_input = call(functools.partial(finish_kernel, cfg), sds((rows, width), BF16), us=2.0)(
        ids, inputs, cotangent, gain, gn, edge
    )

    vkernel, skernel, bias, decay, skip, ingain, outgain = call(
        functools.partial(small_kernel, cfg),
        (
            sds((TAPS, inner)), sds((TAPS, 4 * ns)), sds((2, heads)), sds((1, heads)), sds((1, heads)),
            sds((1, width)), sds((1, inner)),
        ),
        scratch=[pltpu.VMEM((small_rows, LANES), F32)],
        us=1.0,
    )(ids, mine, theirs)
    return (
        mixed,
        grad_input,
        grad_gate,
        grad_value,
        grad_step.reshape(per, 2, own),
        grad_shared,
        grad_output.T,
        vkernel,
        skernel,
        bias,
        decay.reshape(heads),
        skip.reshape(heads),
        ingain.reshape(width),
        outgain.reshape(inner),
    )


def solution(mesh):
    both = P(("dp", "tensor"), None)
    placed = (
        both, P("dp", "tensor"), P("dp", "tensor"), P("dp", None, "tensor"), P("dp", None),
        P("tensor", "dp"), P(), P(), P(), P(), P(), P(), P(), both,
    )
    return jax.shard_map(
        shards,
        mesh=mesh,
        in_specs=placed,
        out_specs=(
            both, both, P("dp", "tensor"), P("dp", "tensor"), P("dp", None, "tensor"), P("dp", None),
            P("tensor", "dp"), P(), P(), P(), P(), P(), P(), P(),
        ),
        check_vma=False,
    )
```

```python
import functools

import jax
import jax.numpy as jnp
from jax import lax
from jax.experimental import pallas as pl
from jax.experimental.pallas import tpu as pltpu
from jax.sharding import PartitionSpec as P

F32 = jnp.float32
BF16 = jnp.bfloat16
EPSILON = 1e-06
SPAN = 128
HALO = 16
TAPS = 4
LANES = 128
LOG2E = 1.4426950408889634
EXACT = lax.Precision.HIGHEST
LIMIT = 4 * 1024 * 1024
MB = 1024 * 1024

NN = (((1,), (0,)), ((), ()))
NT = (((1,), (1,)), ((), ()))
TN = (((0,), (0,)), ((), ()))


def mm(a, b, dims=NN, precision=None):
    return lax.dot_general(a, b, dims, preferred_element_type=F32, precision=precision)


def iota(shape, dim):
    return lax.broadcasted_iota(jnp.int32, shape, dim)


def sigmoid(v):
    return 0.5 * jnp.tanh(0.5 * v) + 0.5


def split(v, n):
    parts = []
    for _ in range(n):
        part = v.astype(BF16)
        parts.append(part)
        v = v - part.astype(F32)
    return parts


def mm_right(ones, v, n):
    total = None
    for part in split(v, n):
        term = mm(ones, part)
        total = term if total is None else total + term
    return total


def mm_left(v, ones, n, dims=(((1,), (0,)), ((), ()))):
    total = None
    for part in split(v, n):
        term = mm(part, ones, dims)
        total = term if total is None else total + term
    return total


def fold(v):
    return v.reshape(v.shape[0] // 8, 8, v.shape[1]).sum(axis=0)


def chunk_rows(c, base=0):
    return pl.ds(base + c * SPAN, SPAN)


def call(kernel, out_shape, scratch=(), us=1.0, limit=LIMIT):
    def run(*args):
        specs = [
            pl.BlockSpec(memory_space=pltpu.SMEM if i == 0 else pltpu.VMEM)
            for i in range(len(args))
        ]
        return pl.pallas_call(
            kernel,
            out_shape=out_shape,
            in_specs=specs,
            out_specs=jax.tree.map(lambda _: pl.BlockSpec(memory_space=pltpu.VMEM), out_shape),
            scratch_shapes=list(scratch),
            cost_estimate=pl.CostEstimate(
                flops=int(us * 1.1e9), bytes_accessed=int(us * 3.0e6), transcendentals=0
            ),
            compiler_params=pltpu.CompilerParams(vmem_limit_bytes=limit),
        )(*args)

    return run


def sds(shape, dtype=F32):
    return jax.ShapeDtypeStruct(shape, dtype)


def put_weights(ids, pieces, outs, shares, per):
    for rel, piece in enumerate(pieces):
        for d in range(shares):
            start = 0
            for out in outs:
                width = out.shape[1] // shares
                if len(pieces) == 1:
                    out[:, d * width : (d + 1) * width] = piece[d, :, start : start + width]
                else:
                    row = pl.multiple_of((ids[1] ^ rel) * per, per)
                    col = pl.multiple_of((ids[0] + shares - d) % shares * width, LANES)
                    out[pl.ds(row, per), pl.ds(col, width)] = piece[d, :, start : start + width]
                start += width


def take_grads(ids, pieces, held, shares, per):
    n = 2 * pieces[0].shape[0] if len(pieces) > 1 else 1
    for rel in range(n):
        for d in range(shares):
            start = 0
            for part in held:
                width = part.shape[1] // shares
                if n == 1:
                    pieces[0][d, :, start : start + width] = part[:, d * width : (d + 1) * width]
                else:
                    row = pl.multiple_of((ids[1] ^ rel) * per, per)
                    col = pl.multiple_of((ids[0] + shares - d) % shares * width, LANES)
                    pieces[rel % 2][rel // 2, d, :, start : start + width] = part[pl.ds(row, per), pl.ds(col, width)]
                start += width


def blocks_of(total, size):
    return [slice(i, min(i + size, total)) for i in range(0, total, size)]


def cyclic(size, d):
    return [(i, (i + d) % size) for i in range(size)]


def xor(size, bit):
    return [(i, i ^ bit) for i in range(size)]


def along(v, d, shares):
    return lax.ppermute(v, "tensor", cyclic(shares, d))


def spread_out(parts, shares):
    return [along(part, d + 1, shares) for d, part in enumerate(parts)]


def after(values, *others):
    out = lax.optimization_barrier((values,) + others)
    return out[0]


def pair_kernel(n, ids, keep, other, *refs):
    for k in range(n):
        refs[len(refs) - n + k][...] = (keep[k].astype(F32) + other[k].astype(F32)).astype(BF16)
    if len(refs) > n:
        mine, theirs, total = refs[:3]
        total[...] = mine[...] + theirs[...]


def quad_kernel(cfg, first, ids, *refs):
    n, shares, cols, ns = cfg["groups"] // 2, cfg["shares"], cfg["cols"], cfg["state"]
    parts, outs, held = refs[:n], refs[n:-1], refs[-1]
    for d in range(shares):
        q = (ids[0] + shares - d) % shares
        total = parts[0][d].astype(F32)
        for part in parts[1:]:
            total = total + part[d].astype(F32)
        if first:
            outs[d][:, :cols] = total[:, :cols].astype(BF16)
            held[q] = total[:, cols:]
        else:
            outs[d][...] = total.astype(BF16)
    if first:
        low = iota((outs[0].shape[0], LANES), 1) < ns
        for k in range(shares // 2):
            both = jnp.where(low, held[2 * k], pltpu.roll(held[2 * k + 1], ns, 1)).astype(BF16)
            for out in outs:
                out[:, cols + k * LANES : cols + (k + 1) * LANES] = both
        for d, out in enumerate(outs):
            step = held[(ids[0] + shares - d) % shares]
            out[:, cols + shares * ns :] = jnp.where(low, pltpu.roll(step, LANES - ns, 1), 0.0).astype(BF16)


def line_kernel(cfg, ids, *refs):
    shares, cols, ns = cfg["shares"], cfg["cols"], cfg["state"]
    parts, (value, step, shared, held) = refs[:shares], refs[shares:]
    for e, part in enumerate(parts):
        held[e] = part[...].astype(F32)
    total = held[(shares - ids[0]) % shares]
    for q in range(1, shares):
        total = total + held[(q + shares - ids[0]) % shares]
    value[...] = total[:, :cols]
    shared[...] = total[:, cols : cols + shares * ns]
    step[...] = total[:, cols + shares * ns :][:, : step.shape[1]]


def line2_kernel(cfg, ids, *refs):
    shares, cols = cfg["shares"], cfg["cols"]
    parts, (gate, out) = refs[:shares], refs[shares:]
    total = parts[0][...].astype(F32)
    for part in parts[1:]:
        total = total + part[...].astype(F32)
    gate[...] = total[:, :cols]
    out[...] = total[:, cols:]


def fill_spread(cfg, spread):
    own, head = cfg["own"], cfg["head"]
    block = own * head
    for j in range(cfg["shares"]):
        lane = iota((LANES, block), 0)
        place = iota((LANES, block), 1) // head
        for d in range(2):
            cols = slice(j * block, (j + 1) * block)
            spread[d, :, cols] = (lane == own * (2 * j + d) + place).astype(F32).astype(BF16)


def prep_kernel(cfg, ids, inputs, cot, gain, bias, decay, skip, taps, normed, normed_t, cot_t, params, sk, raw):
    own, ns = cfg["own"], cfg["state"]
    heads = own * cfg["shares"]
    size = SPAN // 2
    for c in range(inputs.shape[0] // size):
        at = pl.ds(c * size, size)
        wide = inputs[at, :].astype(F32)
        scale = lax.rsqrt(jnp.mean(wide * wide, axis=1, keepdims=True) + EPSILON)
        normed[at, :] = (wide * scale * gain[...]).astype(BF16)
    normed_t[...] = normed[...].T
    cot_t[...] = cot[...].T
    raw[...] = jnp.zeros_like(raw)
    raw[0:2, :heads] = bias[...]
    raw[2:3, :heads] = decay[...]
    raw[3:4, :heads] = skip[...]
    h, lane = iota((LANES, LANES), 0), iota((LANES, LANES), 1)
    fwd, bwd = (
        mm_left(
            raw[...],
            ((h < heads) & (lane == 2 * own * (h // own) + own * d + h % own)).astype(F32).astype(BF16),
            3,
        )
        for d in range(2)
    )
    params[...] = jnp.zeros_like(params)
    params[0:1, :] = fwd[0:1, :] + bwd[1:2, :]
    params[1:2, :] = fwd[2:3, :] + bwd[2:3, :]
    params[2:3, :] = fwd[3:4, :] + bwd[3:4, :]
    low = iota((8, LANES), 1) < ns
    for k in range(4):
        raw[...] = jnp.zeros_like(raw)
        raw[0:TAPS, :] = taps[:, k // 2 * LANES : (k // 2 + 1) * LANES]
        v = raw[...]
        sk[k] = jnp.where(low, pltpu.roll(v, LANES - ns, 1) if k % 2 else v, 0.0)


def small_kernel(cfg, ids, mine, theirs, vkernel, skernel, bias, decay, skip, ingain, outgain, held):
    own, ns, shares = cfg["own"], cfg["state"], cfg["shares"]
    heads = own * shares
    held[...] = mine[...] + theirs[...]
    n = outgain.shape[1] // LANES
    for k in range(n):
        lanes = slice(k * LANES, (k + 1) * LANES)
        for m in range(TAPS):
            vkernel[m : m + 1, lanes] = held[m * n + k : m * n + k + 1, :]
        outgain[:, lanes] = held[cfg["gain_row"] + k : cfg["gain_row"] + k + 1, :]
    for k in range(ingain.shape[1] // LANES):
        row = cfg["input_row"] + k
        ingain[:, k * LANES : (k + 1) * LANES] = held[row : row + 1, :]
    low = iota((1, LANES), 1) < ns
    for m in range(TAPS):
        for k in range(2):
            row = cfg["state_row"] + 4 * m + 2 * k
            both = held[row : row + 2, :]
            odd = jnp.concatenate([both] * 4, axis=0)
            odd = pltpu.roll(odd, ns, 1)[1:2, :]
            skernel[m : m + 1, k * LANES : (k + 1) * LANES] = jnp.where(low, both[0:1, :], odd)
    rest = held[cfg["rest_row"] : cfg["rest_row"] + 8, :]
    lane, h = iota((LANES, LANES), 0), iota((LANES, LANES), 1)
    fwd, bwd = (
        mm_left(
            rest,
            ((h < heads) & (lane == 2 * own * (h // own) + own * d + h % own)).astype(F32).astype(BF16),
            3,
        )
        for d in range(2)
    )
    bias[0:1, :] = fwd[0:1, :heads]
    bias[1:2, :] = bwd[0:1, :heads]
    decay[...] = fwd[1:2, :heads] + bwd[1:2, :heads]
    skip[...] = fwd[2:3, :heads]


def front_kernel(cfg, *refs):
    n = cfg["pieces"]
    ids, halo, normed, gain, vk, sk, params = refs[:7]
    pieces = refs[7 : 7 + n]
    (
        w1, ws, ahead, vext, u_out, x_out, wide_out, side, su_out, bc_out, cct, c2, rho2, c2t, rho2t, dec, states,
        tots, spread, pay1, pay2, pay3, acc, bbt, xw,
    ) = refs[7 + n :]
    shares, own, cols, rows, ns = (cfg[k] for k in ("shares", "own", "cols", "rows", "state"))
    blocks, pages = rows // SPAN, cols // LANES
    put_weights(ids, pieces, (w1, ws), shares, cfg["per"])
    fill_spread(cfg, spread)

    edge = halo[...].astype(F32)
    scale = lax.rsqrt(jnp.mean(edge * edge, axis=1, keepdims=True) + EPSILON)
    ahead[...] = jnp.where(ids[0] > 0, edge * scale * gain[...], 0.0).astype(BF16)
    bbt[...] = jnp.zeros_like(bbt)
    cct[...] = jnp.zeros_like(cct)

    for part in blocks_of(shares * cols, 512):
        acc[0:HALO, part] = mm(ahead[...], w1[:, part])
        acc[HALO:, part] = mm(normed[...], w1[:, part])
    sides, edge = mm(normed[...], ws[...]), mm(ahead[...], ws[...])
    for j in range(shares):
        side[j, :HALO, :] = edge[:, j * LANES : (j + 1) * LANES]
        side[j, HALO:, :] = sides[:, j * LANES : (j + 1) * LANES]
    for j in range(shares):
        here = slice(j * cols, (j + 1) * cols)
        for c in range(blocks):
            vext[chunk_rows(c), here] = acc[chunk_rows(c), here].astype(BF16)
        vext[blocks * SPAN :, here] = acc[blocks * SPAN :, here].astype(BF16)
        for c in range(blocks):
            for p in range(pages + 1):
                here = slice(j * cols + p * LANES, j * cols + (p + 1) * LANES)
                u = None
                for m in range(TAPS):
                    rows_m = chunk_rows(c, HALO - TAPS + 1 + m)
                    if p < pages:
                        term = vk[m : m + 1, here] * acc[rows_m, here]
                    else:
                        term = sk[j, m : m + 1, :] * side[j, rows_m, :]
                    u = term if u is None else u + term
                v = u * sigmoid(u)
                if p < pages:
                    u_out[chunk_rows(c), here] = u.astype(BF16)
                    x_out[chunk_rows(c), here] = v.astype(BF16)
                else:
                    su_out[j, chunk_rows(c), :] = u
                    bc_out[j, chunk_rows(c), :] = v.astype(BF16)
                    turned = v.T[:ns].astype(BF16)
                    d = j // 2
                    target = cct if j % 2 else bbt
                    target[c, d * ns : (d + 1) * ns, d * SPAN : (d + 1) * SPAN] = turned

    lane = iota((SPAN, LANES), 1)
    is_fwd = lane % (2 * own) < own
    at0, at1 = iota((SPAN, SPAN), 0), iota((SPAN, SPAN), 1)
    both = jnp.concatenate([(at0 >= at1).astype(F32), (at0 <= at1).astype(F32)], axis=0).astype(BF16)
    rate = jnp.where(iota((1, LANES), 1) < 2 * own * shares, -jnp.exp(params[1:2, :]), 0.0)
    for c in range(blocks):
        raw = jnp.zeros((SPAN, LANES), F32)
        for j in range(shares):
            moved = pltpu.roll(side[j, chunk_rows(c, HALO), :], (2 * own * j - ns) % LANES, 1)
            raw = jnp.where((lane >= 2 * own * j) & (lane < 2 * own * (j + 1)), moved, raw)
        v = raw + params[0:1, :]
        small = jnp.exp(jnp.minimum(v, 0.0))
        dt = jnp.where(v < -15.0, small, jnp.maximum(v, 0.0) + jnp.log1p(jnp.exp(-jnp.abs(v))))
        log_dt = jnp.where(v < -15.0, v, jnp.log(jnp.maximum(dt, 1e-30)))
        ratio = jnp.where(v < -15.0, 1.0, sigmoid(v) / jnp.maximum(dt, 1e-30))
        a = dt * rate
        sums = mm_right(both, a, 3)
        cum = jnp.where(is_fwd, sums[:SPAN], sums[SPAN:])
        tot = jnp.sum(a, axis=0, keepdims=True)
        rho = cum - log_dt
        cc = cum * LOG2E
        rr = rho * LOG2E
        c2[chunk_rows(c), :] = cc
        rho2[chunk_rows(c), :] = rr
        c2t[c] = cc.T
        rho2t[c] = rr.T
        dec[0, chunk_rows(c), :] = a
        dec[1, chunk_rows(c), :] = ratio
        dec[2, chunk_rows(c), :] = jnp.exp(tot - rho)
        dec[3, chunk_rows(c), :] = jnp.exp(cum)
        tots[c : c + 1, :] = tot
    fwd1 = iota((1, LANES), 1) % (2 * own) < own
    zero = jnp.zeros((1, LANES), F32)
    lead = []
    for c in range(blocks):
        later, sooner = zero, zero
        for k in range(blocks):
            if k > c:
                later = later + tots[k : k + 1, :]
            if k < c:
                sooner = sooner + tots[k : k + 1, :]
        lead.append(jnp.exp(jnp.where(fwd1, later, sooner)))
        tots[blocks + c : blocks + c + 1, :] = jnp.where(fwd1, sooner, later)
    lead = jnp.concatenate(lead + [zero] * (8 - blocks), axis=0)
    whole = tots[0:1, :]
    for c in range(1, blocks):
        whole = whole + tots[c : c + 1, :]
    extra = jnp.concatenate([p.astype(F32) for p in split(whole, 3)] + [zero] * (HALO - 3), axis=0)
    extra = jnp.concatenate([extra, jnp.zeros((HALO, cols - LANES), F32)], axis=1).astype(BF16)
    for pay in (pay1, pay2, pay3):
        pay[shares * ns :, :] = extra

    weights = dec[2].astype(BF16)
    for d in range(2):
        wide_out[d] = mm(weights, spread[d]).astype(BF16)
    grow_f, grow_b = mm_left(lead, spread[0], 2), mm_left(lead, spread[1], 2)
    for c in range(blocks):
        for d in range(2):
            for p in range(shares * pages):
                lanes = slice(p * LANES, (p + 1) * LANES)
                product = wide_out[d, chunk_rows(c), lanes].astype(F32) * x_out[chunk_rows(c), lanes].astype(F32)
                xw[d * SPAN : (d + 1) * SPAN, lanes] = product.astype(BF16)
        states[c] = mm(bbt[c], xw[...]).astype(BF16)
    for j in range(shares):
        at = slice(j * ns, (j + 1) * ns)
        here = slice(j * cols, (j + 1) * cols)
        f, b = jnp.zeros((ns, cols), F32), jnp.zeros((ns, cols), F32)
        for c in range(blocks):
            f = f + grow_f[c : c + 1, here] * states[c, :ns, here].astype(F32)
            b = b + grow_b[c : c + 1, here] * states[c, ns:, here].astype(F32)
        for dist, pay in ((1, pay1), (2, pay2), (3, pay3)):
            pay[at, :] = jnp.where(ids[0] + dist < shares, f, b).astype(BF16)


def stack_pair(first, v):
    zero = jnp.zeros_like(v)
    return jnp.concatenate([jnp.where(first, v, zero), jnp.where(first, zero, v)], axis=0)


def within_kernel(cfg, ids, bc, c2, rho2t, x, y):
    shares, own, rows = (cfg[k] for k in ("shares", "own", "rows"))
    t, s = iota((SPAN, SPAN), 0), iota((SPAN, SPAN), 1)
    low = t > s
    first = iota((SPAN, LANES), 1) < cfg["head"]

    def block(c, _):
        at = pl.ds(pl.multiple_of(c * SPAN, SPAN), SPAN)
        g = jnp.where(low, mm(bc[1, at, :], bc[0, at, :], NT), mm(bc[3, at, :], bc[2, at, :], NT))
        g = jnp.where(t == s, 0.0, g)
        cc = c2[at, :]
        for k in range(shares * own // 2):
            j, p = k // (own // 2), k % (own // 2)
            mats = []
            for i in (2 * p, 2 * p + 1):
                f, b = 2 * own * j + i, 2 * own * j + own + i
                col = jnp.where(low, cc[:, f : f + 1], cc[:, b : b + 1])
                row = jnp.where(low, rho2t[c, f : f + 1, :], rho2t[c, b : b + 1, :])
                mats.append((jnp.exp2(col - row) * g).astype(BF16))
            lanes = slice(k * LANES, (k + 1) * LANES)
            y[at, lanes] = mm(jnp.concatenate(mats, axis=1), stack_pair(first, x[at, lanes])).astype(BF16)
        return 0

    lax.fori_loop(0, rows // SPAN, block, 0)


def gate_kernel(cfg, *refs):
    n = cfg["pieces"]
    ids, normed, cot = refs[:3]
    pieces = refs[3 : 3 + n]
    wg, wo, gate, gn = refs[3 + n :]
    put_weights(ids, pieces, (wg, wo), cfg["shares"], cfg["per"])
    for part in blocks_of(gate.shape[1], 512):
        gate[:, part] = mm(normed[...], wg[:, part]).astype(BF16)
        gn[:, part] = mm(cot[...], wo[:, part]).astype(BF16)


def incoming(ids, cfg, got, j, near, far):
    z, shares, ns = ids[0], cfg["shares"], cfg["state"]
    r1, r2, r3 = (part[j * ns : (j + 1) * ns, :].astype(F32) for part in got)

    def keep(test, v):
        return jnp.where(test, v, 0.0)

    before = keep(z >= 1, r1) + near[0] * keep(z >= 2, r2) + near[1] * keep(z >= 3, r3)
    behind = (
        keep(z <= shares - 2, r3)
        + far[0] * keep(z <= shares - 3, r2)
        + far[1] * keep(z <= shares - 4, r1)
    )
    return before, behind


def middle_kernel(cfg, *refs):
    (
        ids, yin, x, gate, gn, states, bc, cct, dec, tots, spread, params, ogain, r1, r2, r3,
        enter, dy, normal, dgate, dcarry, rr, dlocal, rowsum, keeps, p1, p2, p3,
        ecx, ys, acts, kept, edy, prod,
    ) = refs
    shares, cols, rows, ns = (cfg[k] for k in ("shares", "cols", "rows", "state"))
    blocks, inner = rows // SPAN, cols * shares
    pages = inner // LANES
    zero = jnp.zeros((1, LANES), F32)

    def whole(r):
        v = r[shares * ns :, :LANES].astype(F32)
        return v[0:1, :] + v[1:2, :] + v[2:3, :]

    l1, l2, l3 = whole(r1), whole(r2), whole(r3)
    lines = [tots[c : c + 1, :] for c in range(2 * blocks)] + [l1, l1 + l2, l3, l3 + l2]
    lines = jnp.exp(jnp.concatenate(lines + [zero] * (HALO - len(lines)), axis=0))
    skip_rows = jnp.concatenate([params[2:3, :]] + [zero] * 7, axis=0)
    for d in range(2):
        keeps[d] = mm_left(lines, spread[d], 2)
        ecx[d] = mm(dec[3].astype(BF16), spread[d]).astype(BF16)
    keeps[2, 0:8] = mm_left(skip_rows, spread[0], 2)
    b = 2 * blocks
    for j in range(shares):
        here = slice(j * cols, (j + 1) * cols)
        kf, kb = keeps[0, :, here], keeps[1, :, here]
        e, e_b = incoming(
            ids, cfg, (r1, r2, r3), j,
            (kf[b : b + 1, :], kf[b + 1 : b + 2, :]), (kb[b + 2 : b + 3, :], kb[b + 3 : b + 4, :]),
        )
        for c in range(blocks):
            enter[c, :ns, here] = e.astype(BF16)
            e = kf[c : c + 1, :] * e + states[c, :ns, here].astype(F32)
        for c in reversed(range(blocks)):
            enter[c, ns:, here] = e_b.astype(BF16)
            e_b = kb[c : c + 1, :] * e_b + states[c, ns:, here].astype(F32)
    rowsum[...] = jnp.zeros_like(rowsum)

    def block(c, _):
        at = pl.ds(pl.multiple_of(c * SPAN, SPAN), SPAN)
        for d in range(2):
            kept[d] = mm(bc[1 + 2 * d, at, :ns], enter[c, d * ns : (d + 1) * ns, :])
        square, dot = jnp.zeros((SPAN, LANES), F32), jnp.zeros((SPAN, LANES), F32)
        for p in range(pages):
            lanes = slice(p * LANES, (p + 1) * LANES)
            cf = kept[0, :, lanes] * ecx[0, at, lanes].astype(F32)
            cb = kept[1, :, lanes] * ecx[1, at, lanes].astype(F32)
            kept[0, :, lanes] = cf
            kept[1, :, lanes] = cb
            v = yin[at, lanes].astype(F32) + keeps[2, 0:1, lanes] * x[at, lanes].astype(F32) + cf + cb
            ys[:, lanes] = v
            g = gate[at, lanes].astype(F32)
            act = g * sigmoid(g)
            acts[:, lanes] = act
            gated = v * act
            square = square + gated * gated
            dot = dot + gn[at, lanes].astype(F32) * ogain[:, lanes] * gated
        square = jnp.sum(square, axis=1, keepdims=True)
        dot = jnp.sum(dot, axis=1, keepdims=True)
        inv = lax.rsqrt(square / inner + EPSILON)
        back = inv * inv * inv * dot / inner
        for p in range(pages):
            lanes = slice(p * LANES, (p + 1) * LANES)
            v, act, g = ys[:, lanes], acts[:, lanes], gate[at, lanes].astype(F32)
            gnv, og = gn[at, lanes].astype(F32), ogain[:, lanes]
            sig = sigmoid(g)
            gated = v * act
            scaled = gated * inv
            normal[at, lanes] = (scaled * og).astype(BF16)
            rowsum[0, :, lanes] += fold(gnv * scaled)
            dgated = inv * (gnv * og) - gated * back
            d_scan = dgated * act
            dy[at, lanes] = d_scan.astype(BF16)
            dgate[at, lanes] = (dgated * v * (sig + act * (1.0 - sig))).astype(BF16)
            rowsum[1, :, lanes] += fold(d_scan * x[at, lanes].astype(F32))
            for d in range(2):
                prod[d, at, lanes] = (d_scan * kept[d, :, lanes]).astype(BF16)
                wide = ecx[d, at, lanes].astype(F32) * d_scan
                edy[d * SPAN : (d + 1) * SPAN, lanes] = wide.astype(BF16)
        dlocal[c] = mm(cct[c], edy[...]).astype(BF16)
        for d in range(2):
            dcarry[d, at, :] = mm(edy[d * SPAN : (d + 1) * SPAN, :], enter[c, d * ns : (d + 1) * ns, :], NT)
        return 0

    lax.fori_loop(0, blocks, block, 0)
    rr[...] = mm(prod[0], spread[0], NT) + mm(prod[1], spread[1], NT)

    for j in range(shares):
        here = slice(j * cols, (j + 1) * cols)
        f, b_ = jnp.zeros((ns, cols), F32), jnp.zeros((ns, cols), F32)
        for c in range(blocks):
            f = f + keeps[0, blocks + c : blocks + c + 1, here] * dlocal[c, :ns, here].astype(F32)
            b_ = b_ + keeps[1, blocks + c : blocks + c + 1, here] * dlocal[c, ns:, here].astype(F32)
        for dist, pay in ((1, p1), (2, p2), (3, p3)):
            pay[j * ns : (j + 1) * ns, :] = jnp.where(ids[0] + dist < shares, b_, f).astype(BF16)


def output_kernel(cfg, *refs):
    ids, inputs, cot_t, normed_t, normal, dgate, wg, wo = refs[:8]
    mixed, gx = refs[8:10]
    pieces, held = refs[10:-2], refs[-2:]
    for part in blocks_of(normal.shape[1], 512):
        held[0][:, part] = mm(normed_t[...], dgate[:, part]).astype(BF16)
        held[1][:, part] = mm(cot_t[...], normal[:, part]).astype(BF16)
    take_grads(ids, pieces, held, cfg["shares"], cfg["per"])
    for part in blocks_of(inputs.shape[1], 256):
        mixed[:, part] = (mm(normal[...], wo[part, :], NT) + inputs[:, part].astype(F32)).astype(BF16)
        gx[:, part] = mm(dgate[...], wg[part, :], NT)


def back_within_kernel(cfg, ids, bc, rho2, c2t, x, dy, dcarry, rr, keeps, dx, dbc, da, dk, das, ras):
    shares, own, rows, ns = (cfg[k] for k in ("shares", "own", "rows", "state"))
    s, t = iota((SPAN, SPAN), 0), iota((SPAN, SPAN), 1)
    up = t > s
    first = iota((SPAN, LANES), 1) < cfg["head"]
    after_t = (s >= t).astype(F32).astype(BF16)
    until_t = (s <= t).astype(F32).astype(BF16)
    tri = jnp.concatenate([after_t, until_t], axis=1)
    sums = jnp.concatenate([until_t, after_t], axis=0)
    lane = iota((SPAN, LANES), 1)
    is_fwd = iota((LANES, SPAN), 0) % (2 * own) < own

    def block(c, _):
        at = pl.ds(pl.multiple_of(c * SPAN, SPAN), SPAN)
        g = jnp.where(up, mm(bc[0, at, :], bc[1, at, :], NT), mm(bc[2, at, :], bc[3, at, :], NT))
        g = jnp.where(t == s, 0.0, g)
        rho = rho2[at, :]
        dg = jnp.zeros((SPAN, SPAN), F32)
        das[...] = jnp.zeros_like(das)
        ras[...] = jnp.zeros_like(ras)
        for k in range(shares * own // 2):
            j, p = k // (own // 2), k % (own // 2)
            lanes = slice(k * LANES, (k + 1) * LANES)
            dyp = dy[at, lanes]
            dm = mm(stack_pair(first, x[at, lanes]), dyp, NT)
            ws, zs = [], []
            for q in range(2):
                i = 2 * p + q
                f, b = 2 * own * j + i, 2 * own * j + own + i
                row = jnp.where(up, c2t[c, f : f + 1, :], c2t[c, b : b + 1, :])
                col = jnp.where(up, rho[:, f : f + 1], rho[:, b : b + 1])
                pw = jnp.exp2(row - col)
                ud = dm[q * SPAN : (q + 1) * SPAN] * pw
                dg = dg + ud
                ws.append((pw * g).astype(BF16))
                zd = ud * g
                zs.append(zd.astype(BF16))
                rf = jnp.sum(jnp.where(up, zd, 0.0), axis=0, keepdims=True)
                ras[f : f + 1, :] = rf
                ras[b : b + 1, :] = jnp.sum(zd, axis=0, keepdims=True) - rf
            back = mm(jnp.concatenate(ws, axis=1), stack_pair(first, dyp))
            dx[at, lanes] = (back + keeps[2, 0:1, lanes] * dyp.astype(F32)).astype(BF16)
            cross = mm(jnp.concatenate(zs, axis=0), tri)
            for q in range(2):
                i = 2 * p + q
                f, b = 2 * own * j + i, 2 * own * j + own + i
                part = cross[q * SPAN : (q + 1) * SPAN]
                das[f : f + 1, :] = jnp.sum(jnp.where(up, part[:, :SPAN], 0.0), axis=0, keepdims=True)
                das[b : b + 1, :] = jnp.sum(jnp.where(t < s, part[:, SPAN:], 0.0), axis=0, keepdims=True)
        df = jnp.where(up, dg, 0.0)
        db = jnp.where(t < s, dg, 0.0)
        dbc[0, at, :] = mm(df.astype(BF16), bc[1, at, :])
        dbc[1, at, :] = mm(df.T.astype(BF16), bc[0, at, :])
        dbc[2, at, :] = mm(db.astype(BF16), bc[3, at, :])
        dbc[3, at, :] = mm(db.T.astype(BF16), bc[2, at, :])
        dbc[1, at, :ns] += dcarry[0, at, :]
        dbc[3, at, :ns] += dcarry[1, at, :]
        a = das[...]
        later = jnp.where(lane < SPAN - 1, pltpu.roll(a, SPAN - 1, 1), 0.0)
        sooner = jnp.where(lane > 0, pltpu.roll(a, 1, 1), 0.0)
        kd = ras[...] - a + jnp.where(is_fwd, later, sooner)
        through = mm_right(sums, rr[at, :], 2)
        da[at, :] = a.T + jnp.where(lane % (2 * own) < own, through[:SPAN], through[SPAN:])
        dk[at, :] = kd.T
        return 0

    lax.fori_loop(0, rows // SPAN, block, 0)


def tail_kernel(cfg, *refs):
    (
        ids, x, u, dxi, wide_in, vext, side, su, bc, dbc, dec, enter, da, dk, dlocal, rowsum, keeps, spread,
        r1, r2, r3, vk, sk,
        dp, dps, small,
        du, dsu, dst, dstate, xs, qs, held, xw, prod,
    ) = refs
    shares, own, cols, rows, ns = (cfg[k] for k in ("shares", "own", "cols", "rows", "state"))
    blocks, inner = rows // SPAN, cols * shares
    pages = inner // LANES

    du[0:HALO, :] = jnp.zeros((HALO, inner), F32)
    du[HALO + rows :, :] = jnp.zeros((HALO, inner), F32)
    dsu[...] = jnp.zeros_like(dsu)

    b = 2 * blocks
    total_x = jnp.zeros((8, LANES), F32)
    for j in range(shares):
        here = slice(j * cols, (j + 1) * cols)
        kf, kb = keeps[0, :, here], keeps[1, :, here]
        now_b, now_f = incoming(
            ids, cfg, (r1, r2, r3), j,
            (kb[b : b + 1, :], kb[b + 1 : b + 2, :]), (kf[b + 2 : b + 3, :], kf[b + 3 : b + 4, :]),
        )
        for d, order, now, kept in (
            (0, list(reversed(range(blocks))), now_f, kf),
            (1, list(range(blocks)), now_b, kb),
        ):
            part = slice(d * ns, (d + 1) * ns)
            rows_x = [None] * blocks
            for c in order:
                dstate[c, part, here] = now.astype(BF16)
                rows_x[c] = kept[c : c + 1, :] * jnp.sum(
                    enter[c, part, here].astype(F32) * now, axis=0, keepdims=True
                )
                now = kept[c : c + 1, :] * now + dlocal[c, part, here].astype(F32)
            rows_x = jnp.concatenate(rows_x + [jnp.zeros((8 - blocks, cols), F32)], axis=0)
            total_x = total_x + mm_left(rows_x, spread[d, :, here], 2, NT)
    xs[...] = total_x

    def states_part(c, _):
        at = pl.ds(pl.multiple_of(c * SPAN, SPAN), SPAN)
        moved = pl.ds(pl.multiple_of(c * SPAN + HALO, HALO), SPAN)
        for d in range(2):
            held[d] = mm(bc[2 * d, at, :ns], dstate[c, d * ns : (d + 1) * ns, :])
        for p in range(pages):
            lanes = slice(p * LANES, (p + 1) * LANES)
            xv = x[at, lanes].astype(F32)
            dx = dxi[at, lanes].astype(F32)
            for d in range(2):
                wide = wide_in[d, at, lanes].astype(F32)
                through = held[d, :, lanes] * wide
                dx = dx + through
                prod[d, at, lanes] = (through * xv).astype(BF16)
                xw[d, :, lanes] = (wide * xv).astype(BF16)
            uv = u[at, lanes].astype(F32)
            sig = sigmoid(uv)
            du[moved, lanes] = dx * (sig + uv * sig * (1.0 - sig))
        for d in range(2):
            dst[2 * d, at, :] = dbc[2 * d, at, :]
            dst[2 * d, at, :ns] += mm(xw[d], dstate[c, d * ns : (d + 1) * ns, :], NT)
            dst[2 * d + 1, at, :] = dbc[2 * d + 1, at, :]
        return 0

    lax.fori_loop(0, blocks, states_part, 0)
    qs[...] = mm(prod[0], spread[0], NT) + mm(prod[1], spread[1], NT)
    parts = [(0, HALO)] + [(HALO + c * SPAN, SPAN) for c in range(blocks)]

    for p in range(pages):
        lanes = slice(p * LANES, (p + 1) * LANES)
        sums = [jnp.zeros((8, LANES), F32) for _ in range(TAPS)]
        for start, size in parts:
            old = vext[pl.ds(start, size), lanes].astype(F32)
            dv = None
            for m in range(TAPS):
                shifted = du[pl.ds(start + TAPS - 1 - m, size), lanes]
                term = vk[m : m + 1, lanes] * shifted
                dv = term if dv is None else dv + term
                sums[m] = sums[m] + fold(old * shifted)
            dp[pl.ds(start, size), lanes] = dv.astype(BF16)
        for m in range(TAPS):
            small[m * pages + p : m * pages + p + 1, :] = jnp.sum(sums[m], axis=0, keepdims=True)
        row = cfg["gain_row"] + p
        small[row : row + 1, :] = jnp.sum(rowsum[0, :, lanes], axis=0, keepdims=True)

    lane = iota((SPAN, LANES), 1)
    is_fwd = lane % (2 * own) < own
    at0, at1 = iota((SPAN, SPAN), 0), iota((SPAN, SPAN), 1)
    both = jnp.concatenate([(at0 > at1).astype(F32), (at0 < at1).astype(F32)], axis=0).astype(BF16)
    dbias = jnp.zeros((1, LANES), F32)
    ddecay = jnp.zeros((1, LANES), F32)
    steps = []
    for c in range(blocks):
        at = chunk_rows(c)
        qv = qs[at, :]
        sums = mm_right(both, qv, 2)
        total = da[at, :] + xs[c : c + 1, :] + jnp.where(is_fwd, sums[:SPAN], sums[SPAN:])
        through = total * dec[0, at, :]
        step = (dk[at, :] + qv + through) * dec[1, at, :]
        step = jnp.where(lane < 2 * own * shares, step, 0.0)
        steps.append(step)
        dbias = dbias + jnp.sum(step, axis=0, keepdims=True)
        ddecay = ddecay + jnp.sum(through, axis=0, keepdims=True)
    base = cfg["rest_row"]
    small[base : base + 1, :] = dbias
    small[base + 1 : base + 2, :] = ddecay
    skips = mm_left(rowsum[1], spread[0], 2, NT)
    small[base + 2 : base + 3, :] = jnp.sum(skips, axis=0, keepdims=True)
    small[base + 3 : base + 8, :] = jnp.zeros((5, LANES), F32)

    for k in range(4):
        for c in range(blocks):
            at = chunk_rows(c)
            uv = su[k, at, :]
            sig = sigmoid(uv)
            dsu[k, chunk_rows(c, HALO), :] = dst[k, at, :] * sig * (1.0 + uv * (1.0 - sig))
        sums = [jnp.zeros((8, LANES), F32) for _ in range(TAPS)]
        for start, size in parts:
            old = side[k, pl.ds(start, size), :]
            dv = None
            for m in range(TAPS):
                shifted = dsu[k, pl.ds(start + TAPS - 1 - m, size), :]
                term = sk[k, m : m + 1, :] * shifted
                dv = term if dv is None else dv + term
                sums[m] = sums[m] + fold(old * shifted)
            if start >= HALO:
                moved = pltpu.roll(steps[(start - HALO) // SPAN], (ns - 2 * own * k) % LANES, 1)
                dv = dv + jnp.where((lane >= ns) & (lane < ns + 2 * own), moved, 0.0)
            dps[pl.ds(start, size), k * LANES : (k + 1) * LANES] = dv.astype(BF16)
        for m in range(TAPS):
            row = cfg["state_row"] + m * 4 + k
            small[row : row + 1, :] = jnp.sum(sums[m], axis=0, keepdims=True)
    small[cfg["input_row"] :, :] = jnp.zeros_like(small[cfg["input_row"] :, :])


def last_kernel(cfg, *refs):
    ids, halo, inputs, ahead, normed_t, dp, dps, w1, ws, gx, small_in = refs[:11]
    gn, small = refs[11:13]
    pieces, held = refs[13:-2], refs[-2:]
    shares, rows, width = cfg["shares"], cfg["rows"], inputs.shape[1]
    for grad, out in ((dp, held[0]), (dps, held[1])):
        for part in blocks_of(grad.shape[1], 512):
            total = mm(normed_t[...], grad[HALO:, part]) + mm(ahead[...], grad[:HALO, part], TN)
            out[:, part] = total.astype(BF16)
    take_grads(ids, pieces, held, shares, cfg["per"])
    for part in blocks_of(width, 256):
        gn[:HALO, part] = mm(dp[:HALO, :], w1[part, :], NT) + mm(dps[:HALO, :], ws[part, :], NT)
        back = mm(dp[HALO:, :], w1[part, :], NT) + mm(dps[HALO:, :], ws[part, :], NT)
        gn[HALO:, part] = back + gx[:, part]

    def plain(block):
        wide = block.astype(F32)
        return wide * lax.rsqrt(jnp.mean(wide * wide, axis=1, keepdims=True) + EPSILON)

    total = fold(jnp.where(ids[0] > 0, gn[0:HALO, :] * plain(halo[...]), 0.0))
    for c in range(rows // SPAN):
        total = total + fold(gn[chunk_rows(c, HALO), :] * plain(inputs[chunk_rows(c), :]))
    total = jnp.sum(total, axis=0, keepdims=True)
    small[...] = small_in[...]
    for k in range(width // LANES):
        row = cfg["input_row"] + k
        small[row : row + 1, :] = total[:, k * LANES : (k + 1) * LANES]


def finish_kernel(cfg, ids, inputs, cot, gain, gn, edge, out):
    rows = cfg["rows"]
    size = SPAN // 2
    for c in range(rows // size):
        at = pl.ds(c * size, size)
        wide = inputs[at, :].astype(F32)
        g = gn[pl.ds(HALO + c * size, size), :]
        if c == rows // size - 1:
            g = jnp.concatenate([g[: size - HALO], g[size - HALO :] + edge[...]], axis=0)
        scale = lax.rsqrt(jnp.mean(wide * wide, axis=1, keepdims=True) + EPSILON)
        f = g * gain[...]
        mean = jnp.mean(f * wide, axis=1, keepdims=True)
        grad = cot[at, :].astype(F32) + scale * f - wide * (scale * scale * scale) * mean
        out[at, :] = grad.astype(BF16)


def gather_line(pack, shares):
    return jnp.stack([pack] + [along(pack, d, shares) for d in range(1, shares)])


def gather_layer(held, groups):
    return [held] + [lax.ppermute(held, "dp", xor(groups, 2 * k)) for k in range(1, groups // 2)]


def gather_pair(near, groups):
    pieces = []
    for block in near:
        pieces += [block, lax.ppermute(block, "dp", xor(groups, 1))]
    return pieces


def gather_any(pack):
    rows = lax.all_gather(pack, "dp", axis=0, tiled=True)
    return [lax.all_gather(rows, "tensor", axis=0, tiled=False)]


def scatter_any(pieces):
    part = lax.psum_scatter(pieces[0].astype(F32), "dp", scatter_dimension=1, tiled=True)
    return lax.psum_scatter(part, "tensor", scatter_dimension=0, tiled=False)


def scatter_pair(cfg, ids, keep, send, *small):
    groups, shares, per, c = cfg["groups"], cfg["shares"], cfg["per"], keep.shape[-1]
    others = [lax.ppermute(v, "dp", xor(groups, 1)) for v in (send,) + small]
    n = groups // 2
    shapes = tuple(sds(v.shape) for v in small) + tuple(sds((shares, per, c), BF16) for _ in range(n))
    sums = [v for pair in zip(small, others[1:]) for v in pair]
    return call(functools.partial(pair_kernel, n), shapes, us=1.5)(ids, keep, others[0], *sums)


def scatter_layer(groups, pairs):
    return [pairs[0]] + [lax.ppermute(pairs[k], "dp", xor(groups, 2 * k)) for k in range(1, groups // 2)]


def layer_sum(cfg, ids, parts, first):
    shares, per, cols = (cfg[k] for k in ("shares", "per", "cols"))
    return call(
        functools.partial(quad_kernel, cfg, first),
        (sds((per, 2 * cols), BF16),) * shares,
        scratch=[pltpu.VMEM((shares, per, LANES), F32)],
        us=15.0 if first else 1.5,
    )(ids, *parts)


def scatter_line(shares, blocks):
    return [blocks[0]] + [along(blocks[d], shares - d, shares) for d in range(1, shares)]


def shards(
    inputs, gate_weight, value_weight, step_weight, shared_weight, output_weight, value_kernel,
    shared_kernel, step_bias, decay_log, skip_gain, input_gain, output_gain, cotangent,
):
    shares, groups = lax.axis_size("tensor"), lax.axis_size("dp")
    z, g = lax.axis_index("tensor"), lax.axis_index("dp")
    rows, width = inputs.shape
    per, cols = gate_weight.shape
    own = step_weight.shape[2]
    heads = own * shares
    ns = shared_weight.shape[1] // 4
    inner = cols * shares
    blocks, pages = rows // SPAN, cols // LANES
    fast = groups == 8 and per % 32 == 0
    cfg = dict(
        shares=shares, groups=groups, own=own, head=cols // own, cols=cols, rows=rows, state=ns, per=per,
        pieces=groups if fast else 1,
    )
    cfg["gain_row"] = TAPS * shares * pages
    cfg["state_row"] = cfg["gain_row"] + shares * pages
    cfg["rest_row"] = cfg["state_row"] + 4 * TAPS
    cfg["input_row"] = cfg["rest_row"] + 8
    small_rows = -(-(cfg["input_row"] + width // LANES) // 8) * 8
    ids = (z + jnp.arange(2) * (g - z)).astype(jnp.int32)
    ext = HALO + rows
    pk = cols + LANES

    edge_rows = inputs[rows - HALO :]
    shared_own = lax.dynamic_slice_in_dim(shared_weight, z * ns, ns, 1)
    blank = jnp.zeros((per, LANES - ns - 2 * own), BF16)
    pack1 = jnp.concatenate([value_weight, shared_own, step_weight[:, 0], step_weight[:, 1], blank], axis=1)
    pack2 = jnp.concatenate([gate_weight, output_weight.T], axis=1)

    ogain = output_gain.reshape(1, inner)
    gain = input_gain.reshape(1, width)
    normed, normed_t, cot_t, params, sk = call(
        functools.partial(prep_kernel, cfg),
        (
            sds((rows, width), BF16), sds((width, rows), BF16), sds((width, rows), BF16), sds((8, LANES)),
            sds((4, 8, LANES)),
        ),
        scratch=[pltpu.VMEM((8, LANES), F32)],
        us=3.0,
    )(
        ids, inputs, cotangent, gain, step_bias, decay_log.reshape(1, heads), skip_gain.reshape(1, heads),
        shared_kernel,
    )

    if fast:
        line1 = gather_line(pack1, shares)
        pack2 = jnp.concatenate([pack2, edge_rows], axis=0)
        line2 = [pack2] + [along(after(pack2, line1), d, shares) for d in range(1, shares)]
        halo = line2[1][per:]
        near1 = gather_layer(line1, groups)
        line2 = after(line2, *near1)
        line2 = jnp.stack([block[:per] for block in line2])
        near1, params, sk, ogain, gain, ids, normed, normed_t, cot_t = lax.optimization_barrier(
            (near1, params, sk, ogain, gain, ids, normed, normed_t, cot_t)
        )
        parts1 = gather_pair(near1, groups)
        near2 = gather_layer(after(line2, *near1), groups)
    else:
        parts1, parts2 = gather_any(pack1), gather_any(pack2)
        halo = along(edge_rows, 1, shares)

    full = sds((rows, inner), BF16)
    (
        w1, ws, ahead, vext, u, x, wide, side, su, bc, cct, c2, rho2, c2t, rho2t, dec, states, tots, spread,
        *pays,
    ) = call(
        functools.partial(front_kernel, cfg),
        (
            sds((width, inner), BF16),
            sds((width, shares * LANES), BF16),
            sds((HALO, width), BF16),
            sds((ext, inner), BF16),
            full,
            full,
            sds((2, rows, inner), BF16),
            sds((shares, ext, LANES)),
            sds((4, rows, LANES)),
            sds((4, rows, LANES), BF16),
            sds((blocks, 2 * ns, 2 * SPAN), BF16),
            sds((rows, LANES)),
            sds((rows, LANES)),
            sds((blocks, LANES, SPAN)),
            sds((blocks, LANES, SPAN)),
            sds((4, rows, LANES)),
            sds((blocks, 2 * ns, inner), BF16),
            sds((2 * blocks, LANES)),
            sds((2, LANES, inner), BF16),
            *[sds((shares * ns + HALO, cols), BF16)] * 3,
        ),
        scratch=[
            pltpu.VMEM((ext, inner), F32),
            pltpu.VMEM((blocks, 2 * ns, 2 * SPAN), BF16),
            pltpu.VMEM((2 * SPAN, inner), BF16),
        ],
        us=12.0,
        limit=13 * MB,
    )(ids, halo, normed, gain, value_kernel, sk, params, *parts1)
    got = spread_out(pays, shares)

    yin = call(functools.partial(within_kernel, cfg), full, us=5.0)(
        ids, bc, c2, rho2t, x
    )
    if fast:
        parts2 = gather_pair(after(near2, yin, got[1], got[2]), groups)
    wg, wo, gate, gn_out = call(
        functools.partial(gate_kernel, cfg),
        (sds((width, inner), BF16), sds((width, inner), BF16), full, full),
        us=6.0,
    )(ids, normed, cotangent, *parts2)

    enter, dy, normal, dgate, dcarry, rr, dlocal, rowsum, keeps, *pays = call(
        functools.partial(middle_kernel, cfg),
        (
            sds((blocks, 2 * ns, inner), BF16),
            full,
            full,
            full,
            sds((2, rows, ns)),
            sds((rows, LANES)),
            sds((blocks, 2 * ns, inner), BF16),
            sds((2, 8, inner)),
            sds((3, HALO, inner)),
            *[sds((shares * ns, cols), BF16)] * 3,
        ),
        scratch=[
            pltpu.VMEM((2, rows, inner), BF16),
            pltpu.VMEM((SPAN, inner), F32),
            pltpu.VMEM((SPAN, inner), F32),
            pltpu.VMEM((2, SPAN, inner), F32),
            pltpu.VMEM((2 * SPAN, inner), BF16),
            pltpu.VMEM((2, rows, inner), BF16),
        ],
        us=12.0,
        limit=16 * MB,
    )(ids, yin, x, gate, gn_out, states, bc, cct, dec, tots, spread, params, ogain, *got)
    got = spread_out(pays, shares)

    def piece_shapes(c):
        if fast:
            return (sds((groups // 2, shares, per, c), BF16),) * 2
        return (sds((shares, width, c), BF16),)

    mixed, gx, *grads2 = call(
        functools.partial(output_kernel, cfg),
        (sds((rows, width), BF16), sds((rows, width))) + piece_shapes(2 * cols),
        scratch=[pltpu.VMEM((width, inner), BF16)] * 2,
        us=7.0,
        limit=9 * MB,
    )(ids, inputs, cot_t, normed_t, normal, dgate, wg, wo)
    dy_late = dy
    if fast:
        pairs2 = scatter_pair(cfg, ids, *grads2)
        dy_late = after(dy, pairs2)

    dxi, dbc, da, dk = call(
        functools.partial(back_within_kernel, cfg),
        (full, sds((4, rows, LANES)), sds((rows, LANES)), sds((rows, LANES))),
        scratch=[pltpu.VMEM((LANES, SPAN), F32), pltpu.VMEM((LANES, SPAN), F32)],
        us=9.0,
    )(ids, bc, rho2, c2t, x, dy_late, dcarry, rr, keeps)
    if fast:
        layer2 = scatter_layer(groups, pairs2)

    dp, dps, small = call(
        functools.partial(tail_kernel, cfg),
        (sds((ext, inner), BF16), sds((ext, shares * LANES), BF16), sds((small_rows, LANES))),
        scratch=[
            pltpu.VMEM((ext + HALO, inner), F32),
            pltpu.VMEM((4, ext + HALO, LANES), F32),
            pltpu.VMEM((4, rows, LANES), F32),
            pltpu.VMEM((blocks, 2 * ns, inner), BF16),
            pltpu.VMEM((8, LANES), F32),
            pltpu.VMEM((rows, LANES), F32),
            pltpu.VMEM((2, SPAN, inner), F32),
            pltpu.VMEM((2, SPAN, inner), BF16),
            pltpu.VMEM((2, rows, inner), BF16),
        ],
        us=13.0,
        limit=17 * MB,
    )(
        ids, x, u, dxi, wide, vext, side, su, bc, dbc, dec, enter, da, dk, dlocal, rowsum, keeps, spread,
        *got, value_kernel, sk,
    )
    gn, small, *grads1 = call(
        functools.partial(last_kernel, cfg),
        (sds((ext, width)), sds((small_rows, LANES))) + piece_shapes(pk),
        scratch=[pltpu.VMEM((width, inner), BF16), pltpu.VMEM((width, shares * LANES), BF16)],
        us=6.0,
        limit=9 * MB,
    )(ids, halo, inputs, ahead, normed_t, dp, dps, w1, ws, gx, small)
    first_rows = gn[:HALO]
    if fast:
        small, *pairs1 = scatter_pair(cfg, ids, *after(grads1, *layer2), small)
        blocks2 = layer_sum(cfg, ids, layer2, False)
        layer1 = scatter_layer(groups, pairs1)
        line2 = scatter_line(shares, blocks2)
        small, first_rows, line2 = after((small, first_rows, line2), layer1[1])
        grad_gate, grad_output = call(
            functools.partial(line2_kernel, cfg), (sds((per, cols)), sds((per, cols))), us=1.0
        )(ids, *line2)
        last_parts = scatter_line(shares, layer_sum(cfg, ids, layer1, True))
        steps = [("dp", groups, b) for b in range(1, groups.bit_length() - 1)]
        steps += [("tensor", shares, b) for b in range(shares.bit_length() - 1)]
        for axis, size, b in steps:
            mine, theirs = small, lax.ppermute(small, axis, xor(size, 1 << b))
            small = mine + theirs
        last_parts = after(last_parts, theirs)
        grad_value, grad_step, grad_shared = call(
            functools.partial(line_kernel, cfg),
            (sds((per, cols)), sds((per, 2 * own)), sds((per, shares * ns))),
            scratch=[pltpu.VMEM((shares, per, 2 * cols), F32)],
            us=15.0,
        )(ids, *last_parts)

    else:
        out1, out2 = scatter_any(grads1), scatter_any(grads2)
        grad_gate, grad_output = out2[:, :cols], out2[:, cols:]
        grad_value, grad_step = out1[:, :cols], out1[:, cols + ns : cols + ns + 2 * own]
        grad_shared = lax.all_gather(out1[:, cols : cols + ns], "tensor", axis=1, tiled=True)
        mine = lax.psum(small, ("dp", "tensor"))
        theirs = jnp.zeros_like(mine)

    edge = lax.ppermute(first_rows, "tensor", [(i + 1, i) for i in range(shares - 1)])
    grad_input = call(functools.partial(finish_kernel, cfg), sds((rows, width), BF16), us=2.0)(
        ids, inputs, cotangent, gain, gn, edge
    )

    vkernel, skernel, bias, decay, skip, ingain, outgain = call(
        functools.partial(small_kernel, cfg),
        (
            sds((TAPS, inner)), sds((TAPS, 4 * ns)), sds((2, heads)), sds((1, heads)), sds((1, heads)),
            sds((1, width)), sds((1, inner)),
        ),
        scratch=[pltpu.VMEM((small_rows, LANES), F32)],
        us=1.0,
    )(ids, mine, theirs)
    return (
        mixed,
        grad_input,
        grad_gate,
        grad_value,
        grad_step.reshape(per, 2, own),
        grad_shared,
        grad_output.T,
        vkernel,
        skernel,
        bias,
        decay.reshape(heads),
        skip.reshape(heads),
        ingain.reshape(width),
        outgain.reshape(inner),
    )


def solution(mesh):
    both = P(("dp", "tensor"), None)
    placed = (
        both, P("dp", "tensor"), P("dp", "tensor"), P("dp", None, "tensor"), P("dp", None),
        P("tensor", "dp"), P(), P(), P(), P(), P(), P(), P(), both,
    )
    return jax.shard_map(
        shards,
        mesh=mesh,
        in_specs=placed,
        out_specs=(
            both, both, P("dp", "tensor"), P("dp", "tensor"), P("dp", None, "tensor"), P("dp", None),
            P("tensor", "dp"), P(), P(), P(), P(), P(), P(), P(),
        ),
        check_vma=False,
    )
```

```python
import functools

import jax
import jax.numpy as jnp
from jax import lax
from jax.experimental import pallas as pl
from jax.experimental.pallas import tpu as pltpu
from jax.sharding import PartitionSpec as P

F32 = jnp.float32
BF16 = jnp.bfloat16
EPSILON = 1e-06
SPAN = 128
HALO = 16
TAPS = 4
LANES = 128
LOG2E = 1.4426950408889634
EXACT = lax.Precision.HIGHEST
LIMIT = 4 * 1024 * 1024
MB = 1024 * 1024

NN = (((1,), (0,)), ((), ()))
NT = (((1,), (1,)), ((), ()))
TN = (((0,), (0,)), ((), ()))


def mm(a, b, dims=NN, precision=None):
    return lax.dot_general(a, b, dims, preferred_element_type=F32, precision=precision)


def iota(shape, dim):
    return lax.broadcasted_iota(jnp.int32, shape, dim)


def sigmoid(v):
    return 0.5 * jnp.tanh(0.5 * v) + 0.5


def split(v, n):
    parts = []
    for _ in range(n):
        part = v.astype(BF16)
        parts.append(part)
        v = v - part.astype(F32)
    return parts


def mm_right(ones, v, n):
    total = None
    for part in split(v, n):
        term = mm(ones, part)
        total = term if total is None else total + term
    return total


def mm_left(v, ones, n, dims=(((1,), (0,)), ((), ()))):
    total = None
    for part in split(v, n):
        term = mm(part, ones, dims)
        total = term if total is None else total + term
    return total


def fold(v):
    return v.reshape(v.shape[0] // 8, 8, v.shape[1]).sum(axis=0)


def chunk_rows(c, base=0):
    return pl.ds(base + c * SPAN, SPAN)


def call(kernel, out_shape, scratch=(), us=1.0, limit=LIMIT):
    def run(*args):
        specs = [
            pl.BlockSpec(memory_space=pltpu.SMEM if i == 0 else pltpu.VMEM)
            for i in range(len(args))
        ]
        return pl.pallas_call(
            kernel,
            out_shape=out_shape,
            in_specs=specs,
            out_specs=jax.tree.map(lambda _: pl.BlockSpec(memory_space=pltpu.VMEM), out_shape),
            scratch_shapes=list(scratch),
            cost_estimate=pl.CostEstimate(
                flops=int(us * 1.1e9), bytes_accessed=int(us * 3.0e6), transcendentals=0
            ),
            compiler_params=pltpu.CompilerParams(vmem_limit_bytes=limit),
        )(*args)

    return run


def sds(shape, dtype=F32):
    return jax.ShapeDtypeStruct(shape, dtype)


def put_weights(ids, pieces, outs, shares, per):
    for rel, piece in enumerate(pieces):
        for d in range(shares):
            start = 0
            for out in outs:
                width = out.shape[1] // shares
                if len(pieces) == 1:
                    out[:, d * width : (d + 1) * width] = piece[d, :, start : start + width]
                else:
                    row = pl.multiple_of((ids[1] ^ rel) * per, per)
                    col = pl.multiple_of((ids[0] + shares - d) % shares * width, LANES)
                    out[pl.ds(row, per), pl.ds(col, width)] = piece[d, :, start : start + width]
                start += width


def take_grads(ids, pieces, held, shares, per):
    n = 2 * pieces[0].shape[0] if len(pieces) > 1 else 1
    for rel in range(n):
        for d in range(shares):
            start = 0
            for part in held:
                width = part.shape[1] // shares
                if n == 1:
                    pieces[0][d, :, start : start + width] = part[:, d * width : (d + 1) * width]
                else:
                    row = pl.multiple_of((ids[1] ^ rel) * per, per)
                    col = pl.multiple_of((ids[0] + shares - d) % shares * width, LANES)
                    pieces[rel % 2][rel // 2, d, :, start : start + width] = part[pl.ds(row, per), pl.ds(col, width)]
                start += width


def blocks_of(total, size):
    return [slice(i, min(i + size, total)) for i in range(0, total, size)]


def cyclic(size, d):
    return [(i, (i + d) % size) for i in range(size)]


def xor(size, bit):
    return [(i, i ^ bit) for i in range(size)]


def along(v, d, shares):
    return lax.ppermute(v, "tensor", cyclic(shares, d))


def spread_out(parts, shares):
    return [along(part, d + 1, shares) for d, part in enumerate(parts)]


def after(values, *others):
    out = lax.optimization_barrier((values,) + others)
    return out[0]


def pair_kernel(n, ids, keep, other, *refs):
    for k in range(n):
        refs[len(refs) - n + k][...] = (keep[k].astype(F32) + other[k].astype(F32)).astype(BF16)
    if len(refs) > n:
        mine, theirs, total = refs[:3]
        total[...] = mine[...] + theirs[...]


def quad_kernel(cfg, first, ids, *refs):
    n, shares, cols, ns = cfg["groups"] // 2, cfg["shares"], cfg["cols"], cfg["state"]
    parts, outs, held = refs[:n], refs[n:-1], refs[-1]
    for d in range(shares):
        q = (ids[0] + shares - d) % shares
        total = parts[0][d].astype(F32)
        for part in parts[1:]:
            total = total + part[d].astype(F32)
        if first:
            outs[d][:, :cols] = total[:, :cols].astype(BF16)
            held[q] = total[:, cols:]
        else:
            outs[d][...] = total.astype(BF16)
    if first:
        low = iota((outs[0].shape[0], LANES), 1) < ns
        for k in range(shares // 2):
            both = jnp.where(low, held[2 * k], pltpu.roll(held[2 * k + 1], ns, 1)).astype(BF16)
            for out in outs:
                out[:, cols + k * LANES : cols + (k + 1) * LANES] = both
        for d, out in enumerate(outs):
            step = held[(ids[0] + shares - d) % shares]
            out[:, cols + shares * ns :] = jnp.where(low, pltpu.roll(step, LANES - ns, 1), 0.0).astype(BF16)


def line_kernel(cfg, ids, *refs):
    shares, cols, ns = cfg["shares"], cfg["cols"], cfg["state"]
    parts, (value, step, shared, held) = refs[:shares], refs[shares:]
    for e, part in enumerate(parts):
        held[e] = part[...].astype(F32)
    total = held[(shares - ids[0]) % shares]
    for q in range(1, shares):
        total = total + held[(q + shares - ids[0]) % shares]
    value[...] = total[:, :cols]
    shared[...] = total[:, cols : cols + shares * ns]
    step[...] = total[:, cols + shares * ns :][:, : step.shape[1]]


def line2_kernel(cfg, ids, *refs):
    shares, cols = cfg["shares"], cfg["cols"]
    parts, (gate, out) = refs[:shares], refs[shares:]
    total = parts[0][...].astype(F32)
    for part in parts[1:]:
        total = total + part[...].astype(F32)
    gate[...] = total[:, :cols]
    out[...] = total[:, cols:]


def fill_spread(cfg, spread):
    own, head = cfg["own"], cfg["head"]
    block = own * head
    for j in range(cfg["shares"]):
        lane = iota((LANES, block), 0)
        place = iota((LANES, block), 1) // head
        for d in range(2):
            cols = slice(j * block, (j + 1) * block)
            spread[d, :, cols] = (lane == own * (2 * j + d) + place).astype(F32).astype(BF16)


def prep_kernel(cfg, ids, inputs, cot, gain, bias, decay, skip, taps, normed, normed_t, cot_t, params, sk, raw):
    own, ns = cfg["own"], cfg["state"]
    heads = own * cfg["shares"]
    size = SPAN // 2
    for c in range(inputs.shape[0] // size):
        at = pl.ds(c * size, size)
        wide = inputs[at, :].astype(F32)
        scale = lax.rsqrt(jnp.mean(wide * wide, axis=1, keepdims=True) + EPSILON)
        normed[at, :] = (wide * scale * gain[...]).astype(BF16)
    normed_t[...] = normed[...].T
    cot_t[...] = cot[...].T
    raw[...] = jnp.zeros_like(raw)
    raw[0:2, :heads] = bias[...]
    raw[2:3, :heads] = decay[...]
    raw[3:4, :heads] = skip[...]
    h, lane = iota((LANES, LANES), 0), iota((LANES, LANES), 1)
    fwd, bwd = (
        mm_left(
            raw[...],
            ((h < heads) & (lane == 2 * own * (h // own) + own * d + h % own)).astype(F32).astype(BF16),
            3,
        )
        for d in range(2)
    )
    params[...] = jnp.zeros_like(params)
    params[0:1, :] = fwd[0:1, :] + bwd[1:2, :]
    params[1:2, :] = fwd[2:3, :] + bwd[2:3, :]
    params[2:3, :] = fwd[3:4, :] + bwd[3:4, :]
    low = iota((8, LANES), 1) < ns
    for k in range(4):
        raw[...] = jnp.zeros_like(raw)
        raw[0:TAPS, :] = taps[:, k // 2 * LANES : (k // 2 + 1) * LANES]
        v = raw[...]
        sk[k] = jnp.where(low, pltpu.roll(v, LANES - ns, 1) if k % 2 else v, 0.0)


def small_kernel(cfg, ids, mine, theirs, vkernel, skernel, bias, decay, skip, ingain, outgain, held):
    own, ns, shares = cfg["own"], cfg["state"], cfg["shares"]
    heads = own * shares
    held[...] = mine[...] + theirs[...]
    n = outgain.shape[1] // LANES
    for k in range(n):
        lanes = slice(k * LANES, (k + 1) * LANES)
        for m in range(TAPS):
            vkernel[m : m + 1, lanes] = held[m * n + k : m * n + k + 1, :]
        outgain[:, lanes] = held[cfg["gain_row"] + k : cfg["gain_row"] + k + 1, :]
    for k in range(ingain.shape[1] // LANES):
        row = cfg["input_row"] + k
        ingain[:, k * LANES : (k + 1) * LANES] = held[row : row + 1, :]
    low = iota((1, LANES), 1) < ns
    for m in range(TAPS):
        for k in range(2):
            row = cfg["state_row"] + 4 * m + 2 * k
            both = held[row : row + 2, :]
            odd = jnp.concatenate([both] * 4, axis=0)
            odd = pltpu.roll(odd, ns, 1)[1:2, :]
            skernel[m : m + 1, k * LANES : (k + 1) * LANES] = jnp.where(low, both[0:1, :], odd)
    rest = held[cfg["rest_row"] : cfg["rest_row"] + 8, :]
    lane, h = iota((LANES, LANES), 0), iota((LANES, LANES), 1)
    fwd, bwd = (
        mm_left(
            rest,
            ((h < heads) & (lane == 2 * own * (h // own) + own * d + h % own)).astype(F32).astype(BF16),
            3,
        )
        for d in range(2)
    )
    bias[0:1, :] = fwd[0:1, :heads]
    bias[1:2, :] = bwd[0:1, :heads]
    decay[...] = fwd[1:2, :heads] + bwd[1:2, :heads]
    skip[...] = fwd[2:3, :heads]


def front_kernel(cfg, *refs):
    n = cfg["pieces"]
    ids, halo, normed, gain, vk, sk, params = refs[:7]
    pieces = refs[7 : 7 + n]
    (
        w1, ws, ahead, vext, u_out, x_out, wide_out, side, su_out, bc_out, cct, c2, rho2, c2t, rho2t, dec, states,
        tots, spread, pay1, pay2, pay3, acc, bbt, xw,
    ) = refs[7 + n :]
    shares, own, cols, rows, ns = (cfg[k] for k in ("shares", "own", "cols", "rows", "state"))
    blocks, pages = rows // SPAN, cols // LANES
    put_weights(ids, pieces, (w1, ws), shares, cfg["per"])
    fill_spread(cfg, spread)

    edge = halo[...].astype(F32)
    scale = lax.rsqrt(jnp.mean(edge * edge, axis=1, keepdims=True) + EPSILON)
    ahead[...] = jnp.where(ids[0] > 0, edge * scale * gain[...], 0.0).astype(BF16)
    bbt[...] = jnp.zeros_like(bbt)
    cct[...] = jnp.zeros_like(cct)

    for part in blocks_of(shares * cols, 512):
        acc[0:HALO, part] = mm(ahead[...], w1[:, part])
        acc[HALO:, part] = mm(normed[...], w1[:, part])
    sides, edge = mm(normed[...], ws[...]), mm(ahead[...], ws[...])
    for j in range(shares):
        side[j, :HALO, :] = edge[:, j * LANES : (j + 1) * LANES]
        side[j, HALO:, :] = sides[:, j * LANES : (j + 1) * LANES]
    for j in range(shares):
        here = slice(j * cols, (j + 1) * cols)
        for c in range(blocks):
            vext[chunk_rows(c), here] = acc[chunk_rows(c), here].astype(BF16)
        vext[blocks * SPAN :, here] = acc[blocks * SPAN :, here].astype(BF16)
        for c in range(blocks):
            for p in range(pages + 1):
                here = slice(j * cols + p * LANES, j * cols + (p + 1) * LANES)
                u = None
                for m in range(TAPS):
                    rows_m = chunk_rows(c, HALO - TAPS + 1 + m)
                    if p < pages:
                        term = vk[m : m + 1, here] * acc[rows_m, here]
                    else:
                        term = sk[j, m : m + 1, :] * side[j, rows_m, :]
                    u = term if u is None else u + term
                v = u * sigmoid(u)
                if p < pages:
                    u_out[chunk_rows(c), here] = u.astype(BF16)
                    x_out[chunk_rows(c), here] = v.astype(BF16)
                else:
                    su_out[j, chunk_rows(c), :] = u
                    bc_out[j, chunk_rows(c), :] = v.astype(BF16)
                    turned = v.T[:ns].astype(BF16)
                    d = j // 2
                    target = cct if j % 2 else bbt
                    target[c, d * ns : (d + 1) * ns, d * SPAN : (d + 1) * SPAN] = turned

    lane = iota((SPAN, LANES), 1)
    is_fwd = lane % (2 * own) < own
    at0, at1 = iota((SPAN, SPAN), 0), iota((SPAN, SPAN), 1)
    both = jnp.concatenate([(at0 >= at1).astype(F32), (at0 <= at1).astype(F32)], axis=0).astype(BF16)
    rate = jnp.where(iota((1, LANES), 1) < 2 * own * shares, -jnp.exp(params[1:2, :]), 0.0)
    for c in range(blocks):
        raw = jnp.zeros((SPAN, LANES), F32)
        for j in range(shares):
            moved = pltpu.roll(side[j, chunk_rows(c, HALO), :], (2 * own * j - ns) % LANES, 1)
            raw = jnp.where((lane >= 2 * own * j) & (lane < 2 * own * (j + 1)), moved, raw)
        v = raw + params[0:1, :]
        small = jnp.exp(jnp.minimum(v, 0.0))
        dt = jnp.where(v < -15.0, small, jnp.maximum(v, 0.0) + jnp.log1p(jnp.exp(-jnp.abs(v))))
        log_dt = jnp.where(v < -15.0, v, jnp.log(jnp.maximum(dt, 1e-30)))
        ratio = jnp.where(v < -15.0, 1.0, sigmoid(v) / jnp.maximum(dt, 1e-30))
        a = dt * rate
        sums = mm_right(both, a, 3)
        cum = jnp.where(is_fwd, sums[:SPAN], sums[SPAN:])
        tot = jnp.sum(a, axis=0, keepdims=True)
        rho = cum - log_dt
        cc = cum * LOG2E
        rr = rho * LOG2E
        c2[chunk_rows(c), :] = cc
        rho2[chunk_rows(c), :] = rr
        c2t[c] = cc.T
        rho2t[c] = rr.T
        dec[0, chunk_rows(c), :] = a
        dec[1, chunk_rows(c), :] = ratio
        dec[2, chunk_rows(c), :] = jnp.exp(tot - rho)
        dec[3, chunk_rows(c), :] = jnp.exp(cum)
        tots[c : c + 1, :] = tot
    fwd1 = iota((1, LANES), 1) % (2 * own) < own
    zero = jnp.zeros((1, LANES), F32)
    lead = []
    for c in range(blocks):
        later, sooner = zero, zero
        for k in range(blocks):
            if k > c:
                later = later + tots[k : k + 1, :]
            if k < c:
                sooner = sooner + tots[k : k + 1, :]
        lead.append(jnp.exp(jnp.where(fwd1, later, sooner)))
        tots[blocks + c : blocks + c + 1, :] = jnp.where(fwd1, sooner, later)
    lead = jnp.concatenate(lead + [zero] * (8 - blocks), axis=0)
    whole = tots[0:1, :]
    for c in range(1, blocks):
        whole = whole + tots[c : c + 1, :]
    extra = jnp.concatenate([p.astype(F32) for p in split(whole, 3)] + [zero] * (HALO - 3), axis=0)
    extra = jnp.concatenate([extra, jnp.zeros((HALO, cols - LANES), F32)], axis=1).astype(BF16)
    for pay in (pay1, pay2, pay3):
        pay[shares * ns :, :] = extra

    weights = dec[2].astype(BF16)
    for d in range(2):
        wide_out[d] = mm(weights, spread[d]).astype(BF16)
    grow_f, grow_b = mm_left(lead, spread[0], 2), mm_left(lead, spread[1], 2)
    for c in range(blocks):
        for d in range(2):
            for p in range(shares * pages):
                lanes = slice(p * LANES, (p + 1) * LANES)
                product = wide_out[d, chunk_rows(c), lanes].astype(F32) * x_out[chunk_rows(c), lanes].astype(F32)
                xw[d * SPAN : (d + 1) * SPAN, lanes] = product.astype(BF16)
        states[c] = mm(bbt[c], xw[...]).astype(BF16)
    for j in range(shares):
        at = slice(j * ns, (j + 1) * ns)
        here = slice(j * cols, (j + 1) * cols)
        f, b = jnp.zeros((ns, cols), F32), jnp.zeros((ns, cols), F32)
        for c in range(blocks):
            f = f + grow_f[c : c + 1, here] * states[c, :ns, here].astype(F32)
            b = b + grow_b[c : c + 1, here] * states[c, ns:, here].astype(F32)
        for dist, pay in ((1, pay1), (2, pay2), (3, pay3)):
            pay[at, :] = jnp.where(ids[0] + dist < shares, f, b).astype(BF16)


def stack_pair(first, v):
    zero = jnp.zeros_like(v)
    return jnp.concatenate([jnp.where(first, v, zero), jnp.where(first, zero, v)], axis=0)


def within_kernel(cfg, ids, bc, c2, rho2t, x, y):
    shares, own, rows = (cfg[k] for k in ("shares", "own", "rows"))
    t, s = iota((SPAN, SPAN), 0), iota((SPAN, SPAN), 1)
    low = t > s
    first = iota((SPAN, LANES), 1) < cfg["head"]

    def block(c, _):
        at = pl.ds(pl.multiple_of(c * SPAN, SPAN), SPAN)
        g = jnp.where(low, mm(bc[1, at, :], bc[0, at, :], NT), mm(bc[3, at, :], bc[2, at, :], NT))
        g = jnp.where(t == s, 0.0, g)
        cc = c2[at, :]
        for k in range(shares * own // 2):
            j, p = k // (own // 2), k % (own // 2)
            mats = []
            for i in (2 * p, 2 * p + 1):
                f, b = 2 * own * j + i, 2 * own * j + own + i
                col = jnp.where(low, cc[:, f : f + 1], cc[:, b : b + 1])
                row = jnp.where(low, rho2t[c, f : f + 1, :], rho2t[c, b : b + 1, :])
                mats.append((jnp.exp2(col - row) * g).astype(BF16))
            lanes = slice(k * LANES, (k + 1) * LANES)
            y[at, lanes] = mm(jnp.concatenate(mats, axis=1), stack_pair(first, x[at, lanes])).astype(BF16)
        return 0

    lax.fori_loop(0, rows // SPAN, block, 0)


def gate_kernel(cfg, *refs):
    n = cfg["pieces"]
    ids, normed, cot = refs[:3]
    pieces = refs[3 : 3 + n]
    wg, wo, gate, gn = refs[3 + n :]
    put_weights(ids, pieces, (wg, wo), cfg["shares"], cfg["per"])
    for part in blocks_of(gate.shape[1], 512):
        gate[:, part] = mm(normed[...], wg[:, part]).astype(BF16)
        gn[:, part] = mm(cot[...], wo[:, part]).astype(BF16)


def incoming(ids, cfg, got, j, near, far):
    z, shares, ns = ids[0], cfg["shares"], cfg["state"]
    r1, r2, r3 = (part[j * ns : (j + 1) * ns, :].astype(F32) for part in got)

    def keep(test, v):
        return jnp.where(test, v, 0.0)

    before = keep(z >= 1, r1) + near[0] * keep(z >= 2, r2) + near[1] * keep(z >= 3, r3)
    behind = (
        keep(z <= shares - 2, r3)
        + far[0] * keep(z <= shares - 3, r2)
        + far[1] * keep(z <= shares - 4, r1)
    )
    return before, behind


def middle_kernel(cfg, *refs):
    (
        ids, yin, x, gate, gn, states, bc, cct, dec, tots, spread, params, ogain, r1, r2, r3,
        enter, dy, normal, dgate, dcarry, rr, dlocal, rowsum, keeps, p1, p2, p3,
        ecx, ys, acts, kept, edy, prod,
    ) = refs
    shares, cols, rows, ns = (cfg[k] for k in ("shares", "cols", "rows", "state"))
    blocks, inner = rows // SPAN, cols * shares
    pages = inner // LANES
    zero = jnp.zeros((1, LANES), F32)

    def whole(r):
        v = r[shares * ns :, :LANES].astype(F32)
        return v[0:1, :] + v[1:2, :] + v[2:3, :]

    l1, l2, l3 = whole(r1), whole(r2), whole(r3)
    lines = [tots[c : c + 1, :] for c in range(2 * blocks)] + [l1, l1 + l2, l3, l3 + l2]
    lines = jnp.exp(jnp.concatenate(lines + [zero] * (HALO - len(lines)), axis=0))
    skip_rows = jnp.concatenate([params[2:3, :]] + [zero] * 7, axis=0)
    for d in range(2):
        keeps[d] = mm_left(lines, spread[d], 2)
        ecx[d] = mm(dec[3].astype(BF16), spread[d]).astype(BF16)
    keeps[2, 0:8] = mm_left(skip_rows, spread[0], 2)
    b = 2 * blocks
    for j in range(shares):
        here = slice(j * cols, (j + 1) * cols)
        kf, kb = keeps[0, :, here], keeps[1, :, here]
        e, e_b = incoming(
            ids, cfg, (r1, r2, r3), j,
            (kf[b : b + 1, :], kf[b + 1 : b + 2, :]), (kb[b + 2 : b + 3, :], kb[b + 3 : b + 4, :]),
        )
        for c in range(blocks):
            enter[c, :ns, here] = e.astype(BF16)
            e = kf[c : c + 1, :] * e + states[c, :ns, here].astype(F32)
        for c in reversed(range(blocks)):
            enter[c, ns:, here] = e_b.astype(BF16)
            e_b = kb[c : c + 1, :] * e_b + states[c, ns:, here].astype(F32)
    rowsum[...] = jnp.zeros_like(rowsum)

    def block(c, _):
        at = pl.ds(pl.multiple_of(c * SPAN, SPAN), SPAN)
        for d in range(2):
            kept[d] = mm(bc[1 + 2 * d, at, :ns], enter[c, d * ns : (d + 1) * ns, :])
        square, dot = jnp.zeros((SPAN, LANES), F32), jnp.zeros((SPAN, LANES), F32)
        for p in range(pages):
            lanes = slice(p * LANES, (p + 1) * LANES)
            cf = kept[0, :, lanes] * ecx[0, at, lanes].astype(F32)
            cb = kept[1, :, lanes] * ecx[1, at, lanes].astype(F32)
            kept[0, :, lanes] = cf
            kept[1, :, lanes] = cb
            v = yin[at, lanes].astype(F32) + keeps[2, 0:1, lanes] * x[at, lanes].astype(F32) + cf + cb
            ys[:, lanes] = v
            g = gate[at, lanes].astype(F32)
            act = g * sigmoid(g)
            acts[:, lanes] = act
            gated = v * act
            square = square + gated * gated
            dot = dot + gn[at, lanes].astype(F32) * ogain[:, lanes] * gated
        square = jnp.sum(square, axis=1, keepdims=True)
        dot = jnp.sum(dot, axis=1, keepdims=True)
        inv = lax.rsqrt(square / inner + EPSILON)
        back = inv * inv * inv * dot / inner
        for p in range(pages):
            lanes = slice(p * LANES, (p + 1) * LANES)
            v, act, g = ys[:, lanes], acts[:, lanes], gate[at, lanes].astype(F32)
            gnv, og = gn[at, lanes].astype(F32), ogain[:, lanes]
            sig = sigmoid(g)
            gated = v * act
            scaled = gated * inv
            normal[at, lanes] = (scaled * og).astype(BF16)
            rowsum[0, :, lanes] += fold(gnv * scaled)
            dgated = inv * (gnv * og) - gated * back
            d_scan = dgated * act
            dy[at, lanes] = d_scan.astype(BF16)
            dgate[at, lanes] = (dgated * v * (sig + act * (1.0 - sig))).astype(BF16)
            rowsum[1, :, lanes] += fold(d_scan * x[at, lanes].astype(F32))
            for d in range(2):
                prod[d, at, lanes] = (d_scan * kept[d, :, lanes]).astype(BF16)
                wide = ecx[d, at, lanes].astype(F32) * d_scan
                edy[d * SPAN : (d + 1) * SPAN, lanes] = wide.astype(BF16)
        dlocal[c] = mm(cct[c], edy[...]).astype(BF16)
        for d in range(2):
            dcarry[d, at, :] = mm(edy[d * SPAN : (d + 1) * SPAN, :], enter[c, d * ns : (d + 1) * ns, :], NT)
        return 0

    lax.fori_loop(0, blocks, block, 0)
    rr[...] = mm(prod[0], spread[0], NT) + mm(prod[1], spread[1], NT)

    for j in range(shares):
        here = slice(j * cols, (j + 1) * cols)
        f, b_ = jnp.zeros((ns, cols), F32), jnp.zeros((ns, cols), F32)
        for c in range(blocks):
            f = f + keeps[0, blocks + c : blocks + c + 1, here] * dlocal[c, :ns, here].astype(F32)
            b_ = b_ + keeps[1, blocks + c : blocks + c + 1, here] * dlocal[c, ns:, here].astype(F32)
        for dist, pay in ((1, p1), (2, p2), (3, p3)):
            pay[j * ns : (j + 1) * ns, :] = jnp.where(ids[0] + dist < shares, b_, f).astype(BF16)


def output_kernel(cfg, *refs):
    ids, cot_t, normed_t, normal, dgate, wg = refs[:6]
    gx = refs[6]
    pieces, held = refs[7:-2], refs[-2:]
    for part in blocks_of(normal.shape[1], 512):
        held[0][:, part] = mm(normed_t[...], dgate[:, part]).astype(BF16)
        held[1][:, part] = mm(cot_t[...], normal[:, part]).astype(BF16)
    take_grads(ids, pieces, held, cfg["shares"], cfg["per"])
    for part in blocks_of(gx.shape[1], 256):
        gx[:, part] = mm(dgate[...], wg[part, :], NT)


def mixed_kernel(ids, inputs, normal, wo, mixed):
    for part in blocks_of(inputs.shape[1], 256):
        mixed[:, part] = (mm(normal[...], wo[part, :], NT) + inputs[:, part].astype(F32)).astype(BF16)


def back_within_kernel(cfg, ids, bc, rho2, c2t, x, dy, dcarry, rr, keeps, dx, dbc, da, dk, das, ras):
    shares, own, rows, ns = (cfg[k] for k in ("shares", "own", "rows", "state"))
    s, t = iota((SPAN, SPAN), 0), iota((SPAN, SPAN), 1)
    up = t > s
    first = iota((SPAN, LANES), 1) < cfg["head"]
    after_t = (s >= t).astype(F32).astype(BF16)
    until_t = (s <= t).astype(F32).astype(BF16)
    tri = jnp.concatenate([after_t, until_t], axis=1)
    sums = jnp.concatenate([until_t, after_t], axis=0)
    lane = iota((SPAN, LANES), 1)
    is_fwd = iota((LANES, SPAN), 0) % (2 * own) < own

    def block(c, _):
        at = pl.ds(pl.multiple_of(c * SPAN, SPAN), SPAN)
        g = jnp.where(up, mm(bc[0, at, :], bc[1, at, :], NT), mm(bc[2, at, :], bc[3, at, :], NT))
        g = jnp.where(t == s, 0.0, g)
        rho = rho2[at, :]
        dg = jnp.zeros((SPAN, SPAN), F32)
        das[...] = jnp.zeros_like(das)
        ras[...] = jnp.zeros_like(ras)
        for k in range(shares * own // 2):
            j, p = k // (own // 2), k % (own // 2)
            lanes = slice(k * LANES, (k + 1) * LANES)
            dyp = dy[at, lanes]
            dm = mm(stack_pair(first, x[at, lanes]), dyp, NT)
            ws, zs = [], []
            for q in range(2):
                i = 2 * p + q
                f, b = 2 * own * j + i, 2 * own * j + own + i
                row = jnp.where(up, c2t[c, f : f + 1, :], c2t[c, b : b + 1, :])
                col = jnp.where(up, rho[:, f : f + 1], rho[:, b : b + 1])
                pw = jnp.exp2(row - col)
                ud = dm[q * SPAN : (q + 1) * SPAN] * pw
                dg = dg + ud
                ws.append((pw * g).astype(BF16))
                zd = ud * g
                zs.append(zd.astype(BF16))
                rf = jnp.sum(jnp.where(up, zd, 0.0), axis=0, keepdims=True)
                ras[f : f + 1, :] = rf
                ras[b : b + 1, :] = jnp.sum(zd, axis=0, keepdims=True) - rf
            back = mm(jnp.concatenate(ws, axis=1), stack_pair(first, dyp))
            dx[at, lanes] = (back + keeps[2, 0:1, lanes] * dyp.astype(F32)).astype(BF16)
            cross = mm(jnp.concatenate(zs, axis=0), tri)
            for q in range(2):
                i = 2 * p + q
                f, b = 2 * own * j + i, 2 * own * j + own + i
                part = cross[q * SPAN : (q + 1) * SPAN]
                das[f : f + 1, :] = jnp.sum(jnp.where(up, part[:, :SPAN], 0.0), axis=0, keepdims=True)
                das[b : b + 1, :] = jnp.sum(jnp.where(t < s, part[:, SPAN:], 0.0), axis=0, keepdims=True)
        df = jnp.where(up, dg, 0.0)
        db = jnp.where(t < s, dg, 0.0)
        dbc[0, at, :] = mm(df.astype(BF16), bc[1, at, :])
        dbc[1, at, :] = mm(df.T.astype(BF16), bc[0, at, :])
        dbc[2, at, :] = mm(db.astype(BF16), bc[3, at, :])
        dbc[3, at, :] = mm(db.T.astype(BF16), bc[2, at, :])
        dbc[1, at, :ns] += dcarry[0, at, :]
        dbc[3, at, :ns] += dcarry[1, at, :]
        a = das[...]
        later = jnp.where(lane < SPAN - 1, pltpu.roll(a, SPAN - 1, 1), 0.0)
        sooner = jnp.where(lane > 0, pltpu.roll(a, 1, 1), 0.0)
        kd = ras[...] - a + jnp.where(is_fwd, later, sooner)
        through = mm_right(sums, rr[at, :], 2)
        da[at, :] = a.T + jnp.where(lane % (2 * own) < own, through[:SPAN], through[SPAN:])
        dk[at, :] = kd.T
        return 0

    lax.fori_loop(0, rows // SPAN, block, 0)


def tail_kernel(cfg, *refs):
    (
        ids, x, u, dxi, wide_in, vext, side, su, bc, dbc, dec, enter, da, dk, dlocal, rowsum, keeps, spread,
        r1, r2, r3, vk, sk,
        dp, dps, small,
        du, dsu, dst, dstate, xs, qs, held, xw, prod,
    ) = refs
    shares, own, cols, rows, ns = (cfg[k] for k in ("shares", "own", "cols", "rows", "state"))
    blocks, inner = rows // SPAN, cols * shares
    pages = inner // LANES

    du[0:HALO, :] = jnp.zeros((HALO, inner), F32)
    du[HALO + rows :, :] = jnp.zeros((HALO, inner), F32)
    dsu[...] = jnp.zeros_like(dsu)

    b = 2 * blocks
    total_x = jnp.zeros((8, LANES), F32)
    for j in range(shares):
        here = slice(j * cols, (j + 1) * cols)
        kf, kb = keeps[0, :, here], keeps[1, :, here]
        now_b, now_f = incoming(
            ids, cfg, (r1, r2, r3), j,
            (kb[b : b + 1, :], kb[b + 1 : b + 2, :]), (kf[b + 2 : b + 3, :], kf[b + 3 : b + 4, :]),
        )
        for d, order, now, kept in (
            (0, list(reversed(range(blocks))), now_f, kf),
            (1, list(range(blocks)), now_b, kb),
        ):
            part = slice(d * ns, (d + 1) * ns)
            rows_x = [None] * blocks
            for c in order:
                dstate[c, part, here] = now.astype(BF16)
                rows_x[c] = kept[c : c + 1, :] * jnp.sum(
                    enter[c, part, here].astype(F32) * now, axis=0, keepdims=True
                )
                now = kept[c : c + 1, :] * now + dlocal[c, part, here].astype(F32)
            rows_x = jnp.concatenate(rows_x + [jnp.zeros((8 - blocks, cols), F32)], axis=0)
            total_x = total_x + mm_left(rows_x, spread[d, :, here], 2, NT)
    xs[...] = total_x

    def states_part(c, _):
        at = pl.ds(pl.multiple_of(c * SPAN, SPAN), SPAN)
        moved = pl.ds(pl.multiple_of(c * SPAN + HALO, HALO), SPAN)
        for d in range(2):
            held[d] = mm(bc[2 * d, at, :ns], dstate[c, d * ns : (d + 1) * ns, :])
        for p in range(pages):
            lanes = slice(p * LANES, (p + 1) * LANES)
            xv = x[at, lanes].astype(F32)
            dx = dxi[at, lanes].astype(F32)
            for d in range(2):
                wide = wide_in[d, at, lanes].astype(F32)
                through = held[d, :, lanes] * wide
                dx = dx + through
                prod[d, at, lanes] = (through * xv).astype(BF16)
                xw[d, :, lanes] = (wide * xv).astype(BF16)
            uv = u[at, lanes].astype(F32)
            sig = sigmoid(uv)
            du[moved, lanes] = dx * (sig + uv * sig * (1.0 - sig))
        for d in range(2):
            dst[2 * d, at, :] = dbc[2 * d, at, :]
            dst[2 * d, at, :ns] += mm(xw[d], dstate[c, d * ns : (d + 1) * ns, :], NT)
            dst[2 * d + 1, at, :] = dbc[2 * d + 1, at, :]
        return 0

    lax.fori_loop(0, blocks, states_part, 0)
    qs[...] = mm(prod[0], spread[0], NT) + mm(prod[1], spread[1], NT)
    parts = [(0, HALO)] + [(HALO + c * SPAN, SPAN) for c in range(blocks)]

    for p in range(pages):
        lanes = slice(p * LANES, (p + 1) * LANES)
        sums = [jnp.zeros((8, LANES), F32) for _ in range(TAPS)]
        for start, size in parts:
            old = vext[pl.ds(start, size), lanes].astype(F32)
            dv = None
            for m in range(TAPS):
                shifted = du[pl.ds(start + TAPS - 1 - m, size), lanes]
                term = vk[m : m + 1, lanes] * shifted
                dv = term if dv is None else dv + term
                sums[m] = sums[m] + fold(old * shifted)
            dp[pl.ds(start, size), lanes] = dv.astype(BF16)
        for m in range(TAPS):
            small[m * pages + p : m * pages + p + 1, :] = jnp.sum(sums[m], axis=0, keepdims=True)
        row = cfg["gain_row"] + p
        small[row : row + 1, :] = jnp.sum(rowsum[0, :, lanes], axis=0, keepdims=True)

    lane = iota((SPAN, LANES), 1)
    is_fwd = lane % (2 * own) < own
    at0, at1 = iota((SPAN, SPAN), 0), iota((SPAN, SPAN), 1)
    both = jnp.concatenate([(at0 > at1).astype(F32), (at0 < at1).astype(F32)], axis=0).astype(BF16)
    dbias = jnp.zeros((1, LANES), F32)
    ddecay = jnp.zeros((1, LANES), F32)
    steps = []
    for c in range(blocks):
        at = chunk_rows(c)
        qv = qs[at, :]
        sums = mm_right(both, qv, 2)
        total = da[at, :] + xs[c : c + 1, :] + jnp.where(is_fwd, sums[:SPAN], sums[SPAN:])
        through = total * dec[0, at, :]
        step = (dk[at, :] + qv + through) * dec[1, at, :]
        step = jnp.where(lane < 2 * own * shares, step, 0.0)
        steps.append(step)
        dbias = dbias + jnp.sum(step, axis=0, keepdims=True)
        ddecay = ddecay + jnp.sum(through, axis=0, keepdims=True)
    base = cfg["rest_row"]
    small[base : base + 1, :] = dbias
    small[base + 1 : base + 2, :] = ddecay
    skips = mm_left(rowsum[1], spread[0], 2, NT)
    small[base + 2 : base + 3, :] = jnp.sum(skips, axis=0, keepdims=True)
    small[base + 3 : base + 8, :] = jnp.zeros((5, LANES), F32)

    for k in range(4):
        for c in range(blocks):
            at = chunk_rows(c)
            uv = su[k, at, :]
            sig = sigmoid(uv)
            dsu[k, chunk_rows(c, HALO), :] = dst[k, at, :] * sig * (1.0 + uv * (1.0 - sig))
        sums = [jnp.zeros((8, LANES), F32) for _ in range(TAPS)]
        for start, size in parts:
            old = side[k, pl.ds(start, size), :]
            dv = None
            for m in range(TAPS):
                shifted = dsu[k, pl.ds(start + TAPS - 1 - m, size), :]
                term = sk[k, m : m + 1, :] * shifted
                dv = term if dv is None else dv + term
                sums[m] = sums[m] + fold(old * shifted)
            if start >= HALO:
                moved = pltpu.roll(steps[(start - HALO) // SPAN], (ns - 2 * own * k) % LANES, 1)
                dv = dv + jnp.where((lane >= ns) & (lane < ns + 2 * own), moved, 0.0)
            dps[pl.ds(start, size), k * LANES : (k + 1) * LANES] = dv.astype(BF16)
        for m in range(TAPS):
            row = cfg["state_row"] + m * 4 + k
            small[row : row + 1, :] = jnp.sum(sums[m], axis=0, keepdims=True)
    small[cfg["input_row"] :, :] = jnp.zeros_like(small[cfg["input_row"] :, :])


def last_kernel(cfg, *refs):
    ids, halo, inputs, ahead, normed_t, dp, dps, w1, ws, gx, small_in = refs[:11]
    gn, small = refs[11:13]
    pieces, held = refs[13:-2], refs[-2:]
    shares, rows, width = cfg["shares"], cfg["rows"], inputs.shape[1]
    for grad, out in ((dp, held[0]), (dps, held[1])):
        for part in blocks_of(grad.shape[1], 512):
            total = mm(normed_t[...], grad[HALO:, part]) + mm(ahead[...], grad[:HALO, part], TN)
            out[:, part] = total.astype(BF16)
    take_grads(ids, pieces, held, shares, cfg["per"])
    for part in blocks_of(width, 256):
        gn[:HALO, part] = mm(dp[:HALO, :], w1[part, :], NT) + mm(dps[:HALO, :], ws[part, :], NT)
        back = mm(dp[HALO:, :], w1[part, :], NT) + mm(dps[HALO:, :], ws[part, :], NT)
        gn[HALO:, part] = back + gx[:, part]

    def plain(block):
        wide = block.astype(F32)
        return wide * lax.rsqrt(jnp.mean(wide * wide, axis=1, keepdims=True) + EPSILON)

    total = fold(jnp.where(ids[0] > 0, gn[0:HALO, :] * plain(halo[...]), 0.0))
    for c in range(rows // SPAN):
        total = total + fold(gn[chunk_rows(c, HALO), :] * plain(inputs[chunk_rows(c), :]))
    total = jnp.sum(total, axis=0, keepdims=True)
    small[...] = small_in[...]
    for k in range(width // LANES):
        row = cfg["input_row"] + k
        small[row : row + 1, :] = total[:, k * LANES : (k + 1) * LANES]


def finish_kernel(cfg, ids, inputs, cot, gain, gn, edge, out):
    rows = cfg["rows"]
    size = SPAN // 2
    for c in range(rows // size):
        at = pl.ds(c * size, size)
        wide = inputs[at, :].astype(F32)
        g = gn[pl.ds(HALO + c * size, size), :]
        if c == rows // size - 1:
            g = jnp.concatenate([g[: size - HALO], g[size - HALO :] + edge[...]], axis=0)
        scale = lax.rsqrt(jnp.mean(wide * wide, axis=1, keepdims=True) + EPSILON)
        f = g * gain[...]
        mean = jnp.mean(f * wide, axis=1, keepdims=True)
        grad = cot[at, :].astype(F32) + scale * f - wide * (scale * scale * scale) * mean
        out[at, :] = grad.astype(BF16)


def gather_line(pack, shares):
    return jnp.stack([pack] + [along(pack, d, shares) for d in range(1, shares)])


def gather_layer(held, groups):
    return [held] + [lax.ppermute(held, "dp", xor(groups, 2 * k)) for k in range(1, groups // 2)]


def gather_pair(near, groups):
    pieces = []
    for block in near:
        pieces += [block, lax.ppermute(block, "dp", xor(groups, 1))]
    return pieces


def gather_any(pack):
    rows = lax.all_gather(pack, "dp", axis=0, tiled=True)
    return [lax.all_gather(rows, "tensor", axis=0, tiled=False)]


def scatter_any(pieces):
    part = lax.psum_scatter(pieces[0].astype(F32), "dp", scatter_dimension=1, tiled=True)
    return lax.psum_scatter(part, "tensor", scatter_dimension=0, tiled=False)


def scatter_pair(cfg, ids, keep, send, *small):
    groups, shares, per, c = cfg["groups"], cfg["shares"], cfg["per"], keep.shape[-1]
    others = [lax.ppermute(v, "dp", xor(groups, 1)) for v in (send,) + small]
    n = groups // 2
    shapes = tuple(sds(v.shape) for v in small) + tuple(sds((shares, per, c), BF16) for _ in range(n))
    sums = [v for pair in zip(small, others[1:]) for v in pair]
    return call(functools.partial(pair_kernel, n), shapes, us=1.5)(ids, keep, others[0], *sums)


def scatter_layer(groups, pairs):
    return [pairs[0]] + [lax.ppermute(pairs[k], "dp", xor(groups, 2 * k)) for k in range(1, groups // 2)]


def layer_sum(cfg, ids, parts, first):
    shares, per, cols = (cfg[k] for k in ("shares", "per", "cols"))
    return call(
        functools.partial(quad_kernel, cfg, first),
        (sds((per, 2 * cols), BF16),) * shares,
        scratch=[pltpu.VMEM((shares, per, LANES), F32)],
        us=15.0 if first else 1.5,
    )(ids, *parts)


def scatter_line(shares, blocks):
    return [blocks[0]] + [along(blocks[d], shares - d, shares) for d in range(1, shares)]


def shards(
    inputs, gate_weight, value_weight, step_weight, shared_weight, output_weight, value_kernel,
    shared_kernel, step_bias, decay_log, skip_gain, input_gain, output_gain, cotangent,
):
    shares, groups = lax.axis_size("tensor"), lax.axis_size("dp")
    z, g = lax.axis_index("tensor"), lax.axis_index("dp")
    rows, width = inputs.shape
    per, cols = gate_weight.shape
    own = step_weight.shape[2]
    heads = own * shares
    ns = shared_weight.shape[1] // 4
    inner = cols * shares
    blocks, pages = rows // SPAN, cols // LANES
    fast = groups == 8 and per % 32 == 0
    cfg = dict(
        shares=shares, groups=groups, own=own, head=cols // own, cols=cols, rows=rows, state=ns, per=per,
        pieces=groups if fast else 1,
    )
    cfg["gain_row"] = TAPS * shares * pages
    cfg["state_row"] = cfg["gain_row"] + shares * pages
    cfg["rest_row"] = cfg["state_row"] + 4 * TAPS
    cfg["input_row"] = cfg["rest_row"] + 8
    small_rows = -(-(cfg["input_row"] + width // LANES) // 8) * 8
    ids = (z + jnp.arange(2) * (g - z)).astype(jnp.int32)
    ext = HALO + rows
    pk = cols + LANES

    edge_rows = inputs[rows - HALO :]
    shared_own = lax.dynamic_slice_in_dim(shared_weight, z * ns, ns, 1)
    blank = jnp.zeros((per, LANES - ns - 2 * own), BF16)
    pack1 = jnp.concatenate([value_weight, shared_own, step_weight[:, 0], step_weight[:, 1], blank], axis=1)
    pack2 = jnp.concatenate([gate_weight, output_weight.T], axis=1)

    ogain = output_gain.reshape(1, inner)
    gain = input_gain.reshape(1, width)
    normed, normed_t, cot_t, params, sk = call(
        functools.partial(prep_kernel, cfg),
        (
            sds((rows, width), BF16), sds((width, rows), BF16), sds((width, rows), BF16), sds((8, LANES)),
            sds((4, 8, LANES)),
        ),
        scratch=[pltpu.VMEM((8, LANES), F32)],
        us=3.0,
    )(
        ids, inputs, cotangent, gain, step_bias, decay_log.reshape(1, heads), skip_gain.reshape(1, heads),
        shared_kernel,
    )

    if fast:
        line1 = gather_line(pack1, shares)
        pack2 = jnp.concatenate([pack2, edge_rows], axis=0)
        line2 = [pack2] + [along(after(pack2, line1), d, shares) for d in range(1, shares)]
        halo = line2[1][per:]
        near1 = gather_layer(line1, groups)
        line2 = after(line2, *near1)
        line2 = jnp.stack([block[:per] for block in line2])
        near1, params, sk, ogain, gain, ids, normed, normed_t, cot_t = lax.optimization_barrier(
            (near1, params, sk, ogain, gain, ids, normed, normed_t, cot_t)
        )
        parts1 = gather_pair(near1, groups)
        near2 = gather_layer(after(line2, *near1), groups)
    else:
        parts1, parts2 = gather_any(pack1), gather_any(pack2)
        halo = along(edge_rows, 1, shares)

    full = sds((rows, inner), BF16)
    (
        w1, ws, ahead, vext, u, x, wide, side, su, bc, cct, c2, rho2, c2t, rho2t, dec, states, tots, spread,
        *pays,
    ) = call(
        functools.partial(front_kernel, cfg),
        (
            sds((width, inner), BF16),
            sds((width, shares * LANES), BF16),
            sds((HALO, width), BF16),
            sds((ext, inner), BF16),
            full,
            full,
            sds((2, rows, inner), BF16),
            sds((shares, ext, LANES)),
            sds((4, rows, LANES)),
            sds((4, rows, LANES), BF16),
            sds((blocks, 2 * ns, 2 * SPAN), BF16),
            sds((rows, LANES)),
            sds((rows, LANES)),
            sds((blocks, LANES, SPAN)),
            sds((blocks, LANES, SPAN)),
            sds((4, rows, LANES)),
            sds((blocks, 2 * ns, inner), BF16),
            sds((2 * blocks, LANES)),
            sds((2, LANES, inner), BF16),
            *[sds((shares * ns + HALO, cols), BF16)] * 3,
        ),
        scratch=[
            pltpu.VMEM((ext, inner), F32),
            pltpu.VMEM((blocks, 2 * ns, 2 * SPAN), BF16),
            pltpu.VMEM((2 * SPAN, inner), BF16),
        ],
        us=12.0,
        limit=13 * MB,
    )(ids, halo, normed, gain, value_kernel, sk, params, *parts1)
    got = spread_out(pays, shares)

    yin = call(functools.partial(within_kernel, cfg), full, us=5.0)(
        ids, bc, c2, rho2t, x
    )
    if fast:
        parts2 = gather_pair(after(near2, yin, got[1], got[2]), groups)
    wg, wo, gate, gn_out = call(
        functools.partial(gate_kernel, cfg),
        (sds((width, inner), BF16), sds((width, inner), BF16), full, full),
        us=6.0,
    )(ids, normed, cotangent, *parts2)

    enter, dy, normal, dgate, dcarry, rr, dlocal, rowsum, keeps, *pays = call(
        functools.partial(middle_kernel, cfg),
        (
            sds((blocks, 2 * ns, inner), BF16),
            full,
            full,
            full,
            sds((2, rows, ns)),
            sds((rows, LANES)),
            sds((blocks, 2 * ns, inner), BF16),
            sds((2, 8, inner)),
            sds((3, HALO, inner)),
            *[sds((shares * ns, cols), BF16)] * 3,
        ),
        scratch=[
            pltpu.VMEM((2, rows, inner), BF16),
            pltpu.VMEM((SPAN, inner), F32),
            pltpu.VMEM((SPAN, inner), F32),
            pltpu.VMEM((2, SPAN, inner), F32),
            pltpu.VMEM((2 * SPAN, inner), BF16),
            pltpu.VMEM((2, rows, inner), BF16),
        ],
        us=12.0,
        limit=16 * MB,
    )(ids, yin, x, gate, gn_out, states, bc, cct, dec, tots, spread, params, ogain, *got)
    got = spread_out(pays, shares)

    def piece_shapes(c):
        if fast:
            return (sds((groups // 2, shares, per, c), BF16),) * 2
        return (sds((shares, width, c), BF16),)

    gx, *grads2 = call(
        functools.partial(output_kernel, cfg),
        (sds((rows, width)),) + piece_shapes(2 * cols),
        scratch=[pltpu.VMEM((width, inner), BF16)] * 2,
        us=7.0,
        limit=9 * MB,
    )(ids, cot_t, normed_t, normal, dgate, wg)
    dy_late = dy
    if fast:
        pairs2 = scatter_pair(cfg, ids, *grads2)
        dy_late = after(dy, pairs2)

    dxi, dbc, da, dk = call(
        functools.partial(back_within_kernel, cfg),
        (full, sds((4, rows, LANES)), sds((rows, LANES)), sds((rows, LANES))),
        scratch=[pltpu.VMEM((LANES, SPAN), F32), pltpu.VMEM((LANES, SPAN), F32)],
        us=9.0,
    )(ids, bc, rho2, c2t, x, dy_late, dcarry, rr, keeps)
    if fast:
        layer2 = scatter_layer(groups, pairs2)

    dp, dps, small = call(
        functools.partial(tail_kernel, cfg),
        (sds((ext, inner), BF16), sds((ext, shares * LANES), BF16), sds((small_rows, LANES))),
        scratch=[
            pltpu.VMEM((ext + HALO, inner), F32),
            pltpu.VMEM((4, ext + HALO, LANES), F32),
            pltpu.VMEM((4, rows, LANES), F32),
            pltpu.VMEM((blocks, 2 * ns, inner), BF16),
            pltpu.VMEM((8, LANES), F32),
            pltpu.VMEM((rows, LANES), F32),
            pltpu.VMEM((2, SPAN, inner), F32),
            pltpu.VMEM((2, SPAN, inner), BF16),
            pltpu.VMEM((2, rows, inner), BF16),
        ],
        us=13.0,
        limit=17 * MB,
    )(
        ids, x, u, dxi, wide, vext, side, su, bc, dbc, dec, enter, da, dk, dlocal, rowsum, keeps, spread,
        *got, value_kernel, sk,
    )
    gn, small, *grads1 = call(
        functools.partial(last_kernel, cfg),
        (sds((ext, width)), sds((small_rows, LANES))) + piece_shapes(pk),
        scratch=[pltpu.VMEM((width, inner), BF16), pltpu.VMEM((width, shares * LANES), BF16)],
        us=6.0,
        limit=9 * MB,
    )(ids, halo, inputs, ahead, normed_t, dp, dps, w1, ws, gx, small)
    first_rows = gn[:HALO]
    if fast:
        small, *pairs1 = scatter_pair(cfg, ids, *after(grads1, *layer2), small)
        blocks2 = layer_sum(cfg, ids, layer2, False)
        normal = after(normal, pairs1)
        layer1 = scatter_layer(groups, pairs1)
        line2 = scatter_line(shares, blocks2)
        small, first_rows, line2 = after((small, first_rows, line2), layer1[1])
        grad_gate, grad_output = call(
            functools.partial(line2_kernel, cfg), (sds((per, cols)), sds((per, cols))), us=1.0
        )(ids, *line2)
        last_parts = scatter_line(shares, layer_sum(cfg, ids, layer1, True))
        steps = [("dp", groups, b) for b in range(1, groups.bit_length() - 1)]
        steps += [("tensor", shares, b) for b in range(shares.bit_length() - 1)]
        for axis, size, b in steps:
            mine, theirs = small, lax.ppermute(small, axis, xor(size, 1 << b))
            small = mine + theirs
        last_parts = after(last_parts, theirs)
        grad_value, grad_step, grad_shared = call(
            functools.partial(line_kernel, cfg),
            (sds((per, cols)), sds((per, 2 * own)), sds((per, shares * ns))),
            scratch=[pltpu.VMEM((shares, per, 2 * cols), F32)],
            us=15.0,
        )(ids, *last_parts)

    else:
        out1, out2 = scatter_any(grads1), scatter_any(grads2)
        grad_gate, grad_output = out2[:, :cols], out2[:, cols:]
        grad_value, grad_step = out1[:, :cols], out1[:, cols + ns : cols + ns + 2 * own]
        grad_shared = lax.all_gather(out1[:, cols : cols + ns], "tensor", axis=1, tiled=True)
        mine = lax.psum(small, ("dp", "tensor"))
        theirs = jnp.zeros_like(mine)

    edge = lax.ppermute(first_rows, "tensor", [(i + 1, i) for i in range(shares - 1)])
    mixed = call(mixed_kernel, sds((rows, width), BF16), us=2.0)(ids, inputs, normal, wo)
    grad_input = call(functools.partial(finish_kernel, cfg), sds((rows, width), BF16), us=2.0)(
        ids, inputs, cotangent, gain, gn, edge
    )

    vkernel, skernel, bias, decay, skip, ingain, outgain = call(
        functools.partial(small_kernel, cfg),
        (
            sds((TAPS, inner)), sds((TAPS, 4 * ns)), sds((2, heads)), sds((1, heads)), sds((1, heads)),
            sds((1, width)), sds((1, inner)),
        ),
        scratch=[pltpu.VMEM((small_rows, LANES), F32)],
        us=1.0,
    )(ids, mine, theirs)
    return (
        mixed,
        grad_input,
        grad_gate,
        grad_value,
        grad_step.reshape(per, 2, own),
        grad_shared,
        grad_output.T,
        vkernel,
        skernel,
        bias,
        decay.reshape(heads),
        skip.reshape(heads),
        ingain.reshape(width),
        outgain.reshape(inner),
    )


def solution(mesh):
    both = P(("dp", "tensor"), None)
    placed = (
        both, P("dp", "tensor"), P("dp", "tensor"), P("dp", None, "tensor"), P("dp", None),
        P("tensor", "dp"), P(), P(), P(), P(), P(), P(), P(), both,
    )
    return jax.shard_map(
        shards,
        mesh=mesh,
        in_specs=placed,
        out_specs=(
            both, both, P("dp", "tensor"), P("dp", "tensor"), P("dp", None, "tensor"), P("dp", None),
            P("tensor", "dp"), P(), P(), P(), P(), P(), P(), P(),
        ),
        check_vma=False,
    )
```
